32 devices in a mesh: row: 4 (over x, core), col: 8 (over z, y).
Axes of the slice: x: 2, y: 2, z: 4, core: 2. Of those that a mesh axis runs over, the one named last changes fastest.
Arguments:
- tokens: bfloat16 [64, 128, 256], P('row', 'col'), may hold values from -6 to 6
- grad_out: bfloat16 [64, 128, 256], P('row', 'col'), may hold values from -46 to 46
- w_qkv: bfloat16 [256, 768], replicated, may hold values from -0.375 to 0.375
- w_out: bfloat16 [256, 256], replicated, may hold values from -0.375 to 0.375
- scale: float32 [4], replicated, may hold values from 3 to 12
Outputs:
- grad_tokens: bfloat16 [64, 128, 256], P('row', 'col')
- grad_wqkv: float32 [256, 768], replicated
- grad_wout: float32 [256, 256], replicated
- grad_scale: float32 [4], replicated
The draws below stay inside these ranges and needn't reach their ends.
All inputs are finite; a program needn't handle non-finite values.
Results may differ from the reference program's by a relative error of at most 0.0055.
Values may be sent and summed in bfloat16 or wider, within the bound.
No kernel may reach another device: no remote copies, remote signals or barrier semaphores. Data moves between devices by JAX's collectives and lax.ppermute only.
A program may use at most 64 MiB of HBM per device.

```python
import math
import jax
import jax.numpy as jnp
from jax import lax

HEADS = 4
D = 256
TR = 16
NR = 64
NC = 128
N_ROW = 4


def draw_grad_out(key, part):
    row_pos = jnp.arange(NR, dtype=jnp.float32) / (NR - 1)
    col_pos = jnp.arange(NC, dtype=jnp.float32) / (NC - 1)
    row_factor = jnp.exp(jnp.log(3.0) * row_pos)[:, None, None]
    col_factor = jnp.exp(jnp.log(3.0) * col_pos)[None, :, None]
    base = jnp.clip(jax.random.normal(key, (NR, NC, D), jnp.float32), -4.0, 4.0)
    return (base * row_factor * col_factor).astype(jnp.bfloat16)


def levels(rng, dims, cuts, smallest, high):
    level, own = 1.0, jax.random.fold_in(rng, 6)
    for position, parts in cuts:
        heights = jnp.exp(jax.random.uniform(jax.random.fold_in(own, position), (parts,), jnp.float32, smallest / len(cuts), high / len(cuts)))
        level = level * jnp.repeat(heights, dims[position] // parts).reshape([-1 if axis == position else 1 for axis in range(len(dims))])
    return level


def noise(own_key, extent, width, most, cuts=(), kind=jnp.bfloat16):
    entries = jax.random.normal(own_key, extent, jnp.float32) * width
    if len(cuts) > 0:
        entries = levels(own_key, extent, cuts, -0.22, 0.18) * entries
    return jnp.clip(entries, min=-most, max=most).astype(kind)


def setup_inputs(seed: int = 0) -> dict:
    key_list = jax.random.split(jax.random.key(seed), 6)
    tokens = noise(key_list[0], (NR, NC, D), 1.0, 6.0, ((0, 4), (1, 8)))
    grad_out = draw_grad_out(jax.random.fold_in(key_list[5], 71), 0)
    w_qkv = noise(key_list[2], (D, 3 * D), D ** -0.5, 0.375)
    w_out = noise(key_list[3], (D, D), D ** -0.5, 0.375)
    scale = jnp.clip(jnp.exp(jax.random.uniform(key_list[4], (HEADS,), jnp.float32, math.log(3.0), math.log(12.0))), 3.0, 12.0)
    return dict(tokens=tokens, grad_out=grad_out, w_qkv=w_qkv, w_out=w_out, scale=scale)


def unit_heads(source_array):
    shaped = source_array.reshape(source_array.shape[:-1] + (HEADS, -1))
    normed = shaped * lax.rsqrt(lax.optimization_barrier(jnp.sum(shaped * shaped, axis=-1, keepdims=True)) + 1e-06)
    return normed.reshape(source_array.shape)

def project_heads(qkv_full):
    feature_width = qkv_full.shape[-1] // 3
    return (unit_heads(qkv_full[..., :feature_width]), unit_heads(qkv_full[..., feature_width:2 * feature_width]), qkv_full[..., 2 * feature_width:])

def block_windows(source_array, tile_count):
    trailing_shape = source_array.shape[1:]
    leading = source_array[:tile_count * 8].reshape((tile_count, 8) + trailing_shape)
    trailing = jnp.pad(source_array[8:], [(0, 2)] + [(0, 0)] * len(trailing_shape))
    trailing = trailing[:tile_count * 8].reshape((tile_count, 8) + trailing_shape)[:, :6]
    return jnp.concatenate([leading, trailing], axis=1)

def key_regions(source_array, tile_rows, tile_cols):
    feature_width = source_array.shape[-1]
    head_size = feature_width // HEADS
    by_rows = block_windows(source_array, tile_rows)
    by_cols = block_windows(jnp.moveaxis(by_rows, 2, 0), tile_cols)
    shaped = by_cols.reshape(tile_cols, 14, tile_rows, 14, HEADS, head_size)
    return shaped.transpose(2, 0, 4, 3, 1, 5).reshape(tile_rows, tile_cols, HEADS, 196, head_size)

def edge_mask(first_index, tile_count, span_size, grid_extent):
    positions = first_index + 8 * jnp.arange(tile_count, dtype=jnp.int32)[:, None] + jnp.arange(span_size, dtype=jnp.int32)[None, :]
    return (positions >= 0) & (positions < grid_extent)

def neighbor_attend(query_unit, key_unit, value_rows, scale_map, row_first, col_first, total_rows, total_cols):
    query_rows, query_cols, feature_width = query_unit.shape
    head_size = feature_width // HEADS
    tile_rows = (query_rows + 7) // 8
    tile_cols = (query_cols + 7) // 8
    extra_rows = tile_rows * 8 - query_rows
    extra_cols = tile_cols * 8 - query_cols
    padding = ((0, extra_rows), (0, extra_cols), (0, 0))
    query_unit = jnp.pad(query_unit, padding)
    scale_map = jnp.pad(scale_map, padding)
    key_unit = jnp.pad(key_unit, padding)
    value_rows = jnp.pad(value_rows, padding)
    query_tiles = query_unit.reshape(tile_rows, 8, tile_cols, 8, HEADS, head_size).transpose(0, 2, 4, 1, 3, 5).reshape(tile_rows, tile_cols, HEADS, 64, head_size)
    scale_tiles = scale_map.reshape(tile_rows, 8, tile_cols, 8, HEADS).transpose(0, 2, 4, 1, 3).reshape(tile_rows, tile_cols, HEADS, 64, 1)
    key_tiles = key_regions(key_unit, tile_rows, tile_cols)
    value_tiles = key_regions(value_rows, tile_rows, tile_cols)
    cosine = jnp.einsum('abhqe,abhke->abhqk', query_tiles, key_tiles, precision=lax.Precision.HIGHEST)
    query_row_ok = edge_mask(row_first, tile_rows, 8, total_rows)
    query_col_ok = edge_mask(col_first, tile_cols, 8, total_cols)
    key_row_ok = edge_mask(row_first - 3, tile_rows, 14, total_rows)
    key_col_ok = edge_mask(col_first - 3, tile_cols, 14, total_cols)
    query_ok = (query_row_ok[:, None, :, None] & query_col_ok[None, :, None, :]).reshape(tile_rows, tile_cols, 1, 64, 1)
    key_ok = (key_row_ok[:, None, :, None] & key_col_ok[None, :, None, :]).reshape(tile_rows, tile_cols, 1, 1, 196)
    offsets = jnp.arange(14, dtype=jnp.int32)[None, :] - jnp.arange(8, dtype=jnp.int32)[:, None]
    window_line = (offsets >= 0) & (offsets <= 6)
    window_mask = (window_line[:, None, :, None] & window_line[None, :, None, :]).reshape(64, 196)
    kept_mask = (window_mask & key_ok & query_ok).astype(jnp.float32)
    weights = jnp.exp(scale_tiles * cosine) * kept_mask
    totals = lax.optimization_barrier(jnp.sum(weights, axis=-1, keepdims=True)) + 1.0 - query_ok.astype(jnp.float32)
    weights = weights / totals
    blended = jnp.einsum('abhqk,abhke->abhqe', weights, value_tiles, precision=lax.Precision.HIGHEST)
    blended = blended.reshape(tile_rows, tile_cols, HEADS, 8, 8, head_size).transpose(0, 3, 1, 4, 2, 5).reshape(tile_rows * 8, tile_cols * 8, feature_width)
    return blended[:query_rows, :query_cols]

def reference(tokens, grad_out, w_qkv, w_out, scale):
    feature_width = tokens.shape[2]
    padded_tokens = jnp.pad(tokens, ((6, 6), (6, 6), (0, 0)))
    padded_grads = jnp.pad(grad_out, ((3, 3), (3, 3), (0, 0)))
    contract_last = (((1,), (1,)), ((), ()))
    contract_first = (((0,), (0,)), ((), ()))

    def block_step(carry, block_index):
        sum_wqkv, sum_wout, sum_scale = carry
        first_row = (block_index * TR).astype(jnp.int32)
        token_rows = lax.dynamic_slice_in_dim(padded_tokens, first_row, TR + 12, 0)
        grad_rows = lax.dynamic_slice_in_dim(padded_grads, first_row, TR + 6, 0)
        qkv_full = jnp.dot(token_rows.reshape(-1, feature_width), w_qkv, preferred_element_type=jnp.float32).reshape(TR + 12, NC + 12, 3 * feature_width)
        query_unit, key_unit, value_rows = project_heads(qkv_full)
        grad_attn = lax.dot_general(grad_rows.reshape(-1, feature_width), w_out, contract_last, preferred_element_type=jnp.float32).reshape(TR + 6, NC + 6, feature_width)
        scale_map = jnp.broadcast_to(scale, (TR + 6, NC + 6, HEADS))

        def attend_block(query_part, key_part, value_part, scale_part):
            return neighbor_attend(query_part, key_part, value_part, scale_part, first_row - 3, -3, NR, NC)
        attended, pullback = jax.vjp(attend_block, query_unit[3:-3, 3:-3], key_unit, value_rows, scale_map)
        grad_query, grad_key, grad_value, grad_map = pullback(grad_attn)
        attn_saved = attended[3:-3, 3:-3].astype(jnp.bfloat16).reshape(-1, feature_width)
        grad_inner = grad_rows[3:-3, 3:-3].reshape(-1, feature_width)
        sum_wout = sum_wout + lax.dot_general(attn_saved, grad_inner, contract_first, preferred_element_type=jnp.float32)
        sum_scale = sum_scale + lax.optimization_barrier(jnp.sum(grad_map[3:-3, 3:-3], axis=(0, 1)))
        unused_out, prep_pull = jax.vjp(project_heads, qkv_full[6:-6, 6:-6])
        grad_qkv, = prep_pull((grad_query[3:-3, 3:-3], grad_key[6:-6, 6:-6], grad_value[6:-6, 6:-6]))
        grad_qkv = grad_qkv.astype(jnp.bfloat16).reshape(-1, 3 * feature_width)
        token_inner = token_rows[6:-6, 6:-6].reshape(-1, feature_width)
        grad_block = lax.dot_general(grad_qkv, w_qkv, contract_last, preferred_element_type=jnp.float32).astype(jnp.bfloat16).reshape(TR, NC, feature_width)
        sum_wqkv = sum_wqkv + lax.dot_general(token_inner, grad_qkv, contract_first, preferred_element_type=jnp.float32)
        return ((sum_wqkv, sum_wout, sum_scale), grad_block)
    start_carry = (jnp.zeros((feature_width, 3 * feature_width), jnp.float32), jnp.zeros((feature_width, feature_width), jnp.float32), jnp.zeros((HEADS,), jnp.float32))
    (sum_wqkv, sum_wout, sum_scale), grad_blocks = lax.scan(block_step, start_carry, jnp.arange(N_ROW, dtype=jnp.int32))
    return (grad_blocks.reshape(NR, NC, feature_width), sum_wqkv, sum_wout, sum_scale)
```

```python
import math

import jax
import jax.numpy as jnp
from jax import lax
from jax.experimental import pallas as pl
from jax.experimental.pallas import tpu as pltpu
from jax.sharding import Mesh
from jax.sharding import PartitionSpec as P

HEADS = 4
REACH = 3
F32 = jnp.float32
BF16 = jnp.bfloat16
LAST = (((1,), (1,)), ((), ()))
FIRST = (((0,), (0,)), ((), ()))
LOG2E = math.log2(math.e)
ROW_AXES = ("rowhi", "rowlo")
SPREAD_AXES = ("rowhi", "col")


def dot(a, b, dims=(((1,), (0,)), ((), ()))):
    return lax.dot_general(a, b, dims, preferred_element_type=F32)


def split(x):
    hi = x.astype(BF16)
    return hi, (x - hi.astype(F32)).astype(BF16)


def kernel(
    scale_ref,
    tok_ref,
    go_ref,
    top_ref,
    bot_ref,
    left_ref,
    right_ref,
    wqkv_ref,
    wout_ref,
    gt_ref,
    gw_ref,
    tx,
    gx,
    side,
    qf,
    qr,
    kf,
    kr,
    khi,
    klo,
    vhi,
    vlo,
    ga,
    gq,
    gk,
    gv,
    att,
):
    rows, cols, d = tok_ref.shape
    tall, wide, _ = tx.shape
    qtall, qwide, _ = gx.shape
    per = d // HEADS
    q0 = 8 - REACH - 2
    own_k = 2 * REACH
    own_q = 8 - q0
    n_rows = rows * lax.axis_size(ROW_AXES)
    n_cols = cols * lax.axis_size("col")
    row_first = lax.axis_index(ROW_AXES) * rows
    col_first = lax.axis_index("col") * cols

    zeros = jnp.zeros((tall, 8, d), F32)
    tx[:, 0:8, :] = zeros
    tx[:, 8 + cols : wide, :] = jnp.zeros((tall, wide - 8 - cols, d), F32)
    gx[:, 0:8, :] = jnp.zeros((qtall, 8, d), F32)
    edge = 2 * REACH * cols
    tx[own_k : own_k + rows, 8 : 8 + cols, :] = tok_ref[...].astype(F32)
    tx[0:own_k, 8 : 8 + cols, :] = top_ref[0:edge].astype(F32).reshape(own_k, cols, d)
    tx[own_k + rows : tall, 8 : 8 + cols, :] = (
        bot_ref[0:edge].astype(F32).reshape(own_k, cols, d)
    )
    gx[REACH : REACH + rows, own_q : own_q + cols, :] = go_ref[...].astype(F32)
    gx[0:REACH, own_q : own_q + cols, :] = top_ref[edge:].astype(F32).reshape(REACH, cols, d)
    gx[REACH + rows : qtall, own_q : own_q + cols, :] = (
        bot_ref[edge:].astype(F32).reshape(REACH, cols, d)
    )
    for ref, at_k, at_q in (
        (left_ref, 8 - own_k, own_q - REACH),
        (right_ref, 8 + cols, own_q + cols),
    ):
        side[...] = ref[...].astype(F32)
        for r in range(tall):
            tx[r, at_k : at_k + own_k, :] = side[r * own_k : (r + 1) * own_k]
        base = tall * own_k
        for r in range(qtall):
            gx[r, at_q : at_q + REACH, :] = side[base + r * REACH : base + (r + 1) * REACH]

    lane_head = lax.broadcasted_iota(jnp.int32, (1, d), 1) // per
    ones = (
        lax.broadcasted_iota(jnp.int32, (d, d), 0) // per
        == lax.broadcasted_iota(jnp.int32, (d, d), 1) // per
    ).astype(BF16)

    def head_sum(x):
        hi, lo = split(x)
        return dot(hi, ones) + dot(lo, ones)

    step = 4
    for c in range(tall // step):
        at = slice(c * step, (c + 1) * step)
        x = tx[at].reshape(step * wide, d).astype(BF16)
        qkv = dot(x, wqkv_ref[...])
        q, k, v = qkv[:, :d], qkv[:, d : 2 * d], qkv[:, 2 * d :]
        rq = lax.rsqrt(head_sum(q * q) + 1e-06)
        rk = lax.rsqrt(head_sum(k * k) + 1e-06)
        q = q * rq
        k = k * rk
        qf[at] = q.reshape(step, wide, d)
        qr[at] = rq.reshape(step, wide, d)
        kf[at] = k.reshape(step, wide, d)
        kr[at] = rk.reshape(step, wide, d)
        flat = slice(c * step * wide, (c + 1) * step * wide)
        khi[flat], klo[flat] = split(k)
        vhi[flat], vlo[flat] = split(v)
    ga[...] = dot(gx[...].reshape(qtall * qwide, d).astype(BF16), wout_ref[...], LAST)

    gk[...] = jnp.zeros_like(gk)
    gv[...] = jnp.zeros_like(gv)

    nq = 2 * qwide
    span = 2 + 2 * REACH
    nk = span * wide
    i = lax.broadcasted_iota(jnp.int32, (nq, nk), 0)
    j = lax.broadcasted_iota(jnp.int32, (nq, nk), 1)
    dr = j // wide - i // qwide
    dc = j % wide - i % qwide
    key_col = j % wide + (col_first - 8)
    near = (dr >= 0) & (dr <= 2 * REACH) & (dc >= 0) & (dc <= 2 * REACH)
    near = (near & (key_col >= 0) & (key_col < n_cols)).astype(F32)
    jr = lax.broadcasted_iota(jnp.int32, (1, nk), 1) // wide
    iq = lax.broadcasted_iota(jnp.int32, (nq, 1), 0)
    own_col = (iq % qwide >= own_q) & (iq % qwide < own_q + cols)
    sl = jnp.zeros((1, d), F32)
    for h in range(HEADS):
        sl = jnp.where(lane_head == h, scale_ref[h], sl)
    head_lanes = [lane_head == h for h in range(HEADS)]

    def spread(x):
        zero = jnp.zeros_like(x)
        return jnp.concatenate([jnp.where(m, x, zero) for m in head_lanes], axis=0)

    def gather(x):
        out = x[0:nq]
        for h in range(1, HEADS):
            out = jnp.where(head_lanes[h], x[h * nq : (h + 1) * nq], out)
        return out

    def band(b, total):
        q = qf[pl.ds(2 * b + REACH, 2), q0 : q0 + qwide, :].reshape(nq, d)
        q_hi, q_lo = split(q * (sl * LOG2E))
        g = ga[pl.ds(pl.multiple_of(b * nq, nq), nq), :]
        g_hi, g_lo = split(g)
        keys = pl.ds(pl.multiple_of(b * 2 * wide, 2 * wide), nk)
        k_hi, k_lo, v_hi, v_lo = khi[keys], klo[keys], vhi[keys], vlo[keys]
        qs_hi, qs_lo, gs_hi, gs_lo = spread(q_hi), spread(q_lo), spread(g_hi), spread(g_lo)
        s = dot(qs_hi, k_hi, LAST) + dot(qs_lo, k_hi, LAST) + dot(qs_hi, k_lo, LAST)
        dp = dot(gs_hi, v_hi, LAST) + dot(gs_lo, v_hi, LAST) + dot(gs_hi, v_lo, LAST)
        key_row = jr + (row_first - 2 * REACH + 2 * b)
        mask = near * ((key_row >= 0) & (key_row < n_rows)).astype(F32)
        e = (jnp.exp2(s).reshape(HEADS, nq, nk) * mask[None]).reshape(HEADS * nq, nk)
        r = 1.0 / (jnp.sum(e, axis=1, keepdims=True) + 1e-30)
        p = e * r
        ds = p * (dp - jnp.sum(p * dp, axis=1, keepdims=True))
        q_row = iq // qwide + 2 * b
        own = own_col & (q_row >= REACH) & (q_row < REACH + rows)
        own = jnp.concatenate([own.astype(F32)] * HEADS, axis=0)
        total = total + own * jnp.sum(ds * s, axis=1, keepdims=True)
        p_b, ds_b = p.astype(BF16), ds.astype(BF16)
        att[pl.ds(2 * b, 2)] = gather(dot(p_b, v_hi)).reshape(2, qwide, d)
        gq[pl.ds(2 * b, 2)] = (gather(dot(ds_b, k_hi)) * sl).reshape(2, qwide, d)
        gk[pl.ds(2 * b, span)] += dot(ds_b, qs_hi, FIRST).reshape(span, wide, d)
        gv[pl.ds(2 * b, span)] += dot(p_b, gs_hi, FIRST).reshape(span, wide, d)
        return total

    total = lax.fori_loop(0, qtall // 2, band, jnp.zeros((HEADS * nq, 1), F32))

    n = rows * cols
    at_k = (slice(own_k, own_k + rows), slice(8, 8 + cols))
    at_q = (slice(REACH, REACH + rows), slice(own_q, own_q + cols))

    def unit_back(unit, r, g):
        return r * (g - unit * head_sum(unit * g))

    g_q = unit_back(qf[at_k].reshape(n, d), qr[at_k].reshape(n, d), gq[at_q].reshape(n, d))
    g_k = unit_back(
        kf[at_k].reshape(n, d), kr[at_k].reshape(n, d), gk[at_k].reshape(n, d) * (1.0 / LOG2E)
    )
    g_v = gv[at_k].reshape(n, d)
    grads = jnp.concatenate([g_q.astype(BF16), g_k.astype(BF16), g_v.astype(BF16)], axis=1)
    gt_ref[...] = dot(grads, wqkv_ref[...], LAST).astype(BF16).reshape(rows, cols, d)
    wq = dot(tok_ref[...].reshape(n, d), grads, FIRST)
    wo = dot(
        att[at_q].reshape(n, d).astype(BF16), go_ref[...].reshape(n, d), FIRST
    )
    half = d // 2
    lane = lax.broadcasted_iota(jnp.int32, (8, 4 * d), 1)
    sums = jnp.zeros((8, 4 * d), F32)
    for h in range(HEADS):
        t = jnp.sum(total[h * nq : (h + 1) * nq], axis=0, keepdims=True)
        t = t / (scale_ref[h] * LOG2E)
        sums = jnp.where(lane == h, t, sums)
    for c in range(2):
        gw_ref[c, 0:half, 0 : 3 * d] = wq[c * half : (c + 1) * half]
        gw_ref[c, 0:half, 3 * d :] = wo[c * half : (c + 1) * half]
        gw_ref[c, half:, :] = sums


def local_grads(scale, tokens, grad_out, top, bot, left, right, w_qkv, w_out):
    rows, cols, d = tokens.shape
    tall = rows + 4 * REACH
    wide = -(-(cols + 4 * REACH + 2) // 16) * 16
    qtall = rows + 2 * REACH
    qwide = -(-(cols + 2 * REACH + 2) // 8) * 8
    vmem = pl.BlockSpec(memory_space=pltpu.VMEM)
    grid = lambda dt: pltpu.VMEM((tall, wide, d), dt)
    qgrid = lambda dt: pltpu.VMEM((qtall, qwide, d), dt)
    flat = lambda dt: pltpu.VMEM((tall * wide, d), dt)
    return pl.pallas_call(
        kernel,
        out_shape=(
            jax.ShapeDtypeStruct((rows, cols, d), BF16),
            jax.ShapeDtypeStruct((2, d // 2 + 8, 4 * d), F32),
        ),
        in_specs=[pl.BlockSpec(memory_space=pltpu.SMEM)] + [vmem] * 8,
        out_specs=(vmem, vmem),
        scratch_shapes=[
            grid(F32),
            qgrid(F32),
            pltpu.VMEM(left.shape, F32),
            grid(F32),
            grid(F32),
            grid(F32),
            grid(F32),
            flat(BF16),
            flat(BF16),
            flat(BF16),
            flat(BF16),
            pltpu.VMEM((qtall * qwide, d), F32),
            qgrid(F32),
            grid(F32),
            grid(F32),
            qgrid(F32),
        ],
        compiler_params=pltpu.CompilerParams(vmem_limit_bytes=48 * 1024 * 1024),
        cost_estimate=pl.CostEstimate(
            flops=8_000_000_000, bytes_accessed=4_000_000, transcendentals=600_000
        ),
    )(scale, tokens, grad_out, top, bot, left, right, w_qkv, w_out)


def passed(x, axis, by):
    size = lax.axis_size(axis)
    return lax.ppermute(x, axis, [(i, i + by) for i in range(size) if 0 <= i + by < size])


def shards(tokens, grad_out, w_qkv, w_out, scale):
    rows, cols, d = tokens.shape
    wide = 2 * REACH

    def flat(*parts):
        return jnp.concatenate([p.reshape(-1, d) for p in parts], axis=0)

    top = passed(flat(tokens[rows - wide :], grad_out[rows - REACH :]), ROW_AXES, 1)
    bot = passed(flat(tokens[:wide], grad_out[:REACH]), ROW_AXES, -1)
    edge = wide * cols

    def tall(x, lo, hi):
        lo, hi = lo.reshape(-1, cols, d), hi.reshape(-1, cols, d)
        return lambda s: jnp.concatenate([lo[:, s], x[:, s], hi[:, s]], axis=0)

    tok_tall = tall(tokens, top[:edge], bot[:edge])
    go_tall = tall(grad_out, top[edge:], bot[edge:])
    left = passed(flat(tok_tall(slice(cols - wide, cols)), go_tall(slice(cols - REACH, cols))), "col", 1)
    right = passed(flat(tok_tall(slice(0, wide)), go_tall(slice(0, REACH))), "col", -1)

    grad_tokens, partial = local_grads(
        scale, tokens, grad_out, top, bot, left, right, w_qkv, w_out
    )

    lo = lax.axis_index("rowlo")
    swap = [(0, 1), (1, 0)]
    kept = lax.dynamic_index_in_dim(partial, lo, 0, keepdims=False)
    sent = lax.dynamic_index_in_dim(partial, 1 - lo, 0, keepdims=False)
    kept = kept + lax.ppermute(sent, "rowlo", swap)
    half = d // 2
    n = lax.axis_size(SPREAD_AXES)
    pieces = half // n if half % n == 0 else 1
    part = kept[:half].reshape(n, pieces, -1)
    sums = kept[half, :HEADS]
    sums_hi = lax.reduce_precision(sums, 8, 7)
    sums = jnp.concatenate([sums_hi, sums - sums_hi, jnp.zeros((128 - 2 * HEADS,), F32)])
    part = jnp.concatenate(
        [part.astype(BF16), jnp.broadcast_to(sums.astype(BF16), (n, pieces, 128))], axis=2
    )
    part = lax.all_to_all(part, SPREAD_AXES, 0, 0, tiled=True).astype(F32)
    part = jnp.sum(part, axis=0)
    sums = part[0, -128:]
    grad_scale = sums[:HEADS] + sums[HEADS : 2 * HEADS]
    part = part[:, :-128].astype(BF16)
    mine = lax.all_to_all(
        jnp.broadcast_to(part[None], (n,) + part.shape), SPREAD_AXES, 0, 0, tiled=True
    ).reshape(half, 4 * d)
    other = lax.ppermute(mine, "rowlo", swap)
    first = lo == 0
    upper = jnp.where(first, mine, other).astype(F32)
    lower = jnp.where(first, other, mine).astype(F32)
    grads = jnp.concatenate([upper, lower], axis=0)
    return grad_tokens, grads[:, : 3 * d], grads[:, 3 * d :], grad_scale


def solution(mesh):
    n_row, n_col = mesh.devices.shape
    fine = Mesh(mesh.devices.reshape(n_row // 2, 2, n_col), ("rowhi", "rowlo", "col"))
    block = P(ROW_AXES, "col", None)
    return jax.shard_map(
        shards,
        mesh=fine,
        in_specs=(block, block, P(), P(), P()),
        out_specs=(block, P(), P(), P()),
        check_vma=False,
    )
```

```python
import math

import jax
import jax.numpy as jnp
from jax import lax
from jax.experimental import pallas as pl
from jax.experimental.pallas import tpu as pltpu
from jax.sharding import Mesh
from jax.sharding import PartitionSpec as P

HEADS = 4
REACH = 3
F32 = jnp.float32
BF16 = jnp.bfloat16
LAST = (((1,), (1,)), ((), ()))
FIRST = (((0,), (0,)), ((), ()))
LOG2E = math.log2(math.e)
ROW_AXES = ("rowhi", "rowlo")
SPREAD_AXES = ("rowhi", "col")


def dot(a, b, dims=(((1,), (0,)), ((), ()))):
    return lax.dot_general(a, b, dims, preferred_element_type=F32)


def split(x):
    hi = x.astype(BF16)
    return hi, (x - hi.astype(F32)).astype(BF16)


def kernel(
    scale_ref,
    tok_ref,
    go_ref,
    top_ref,
    bot_ref,
    left_ref,
    right_ref,
    wqkv_ref,
    wout_ref,
    gt_ref,
    gw_ref,
    tx,
    gx,
    side,
    ends,
    qf,
    qr,
    kf,
    kr,
    khi,
    klo,
    vhi,
    vlo,
    qhi,
    qlo,
    ghi,
    glo,
    sbuf,
    dbuf,
    pbuf,
    dsbuf,
    gq,
    gk,
    gv,
    att,
):
    rows, cols, d = tok_ref.shape
    tall, wide, _ = tx.shape
    qtall, qwide, _ = gx.shape
    per = d // HEADS
    q0 = 8 - REACH - 2
    own_k = 2 * REACH
    own_q = 8 - q0
    n_rows = rows * lax.axis_size(ROW_AXES)
    n_cols = cols * lax.axis_size("col")
    row_first = lax.axis_index(ROW_AXES) * rows
    col_first = lax.axis_index("col") * cols

    tx[:, 0:8, :] = jnp.zeros((tall, 8, d), F32)
    tx[:, 8 + cols : wide, :] = jnp.zeros((tall, wide - 8 - cols, d), F32)
    gx[:, 0:8, :] = jnp.zeros((qtall, 8, d), F32)
    left_k, right_k = 8 - own_k, 8 + cols
    left_q, right_q = own_q - REACH, own_q + cols
    tx[own_k : own_k + rows, 8 : 8 + cols, :] = tok_ref[...].astype(F32)
    gx[REACH : REACH + rows, own_q : own_q + cols, :] = go_ref[...].astype(F32)
    for ref, at_k, at_q in ((left_ref, left_k, left_q), (right_ref, right_k, right_q)):
        side[...] = ref[...].astype(F32)
        for r in range(rows):
            tx[own_k + r, at_k : at_k + own_k, :] = side[r * own_k : (r + 1) * own_k]
        base = rows * own_k
        for r in range(rows):
            gx[REACH + r, at_q : at_q + REACH, :] = side[base + r * REACH : base + (r + 1) * REACH]
    for ref, row_k, row_q in ((top_ref, 0, 0), (bot_ref, own_k + rows, REACH + rows)):
        ends[...] = ref[...].astype(F32)
        at = 0
        for grid, row, reach, col, width in (
            (tx, row_k, own_k, 8, cols),
            (gx, row_q, REACH, own_q, cols),
            (tx, row_k, own_k, left_k, own_k),
            (tx, row_k, own_k, right_k, own_k),
            (gx, row_q, REACH, left_q, REACH),
            (gx, row_q, REACH, right_q, REACH),
        ):
            for r in range(reach):
                grid[row + r, col : col + width, :] = ends[at : at + width]
                at += width

    lane_head = lax.broadcasted_iota(jnp.int32, (1, d), 1) // per
    ones = (
        lax.broadcasted_iota(jnp.int32, (d, d), 0) // per
        == lax.broadcasted_iota(jnp.int32, (d, d), 1) // per
    ).astype(BF16)

    def head_sum(x):
        hi, lo = split(x)
        return dot(hi, ones) + dot(lo, ones)

    sl = jnp.zeros((1, d), F32)
    for h in range(HEADS):
        sl = jnp.where(lane_head == h, scale_ref[h], sl)
    head_lanes = [lane_head == h for h in range(HEADS)]

    step = 4
    for c in range(tall // step):
        at = slice(c * step, (c + 1) * step)
        x = tx[at].reshape(step * wide, d).astype(BF16)
        kv = dot(x, wqkv_ref[:, d:])
        k = kv[:, :d]
        rk = lax.rsqrt(head_sum(k * k) + 1e-06)
        k = k * rk
        kf[at] = k.reshape(step, wide, d)
        kr[at] = rk.reshape(step, wide, d)
        flat = slice(c * step * wide, (c + 1) * step * wide)
        khi[flat], klo[flat] = split(k)
        vhi[flat], vlo[flat] = split(kv[:, d:])
    nq = 2 * qwide
    for c in range(0, qtall, 4):
        step = min(4, qtall - c)
        at = slice(c, c + step)
        x = tx[REACH + c : REACH + c + step, q0 : q0 + qwide, :].reshape(step * qwide, d)
        q = dot(x.astype(BF16), wqkv_ref[:, :d])
        rq = lax.rsqrt(head_sum(q * q) + 1e-06)
        q = q * rq
        qf[at] = q.reshape(step, qwide, d)
        qr[at] = rq.reshape(step, qwide, d)
        flat = slice(c * qwide, (c + step) * qwide)
        qhi[flat], qlo[flat] = split(q * (sl * LOG2E))
        g = dot(gx[at].reshape(step * qwide, d).astype(BF16), wout_ref[...], LAST)
        ghi[flat], glo[flat] = split(g)

    gk[...] = jnp.zeros_like(gk)
    gv[...] = jnp.zeros_like(gv)

    span = 2 + 2 * REACH
    nk = span * wide
    i = lax.broadcasted_iota(jnp.int32, (nq, nk), 0)
    j = lax.broadcasted_iota(jnp.int32, (nq, nk), 1)
    dr = j // wide - i // qwide
    dc = j % wide - i % qwide
    key_col = j % wide + (col_first - 8)
    near = (dr >= 0) & (dr <= 2 * REACH) & (dc >= 0) & (dc <= 2 * REACH)
    near = (near & (key_col >= 0) & (key_col < n_cols)).astype(F32)
    jr = lax.broadcasted_iota(jnp.int32, (1, nk), 1) // wide
    iq = lax.broadcasted_iota(jnp.int32, (nq, 1), 0)
    own_col = (iq % qwide >= own_q) & (iq % qwide < own_q + cols)

    def spread(x):
        zero = jnp.zeros_like(x)
        return jnp.concatenate([jnp.where(m, x, zero) for m in head_lanes], axis=0)

    def gather(x):
        out = x[0:nq]
        for h in range(1, HEADS):
            out = jnp.where(head_lanes[h], x[h * nq : (h + 1) * nq], out)
        return out

    def places(b):
        if isinstance(b, int):
            return slice(b * nq, (b + 1) * nq), slice(b * 2 * wide, b * 2 * wide + nk)
        return (
            pl.ds(pl.multiple_of(b * nq, nq), nq),
            pl.ds(pl.multiple_of(b * 2 * wide, 2 * wide), nk),
        )

    def scores(b):
        at, keys = places(b)
        q_hi, q_lo = spread(qhi[at]), spread(qlo[at])
        k_hi = khi[keys]
        sbuf[...] = dot(q_hi, k_hi, LAST) + dot(q_lo, k_hi, LAST) + dot(q_hi, klo[keys], LAST)
        g_hi, g_lo = spread(ghi[at]), spread(glo[at])
        v_hi = vhi[keys]
        dbuf[...] = dot(g_hi, v_hi, LAST) + dot(g_lo, v_hi, LAST) + dot(g_hi, vlo[keys], LAST)

    def softmax(b, total):
        key_row = jr + (row_first - 2 * REACH + 2 * b)
        mask = near * ((key_row >= 0) & (key_row < n_rows)).astype(F32)
        q_row = iq // qwide + 2 * b
        own = (own_col & (q_row >= REACH) & (q_row < REACH + rows)).astype(F32)
        out = []
        for h in range(HEADS):
            at = slice(h * nq, (h + 1) * nq)
            s, dp = sbuf[at], dbuf[at]
            e = jnp.exp2(s) * mask
            r = 1.0 / (jnp.sum(e, axis=1, keepdims=True) + 1e-30)
            p = e * r
            ds = p * (dp - jnp.sum(p * dp, axis=1, keepdims=True))
            out.append(total[h] + own * jnp.sum(ds * s, axis=1, keepdims=True))
            pbuf[at] = p.astype(BF16)
            dsbuf[at] = ds.astype(BF16)
        return tuple(out)

    def grads_of(b):
        at, keys = places(b)
        p, ds = pbuf[...], dsbuf[...]
        two = slice(2 * b, 2 * b + 2) if isinstance(b, int) else pl.ds(2 * b, 2)
        eight = slice(2 * b, 2 * b + span) if isinstance(b, int) else pl.ds(2 * b, span)
        att[two] = gather(dot(p, vhi[keys])).reshape(2, qwide, d)
        gq[two] = gather(dot(ds, khi[keys])).reshape(2, qwide, d)
        gk[eight] += dot(ds, spread(qhi[at]), FIRST).reshape(span, wide, d)
        gv[eight] += dot(p, spread(ghi[at]), FIRST).reshape(span, wide, d)

    bands = qtall // 2
    total = tuple(jnp.zeros((nq, 1), F32) for _ in range(HEADS))
    scores(0)
    total = softmax(0, total)
    scores(1)

    def steady(b, total):
        grads_of(b - 1)
        total = softmax(b, total)
        scores(b + 1)
        return total

    total = lax.fori_loop(1, bands - 1, steady, total)
    grads_of(bands - 2)
    total = softmax(bands - 1, total)
    grads_of(bands - 1)

    n = rows * cols
    at_k = (slice(own_k, own_k + rows), slice(8, 8 + cols))
    at_q = (slice(REACH, REACH + rows), slice(own_q, own_q + cols))

    def unit_back(unit, r, g):
        return r * (g - unit * head_sum(unit * g))

    g_q = unit_back(qf[at_q].reshape(n, d), qr[at_q].reshape(n, d), gq[at_q].reshape(n, d) * sl)
    g_k = unit_back(
        kf[at_k].reshape(n, d), kr[at_k].reshape(n, d), gk[at_k].reshape(n, d) * (1.0 / LOG2E)
    )
    g_v = gv[at_k].reshape(n, d)
    grads = jnp.concatenate([g_q.astype(BF16), g_k.astype(BF16), g_v.astype(BF16)], axis=1)
    gt_ref[...] = dot(grads, wqkv_ref[...], LAST).astype(BF16).reshape(rows, cols, d)
    wq = dot(tok_ref[...].reshape(n, d), grads, FIRST)
    wo = dot(att[at_q].reshape(n, d).astype(BF16), go_ref[...].reshape(n, d), FIRST)
    half = d // 2
    lane = lax.broadcasted_iota(jnp.int32, (8, 4 * d), 1)
    sums = jnp.zeros((8, 4 * d), F32)
    for h in range(HEADS):
        t = jnp.sum(total[h], axis=0, keepdims=True)
        t = t / (scale_ref[h] * LOG2E)
        sums = jnp.where(lane == h, t, sums)
    for c in range(2):
        gw_ref[c, 0:half, 0 : 3 * d] = wq[c * half : (c + 1) * half]
        gw_ref[c, 0:half, 3 * d :] = wo[c * half : (c + 1) * half]
        gw_ref[c, half:, :] = sums


def local_grads(scale, tokens, grad_out, top, bot, left, right, w_qkv, w_out):
    rows, cols, d = tokens.shape
    tall = rows + 4 * REACH
    wide = -(-(cols + 4 * REACH + 2) // 16) * 16
    qtall = rows + 2 * REACH
    qwide = -(-(cols + 2 * REACH + 2) // 8) * 8
    nk = (2 + 2 * REACH) * wide
    vmem = pl.BlockSpec(memory_space=pltpu.VMEM)
    grid = pltpu.VMEM((tall, wide, d), F32)
    qgrid = pltpu.VMEM((qtall, qwide, d), F32)
    flat = pltpu.VMEM((tall * wide, d), BF16)
    qflat = pltpu.VMEM((qtall * qwide, d), BF16)
    tile = lambda dt: pltpu.VMEM((HEADS * 2 * qwide, nk), dt)
    return pl.pallas_call(
        kernel,
        out_shape=(
            jax.ShapeDtypeStruct((rows, cols, d), BF16),
            jax.ShapeDtypeStruct((2, d // 2 + 8, 4 * d), F32),
        ),
        in_specs=[pl.BlockSpec(memory_space=pltpu.SMEM)] + [vmem] * 8,
        out_specs=(vmem, vmem),
        scratch_shapes=[
            grid,
            qgrid,
            pltpu.VMEM(left.shape, F32),
            pltpu.VMEM(top.shape, F32),
            qgrid,
            qgrid,
            grid,
            grid,
            flat,
            flat,
            flat,
            flat,
            qflat,
            qflat,
            qflat,
            qflat,
            tile(F32),
            tile(F32),
            tile(BF16),
            tile(BF16),
            qgrid,
            grid,
            grid,
            qgrid,
        ],
        compiler_params=pltpu.CompilerParams(vmem_limit_bytes=48 * 1024 * 1024),
        cost_estimate=pl.CostEstimate(
            flops=8_000_000_000, bytes_accessed=4_000_000, transcendentals=600_000
        ),
    )(scale, tokens, grad_out, top, bot, left, right, w_qkv, w_out)


def passed(x, axis, by):
    size = lax.axis_size(axis)
    return lax.ppermute(x, axis, [(i, i + by) for i in range(size) if 0 <= i + by < size])


def shards(tokens, grad_out, w_qkv, w_out, scale):
    rows, cols, d = tokens.shape
    wide = 2 * REACH

    def flat(*parts):
        return jnp.concatenate([p.reshape(-1, d) for p in parts], axis=0)

    left = passed(flat(tokens[:, cols - wide :], grad_out[:, cols - REACH :]), "col", 1)
    right = passed(flat(tokens[:, :wide], grad_out[:, :REACH]), "col", -1)
    cut = rows * wide

    def edge(lo_k, lo_q):
        tok = slice(lo_k * wide, (lo_k + wide) * wide)
        go = slice(cut + lo_q * REACH, cut + (lo_q + REACH) * REACH)
        return flat(
            tokens[lo_k : lo_k + wide],
            grad_out[lo_q : lo_q + REACH],
            left[tok],
            right[tok],
            left[go],
            right[go],
        )

    top = passed(edge(rows - wide, rows - REACH), ROW_AXES, 1)
    bot = passed(edge(0, 0), ROW_AXES, -1)

    grad_tokens, partial = local_grads(
        scale, tokens, grad_out, top, bot, left, right, w_qkv, w_out
    )

    lo = lax.axis_index("rowlo")
    swap = [(0, 1), (1, 0)]
    kept = lax.dynamic_index_in_dim(partial, lo, 0, keepdims=False)
    sent = lax.dynamic_index_in_dim(partial, 1 - lo, 0, keepdims=False)
    kept = kept + lax.ppermute(sent, "rowlo", swap)
    half = d // 2
    n = lax.axis_size(SPREAD_AXES)
    pieces = half // n if half % n == 0 else 1
    part = kept[:half].reshape(n, pieces, -1)
    sums = kept[half, :HEADS]
    sums_hi = lax.reduce_precision(sums, 8, 7)
    sums = jnp.concatenate([sums_hi, sums - sums_hi, jnp.zeros((128 - 2 * HEADS,), F32)])
    part = jnp.concatenate(
        [part.astype(BF16), jnp.broadcast_to(sums.astype(BF16), (n, pieces, 128))], axis=2
    )
    part = lax.all_to_all(part, SPREAD_AXES, 0, 0, tiled=True).astype(F32)
    part = jnp.sum(part, axis=0)
    sums = part[0, -128:]
    grad_scale = sums[:HEADS] + sums[HEADS : 2 * HEADS]
    part = part[:, :-128].astype(BF16)
    mine = lax.all_to_all(
        jnp.broadcast_to(part[None], (n,) + part.shape), SPREAD_AXES, 0, 0, tiled=True
    ).reshape(half, 4 * d)
    other = lax.ppermute(mine, "rowlo", swap)
    first = lo == 0
    upper = jnp.where(first, mine, other).astype(F32)
    lower = jnp.where(first, other, mine).astype(F32)
    grads = jnp.concatenate([upper, lower], axis=0)
    return grad_tokens, grads[:, : 3 * d], grads[:, 3 * d :], grad_scale


def solution(mesh):
    n_row, n_col = mesh.devices.shape
    fine = Mesh(mesh.devices.reshape(n_row // 2, 2, n_col), ("rowhi", "rowlo", "col"))
    block = P(ROW_AXES, "col", None)
    return jax.shard_map(
        shards,
        mesh=fine,
        in_specs=(block, block, P(), P(), P()),
        out_specs=(block, P(), P(), P()),
        check_vma=False,
    )
```

```python
import math

import jax
import jax.numpy as jnp
from jax import lax
from jax.experimental import pallas as pl
from jax.experimental.pallas import tpu as pltpu
from jax.sharding import Mesh
from jax.sharding import PartitionSpec as P

HEADS = 4
REACH = 3
F32 = jnp.float32
BF16 = jnp.bfloat16
LAST = (((1,), (1,)), ((), ()))
FIRST = (((0,), (0,)), ((), ()))
LOG2E = math.log2(math.e)
ROW_AXES = ("rowhi", "rowlo")
SPREAD_AXES = ("rowhi", "col")


def dot(a, b, dims=(((1,), (0,)), ((), ()))):
    return lax.dot_general(a, b, dims, preferred_element_type=F32)


def split(x):
    hi = x.astype(BF16)
    return hi, (x - hi.astype(F32)).astype(BF16)


def pin(x):
    return pltpu.with_memory_space_constraint(x, pltpu.HBM)


def piece_layout(rows):
    wide = 2 * REACH
    seg = -(-(wide * wide + REACH * REACH) // 16) * 16
    mid_tok = (rows - 2 * wide) * wide
    mid = -(-(mid_tok + (rows - 2 * REACH) * REACH) // 16) * 16
    tok, go = [], []
    for r in range(rows):
        if r < wide:
            tok.append(r * wide)
        elif r < rows - wide:
            tok.append(seg + (r - wide) * wide)
        else:
            tok.append(seg + mid + (r - rows + wide) * wide)
        if r < REACH:
            go.append(wide * wide + r * REACH)
        elif r < rows - REACH:
            go.append(seg + mid_tok + (r - REACH) * REACH)
        else:
            go.append(seg + mid + wide * wide + (r - rows + REACH) * REACH)
    return seg, seg + mid, 2 * seg + mid, tok, go


def pack(tok_hbm, go_hbm, tok_ref, go_ref, col_a, col_b, row_a, row_b, tf, gf, first, last, sems):
    rows, cols, d = tok_ref.shape
    copies = [
        pltpu.make_async_copy(tok_hbm, tok_ref, sems.at[0]),
        pltpu.make_async_copy(go_hbm, go_ref, sems.at[1]),
    ]
    for c in copies:
        c.start()
    wide = 2 * REACH
    _, _, _, tok_at, go_at = piece_layout(rows)
    even_row = lax.axis_index("rowlo") % 2 == 0
    even_col = lax.axis_index("col") % 2 == 0
    first[...] = jnp.zeros_like(first)
    last[...] = jnp.zeros_like(last)
    for c in copies:
        c.wait()
    tf[...] = tok_ref[...].astype(F32)
    gf[...] = go_ref[...].astype(F32)
    for r in range(rows):
        first[tok_at[r] : tok_at[r] + wide] = tf[r, 0:wide, :]
        last[tok_at[r] : tok_at[r] + wide] = tf[r, cols - wide : cols, :]
        first[go_at[r] : go_at[r] + REACH] = gf[r, 0:REACH, :]
        last[go_at[r] : go_at[r] + REACH] = gf[r, cols - REACH : cols, :]
    lo, hi = first[...], last[...]
    col_a[...] = jnp.where(even_col, hi, lo).astype(BF16)
    col_b[...] = jnp.where(even_col, lo, hi).astype(BF16)
    cut = wide * cols
    end = cut + REACH * cols
    lo = tf[0:wide].reshape(cut, d)
    hi = tf[rows - wide : rows].reshape(cut, d)
    row_a[0:cut] = jnp.where(even_row, hi, lo).astype(BF16)
    row_b[0:cut] = jnp.where(even_row, lo, hi).astype(BF16)
    lo = gf[0:REACH].reshape(end - cut, d)
    hi = gf[rows - REACH : rows].reshape(end - cut, d)
    row_a[cut:end] = jnp.where(even_row, hi, lo).astype(BF16)
    row_b[cut:end] = jnp.where(even_row, lo, hi).astype(BF16)


def packed(tokens, grad_out):
    rows, cols, d = tokens.shape
    size = piece_layout(rows)[2]
    vmem = pl.BlockSpec(memory_space=pltpu.VMEM)
    col = jax.ShapeDtypeStruct((size, d), BF16)
    row = jax.ShapeDtypeStruct((3 * REACH * cols, d), BF16)
    whole = jax.ShapeDtypeStruct((rows, cols, d), BF16)
    block = pltpu.VMEM((rows, cols, d), F32)
    return pl.pallas_call(
        pack,
        out_shape=(whole, whole, col, col, row, row),
        in_specs=[pl.BlockSpec(memory_space=pltpu.HBM)] * 2,
        out_specs=(vmem,) * 6,
        scratch_shapes=[
            block,
            block,
            pltpu.VMEM((size, d), F32),
            pltpu.VMEM((size, d), F32),
            pltpu.SemaphoreType.DMA((2,)),
        ],
        compiler_params=pltpu.CompilerParams(vmem_limit_bytes=8 * 1024 * 1024),
        cost_estimate=pl.CostEstimate(flops=0, bytes_accessed=1_000_000, transcendentals=0),
    )(pin(tokens), pin(grad_out))


def kernel(
    scale_hbm,
    tok_ref,
    go_ref,
    row_a,
    row_b,
    col_a,
    col_b,
    wqkv_hbm,
    wout_hbm,
    gt_ref,
    gw_ref,
    scale_ref,
    wqkv_ref,
    wout_ref,
    sems,
    tx,
    gx,
    side,
    ends,
    qf,
    qr,
    kf,
    kr,
    khi,
    klo,
    vhi,
    vlo,
    qhi,
    qlo,
    ghi,
    glo,
    sbuf,
    dbuf,
    pbuf,
    dsbuf,
    gq,
    gk,
    gv,
    att,
):
    copies = [
        pltpu.make_async_copy(scale_hbm, scale_ref, sems.at[0]),
        pltpu.make_async_copy(wqkv_hbm, wqkv_ref, sems.at[1]),
        pltpu.make_async_copy(wout_hbm, wout_ref, sems.at[2]),
    ]
    for c in copies:
        c.start()
    rows, cols, d = tok_ref.shape
    tall, wide, _ = tx.shape
    qtall, qwide, _ = gx.shape
    per = d // HEADS
    q0 = 8 - REACH - 2
    own_k = 2 * REACH
    own_q = 8 - q0
    n_rows = rows * lax.axis_size(ROW_AXES)
    n_cols = cols * lax.axis_size("col")
    row_first = lax.axis_index(ROW_AXES) * rows
    col_first = lax.axis_index("col") * cols

    tx[:, 0:8, :] = jnp.zeros((tall, 8, d), F32)
    tx[:, 8 + cols : wide, :] = jnp.zeros((tall, wide - 8 - cols, d), F32)
    gx[:, 0:8, :] = jnp.zeros((qtall, 8, d), F32)
    left_k, right_k = 8 - own_k, 8 + cols
    left_q, right_q = own_q - REACH, own_q + cols
    tx[own_k : own_k + rows, 8 : 8 + cols, :] = tok_ref[...].astype(F32)
    gx[REACH : REACH + rows, own_q : own_q + cols, :] = go_ref[...].astype(F32)
    even_row = lax.axis_index("rowlo") % 2 == 0
    even_col = lax.axis_index("col") % 2 == 0
    seg, _, _, tok_at, go_at = piece_layout(rows)
    for even, at_k, at_q in ((~even_col, left_k, left_q), (even_col, right_k, right_q)):
        side[...] = jnp.where(even, col_a[...].astype(F32), col_b[...].astype(F32))
        for r in range(rows):
            tx[own_k + r, at_k : at_k + own_k, :] = side[tok_at[r] : tok_at[r] + own_k]
            gx[REACH + r, at_q : at_q + REACH, :] = side[go_at[r] : go_at[r] + REACH]
    cut = own_k * cols
    end = cut + REACH * cols
    for even, row_k, row_q in ((~even_row, 0, 0), (even_row, own_k + rows, REACH + rows)):
        ends[...] = jnp.where(even, row_a[...].astype(F32), row_b[...].astype(F32))
        tx[row_k : row_k + own_k, 8 : 8 + cols, :] = ends[0:cut].reshape(own_k, cols, d)
        gx[row_q : row_q + REACH, own_q : own_q + cols, :] = ends[cut:end].reshape(REACH, cols, d)
        first, last = ends[end : end + seg], ends[end + seg : end + 2 * seg]
        ends[end : end + seg] = jnp.where(even_col, last, first)
        ends[end + seg : end + 2 * seg] = jnp.where(even_col, first, last)
        for base, at_k, at_q in ((end, left_k, left_q), (end + seg, right_k, right_q)):
            for r in range(own_k):
                at = base + r * own_k
                tx[row_k + r, at_k : at_k + own_k, :] = ends[at : at + own_k]
            for r in range(REACH):
                at = base + own_k * own_k + r * REACH
                gx[row_q + r, at_q : at_q + REACH, :] = ends[at : at + REACH]

    lane_head = lax.broadcasted_iota(jnp.int32, (1, d), 1) // per
    ones = (
        lax.broadcasted_iota(jnp.int32, (d, d), 0) // per
        == lax.broadcasted_iota(jnp.int32, (d, d), 1) // per
    ).astype(BF16)

    def head_sum(x):
        hi, lo = split(x)
        return dot(hi, ones) + dot(lo, ones)

    for c in copies:
        c.wait()
    sl = jnp.zeros((1, d), F32)
    for h in range(HEADS):
        sl = jnp.where(lane_head == h, scale_ref[h], sl)
    head_lanes = [lane_head == h for h in range(HEADS)]

    step = 4
    for c in range(tall // step):
        at = slice(c * step, (c + 1) * step)
        x = tx[at].reshape(step * wide, d).astype(BF16)
        kv = dot(x, wqkv_ref[:, d:])
        k = kv[:, :d]
        rk = lax.rsqrt(head_sum(k * k) + 1e-06)
        k = k * rk
        kf[at] = k.reshape(step, wide, d)
        kr[at] = rk.reshape(step, wide, d)
        flat = slice(c * step * wide, (c + 1) * step * wide)
        khi[flat], klo[flat] = split(k)
        vhi[flat], vlo[flat] = split(kv[:, d:])
    nq = 2 * qwide
    for c in range(0, qtall, 4):
        step = min(4, qtall - c)
        at = slice(c, c + step)
        x = tx[REACH + c : REACH + c + step, q0 : q0 + qwide, :].reshape(step * qwide, d)
        q = dot(x.astype(BF16), wqkv_ref[:, :d])
        rq = lax.rsqrt(head_sum(q * q) + 1e-06)
        q = q * rq
        qf[at] = q.reshape(step, qwide, d)
        qr[at] = rq.reshape(step, qwide, d)
        flat = slice(c * qwide, (c + step) * qwide)
        qhi[flat], qlo[flat] = split(q * (sl * LOG2E))
        g = dot(gx[at].reshape(step * qwide, d).astype(BF16), wout_ref[...], LAST)
        ghi[flat], glo[flat] = split(g)

    gk[...] = jnp.zeros_like(gk)
    gv[...] = jnp.zeros_like(gv)

    span = 2 + 2 * REACH
    nk = span * wide
    i = lax.broadcasted_iota(jnp.int32, (nq, nk), 0)
    j = lax.broadcasted_iota(jnp.int32, (nq, nk), 1)
    dr = j // wide - i // qwide
    dc = j % wide - i % qwide
    key_col = j % wide + (col_first - 8)
    near = (dr >= 0) & (dr <= 2 * REACH) & (dc >= 0) & (dc <= 2 * REACH)
    near = (near & (key_col >= 0) & (key_col < n_cols)).astype(F32)
    jr = lax.broadcasted_iota(jnp.int32, (1, nk), 1) // wide
    iq = lax.broadcasted_iota(jnp.int32, (nq, 1), 0)
    own_col = (iq % qwide >= own_q) & (iq % qwide < own_q + cols)

    def spread(x):
        zero = jnp.zeros_like(x)
        return jnp.concatenate([jnp.where(m, x, zero) for m in head_lanes], axis=0)

    def gather(x):
        out = x[0:nq]
        for h in range(1, HEADS):
            out = jnp.where(head_lanes[h], x[h * nq : (h + 1) * nq], out)
        return out

    def places(b):
        if isinstance(b, int):
            return slice(b * nq, (b + 1) * nq), slice(b * 2 * wide, b * 2 * wide + nk)
        return (
            pl.ds(pl.multiple_of(b * nq, nq), nq),
            pl.ds(pl.multiple_of(b * 2 * wide, 2 * wide), nk),
        )

    def scores(b):
        at, keys = places(b)
        q_hi, q_lo = spread(qhi[at]), spread(qlo[at])
        k_hi = khi[keys]
        sbuf[...] = dot(q_hi, k_hi, LAST) + dot(q_lo, k_hi, LAST) + dot(q_hi, klo[keys], LAST)
        g_hi, g_lo = spread(ghi[at]), spread(glo[at])
        v_hi = vhi[keys]
        dbuf[...] = dot(g_hi, v_hi, LAST) + dot(g_lo, v_hi, LAST) + dot(g_hi, vlo[keys], LAST)

    def softmax(b, total):
        key_row = jr + (row_first - 2 * REACH + 2 * b)
        mask = near * ((key_row >= 0) & (key_row < n_rows)).astype(F32)
        q_row = iq // qwide + 2 * b
        own = (own_col & (q_row >= REACH) & (q_row < REACH + rows)).astype(F32)
        out = []
        for h in range(HEADS):
            at = slice(h * nq, (h + 1) * nq)
            s, dp = sbuf[at], dbuf[at]
            e = jnp.exp2(s) * mask
            r = 1.0 / (jnp.sum(e, axis=1, keepdims=True) + 1e-30)
            p = e * r
            ds = p * (dp - jnp.sum(p * dp, axis=1, keepdims=True))
            out.append(total[h] + own * jnp.sum(ds * s, axis=1, keepdims=True))
            pbuf[at] = p.astype(BF16)
            dsbuf[at] = ds.astype(BF16)
        return tuple(out)

    def grads_of(b):
        at, keys = places(b)
        p, ds = pbuf[...], dsbuf[...]
        two = slice(2 * b, 2 * b + 2) if isinstance(b, int) else pl.ds(2 * b, 2)
        eight = slice(2 * b, 2 * b + span) if isinstance(b, int) else pl.ds(2 * b, span)
        att[two] = gather(dot(p, vhi[keys])).reshape(2, qwide, d)
        gq[two] = gather(dot(ds, khi[keys])).reshape(2, qwide, d)
        gk[eight] += dot(ds, spread(qhi[at]), FIRST).reshape(span, wide, d)
        gv[eight] += dot(p, spread(ghi[at]), FIRST).reshape(span, wide, d)

    bands = qtall // 2
    total = tuple(jnp.zeros((nq, 1), F32) for _ in range(HEADS))
    scores(0)
    total = softmax(0, total)
    scores(1)

    def steady(b, total):
        grads_of(b - 1)
        total = softmax(b, total)
        scores(b + 1)
        return total

    total = lax.fori_loop(1, bands - 1, steady, total)
    grads_of(bands - 2)
    total = softmax(bands - 1, total)
    grads_of(bands - 1)

    n = rows * cols
    at_k = (slice(own_k, own_k + rows), slice(8, 8 + cols))
    at_q = (slice(REACH, REACH + rows), slice(own_q, own_q + cols))

    def unit_back(unit, r, g):
        return r * (g - unit * head_sum(unit * g))

    g_q = unit_back(qf[at_q].reshape(n, d), qr[at_q].reshape(n, d), gq[at_q].reshape(n, d) * sl)
    g_k = unit_back(
        kf[at_k].reshape(n, d), kr[at_k].reshape(n, d), gk[at_k].reshape(n, d) * (1.0 / LOG2E)
    )
    g_v = gv[at_k].reshape(n, d)
    grads = jnp.concatenate([g_q.astype(BF16), g_k.astype(BF16), g_v.astype(BF16)], axis=1)
    gt_ref[...] = dot(grads, wqkv_ref[...], LAST).astype(BF16).reshape(rows, cols, d)
    wq = dot(tok_ref[...].reshape(n, d), grads, FIRST)
    wo = dot(att[at_q].reshape(n, d).astype(BF16), go_ref[...].reshape(n, d), FIRST)
    half = d // 2
    lane = lax.broadcasted_iota(jnp.int32, (8, 4 * d), 1)
    sums = jnp.zeros((8, 4 * d), F32)
    for h in range(HEADS):
        t = jnp.sum(total[h], axis=0, keepdims=True)
        t = t / (scale_ref[h] * LOG2E)
        sums = jnp.where(lane == h, t, sums)
    for c in range(2):
        gw_ref[c, 0:half, 0 : 3 * d] = wq[c * half : (c + 1) * half]
        gw_ref[c, 0:half, 3 * d :] = wo[c * half : (c + 1) * half]
        gw_ref[c, half:, :] = sums


def local_grads(scale, tokens, grad_out, row_a, row_b, col_a, col_b, w_qkv, w_out):
    rows, cols, d = tokens.shape
    tall = rows + 4 * REACH
    wide = -(-(cols + 4 * REACH + 2) // 16) * 16
    qtall = rows + 2 * REACH
    qwide = -(-(cols + 2 * REACH + 2) // 8) * 8
    nk = (2 + 2 * REACH) * wide
    vmem = pl.BlockSpec(memory_space=pltpu.VMEM)
    hbm = pl.BlockSpec(memory_space=pltpu.HBM)
    grid = pltpu.VMEM((tall, wide, d), F32)
    qgrid = pltpu.VMEM((qtall, qwide, d), F32)
    flat = pltpu.VMEM((tall * wide, d), BF16)
    qflat = pltpu.VMEM((qtall * qwide, d), BF16)
    tile = lambda dt: pltpu.VMEM((HEADS * 2 * qwide, nk), dt)
    return pl.pallas_call(
        kernel,
        out_shape=(
            jax.ShapeDtypeStruct((rows, cols, d), BF16),
            jax.ShapeDtypeStruct((2, d // 2 + 8, 4 * d), F32),
        ),
        in_specs=[hbm] + [vmem] * 6 + [hbm] * 2,
        out_specs=(vmem, vmem),
        scratch_shapes=[
            pltpu.SMEM((HEADS,), F32),
            pltpu.VMEM(w_qkv.shape, BF16),
            pltpu.VMEM(w_out.shape, BF16),
            pltpu.SemaphoreType.DMA((3,)),
            grid,
            qgrid,
            pltpu.VMEM(col_a.shape, F32),
            pltpu.VMEM(row_a.shape, F32),
            qgrid,
            qgrid,
            grid,
            grid,
            flat,
            flat,
            flat,
            flat,
            qflat,
            qflat,
            qflat,
            qflat,
            tile(F32),
            tile(F32),
            tile(BF16),
            tile(BF16),
            qgrid,
            grid,
            grid,
            qgrid,
        ],
        compiler_params=pltpu.CompilerParams(vmem_limit_bytes=32 * 1024 * 1024),
        cost_estimate=pl.CostEstimate(
            flops=8_000_000_000, bytes_accessed=4_000_000, transcendentals=600_000
        ),
    )(pin(scale), tokens, grad_out, row_a, row_b, col_a, col_b, pin(w_qkv), pin(w_out))


def swap_pairs(x, axis, first):
    pairs = []
    for i in range(first, lax.axis_size(axis) - 1, 2):
        pairs += [(i, i + 1), (i + 1, i)]
    return lax.ppermute(x, axis, pairs)


def shards(tokens, grad_out, w_qkv, w_out, scale):
    rows, cols, d = tokens.shape
    tokens, grad_out, col_a, col_b, row_a, row_b = packed(tokens, grad_out)
    col_b = swap_pairs(col_b, "col", 1)
    col_a = swap_pairs(col_a, "col", 0)
    seg, last, _, _, _ = piece_layout(rows)
    odd = lax.axis_index("rowlo") % 2

    def with_corners(row, at):
        return jnp.concatenate(
            [row] + [lax.dynamic_slice_in_dim(c, at, seg, 0) for c in (col_a, col_b)], axis=0
        )

    row_b = swap_pairs(with_corners(row_b, odd * last), ROW_AXES, 1)
    row_a = swap_pairs(with_corners(row_a, (1 - odd) * last), ROW_AXES, 0)

    grad_tokens, partial = local_grads(
        scale, tokens, grad_out, row_a, row_b, col_a, col_b, w_qkv, w_out
    )

    lo = lax.axis_index("rowlo")
    swap = [(0, 1), (1, 0)]
    kept = lax.dynamic_index_in_dim(partial, lo, 0, keepdims=False)
    sent = lax.dynamic_index_in_dim(partial, 1 - lo, 0, keepdims=False)
    kept = kept + lax.ppermute(sent, "rowlo", swap)
    half = d // 2
    n = lax.axis_size(SPREAD_AXES)
    pieces = half // n if half % n == 0 else 1
    part = kept[:half].reshape(n, pieces, -1)
    sums = kept[half, :HEADS]
    sums_hi = lax.reduce_precision(sums, 8, 7)
    sums = jnp.concatenate([sums_hi, sums - sums_hi, jnp.zeros((128 - 2 * HEADS,), F32)])
    part = jnp.concatenate(
        [part.astype(BF16), jnp.broadcast_to(sums.astype(BF16), (n, pieces, 128))], axis=2
    )
    part = lax.all_to_all(part, SPREAD_AXES, 0, 0, tiled=True).astype(F32)
    part = jnp.sum(part, axis=0)
    sums = part[0, -128:]
    grad_scale = sums[:HEADS] + sums[HEADS : 2 * HEADS]
    part = part[:, :-128].astype(BF16)
    mine = lax.all_to_all(
        jnp.broadcast_to(part[None], (n,) + part.shape), SPREAD_AXES, 0, 0, tiled=True
    ).reshape(half, 4 * d)
    other = lax.ppermute(mine, "rowlo", swap)
    first = lo == 0
    upper = jnp.where(first, mine, other).astype(F32)
    lower = jnp.where(first, other, mine).astype(F32)
    grads = jnp.concatenate([upper, lower], axis=0)
    return grad_tokens, grads[:, : 3 * d], grads[:, 3 * d :], grad_scale


def solution(mesh):
    n_row, n_col = mesh.devices.shape
    fine = Mesh(mesh.devices.reshape(n_row // 2, 2, n_col), ("rowhi", "rowlo", "col"))
    block = P(ROW_AXES, "col", None)
    return jax.shard_map(
        shards,
        mesh=fine,
        in_specs=(block, block, P(), P(), P()),
        out_specs=(block, P(), P(), P()),
        check_vma=False,
    )
```

```python
import math

import jax
import jax.numpy as jnp
from jax import lax
from jax.experimental import pallas as pl
from jax.experimental.pallas import tpu as pltpu
from jax.sharding import Mesh
from jax.sharding import PartitionSpec as P

HEADS = 4
REACH = 3
F32 = jnp.float32
BF16 = jnp.bfloat16
LAST = (((1,), (1,)), ((), ()))
FIRST = (((0,), (0,)), ((), ()))
LOG2E = math.log2(math.e)
ROW_AXES = ("rowhi", "rowlo")
SPREAD_AXES = ("rowhi", "col")


def dot(a, b, dims=(((1,), (0,)), ((), ()))):
    return lax.dot_general(a, b, dims, preferred_element_type=F32)


def split(x):
    hi = x.astype(BF16)
    return hi, (x - hi.astype(F32)).astype(BF16)


def pin(x):
    return pltpu.with_memory_space_constraint(x, pltpu.HBM)


def piece_layout(rows):
    wide = 2 * REACH
    seg = -(-(wide * wide + REACH * REACH) // 16) * 16
    mid_tok = (rows - 2 * wide) * wide
    mid = -(-(mid_tok + (rows - 2 * REACH) * REACH) // 16) * 16
    tok, go = [], []
    for r in range(rows):
        if r < wide:
            tok.append(r * wide)
        elif r < rows - wide:
            tok.append(seg + (r - wide) * wide)
        else:
            tok.append(seg + mid + (r - rows + wide) * wide)
        if r < REACH:
            go.append(wide * wide + r * REACH)
        elif r < rows - REACH:
            go.append(seg + mid_tok + (r - REACH) * REACH)
        else:
            go.append(seg + mid + wide * wide + (r - rows + REACH) * REACH)
    return seg, seg + mid, 2 * seg + mid, tok, go


def pack(tok_hbm, go_hbm, tok_ref, go_ref, col_a, col_b, row_a, row_b, tf, gf, first, last, sems):
    rows, cols, d = tok_ref.shape
    copies = [
        pltpu.make_async_copy(tok_hbm, tok_ref, sems.at[0]),
        pltpu.make_async_copy(go_hbm, go_ref, sems.at[1]),
    ]
    for c in copies:
        c.start()
    wide = 2 * REACH
    _, _, _, tok_at, go_at = piece_layout(rows)
    even_row = lax.axis_index("rowlo") % 2 == 0
    even_col = lax.axis_index("col") % 2 == 0
    first[...] = jnp.zeros_like(first)
    last[...] = jnp.zeros_like(last)
    for c in copies:
        c.wait()
    tf[...] = tok_ref[...].astype(F32)
    gf[...] = go_ref[...].astype(F32)
    for r in range(rows):
        first[tok_at[r] : tok_at[r] + wide] = tf[r, 0:wide, :]
        last[tok_at[r] : tok_at[r] + wide] = tf[r, cols - wide : cols, :]
        first[go_at[r] : go_at[r] + REACH] = gf[r, 0:REACH, :]
        last[go_at[r] : go_at[r] + REACH] = gf[r, cols - REACH : cols, :]
    lo, hi = first[...], last[...]
    col_a[...] = jnp.where(even_col, hi, lo).astype(BF16)
    col_b[...] = jnp.where(even_col, lo, hi).astype(BF16)
    cut = wide * cols
    end = cut + REACH * cols
    lo = tf[0:wide].reshape(cut, d)
    hi = tf[rows - wide : rows].reshape(cut, d)
    row_a[0:cut] = jnp.where(even_row, hi, lo).astype(BF16)
    row_b[0:cut] = jnp.where(even_row, lo, hi).astype(BF16)
    lo = gf[0:REACH].reshape(end - cut, d)
    hi = gf[rows - REACH : rows].reshape(end - cut, d)
    row_a[cut:end] = jnp.where(even_row, hi, lo).astype(BF16)
    row_b[cut:end] = jnp.where(even_row, lo, hi).astype(BF16)


def packed(tokens, grad_out):
    rows, cols, d = tokens.shape
    size = piece_layout(rows)[2]
    vmem = pl.BlockSpec(memory_space=pltpu.VMEM)
    col = jax.ShapeDtypeStruct((size, d), BF16)
    row = jax.ShapeDtypeStruct((3 * REACH * cols, d), BF16)
    whole = jax.ShapeDtypeStruct((rows, cols, d), BF16)
    block = pltpu.VMEM((rows, cols, d), F32)
    return pl.pallas_call(
        pack,
        out_shape=(whole, whole, col, col, row, row),
        in_specs=[pl.BlockSpec(memory_space=pltpu.HBM)] * 2,
        out_specs=(vmem,) * 6,
        scratch_shapes=[
            block,
            block,
            pltpu.VMEM((size, d), F32),
            pltpu.VMEM((size, d), F32),
            pltpu.SemaphoreType.DMA((2,)),
        ],
        compiler_params=pltpu.CompilerParams(vmem_limit_bytes=8 * 1024 * 1024),
        cost_estimate=pl.CostEstimate(flops=0, bytes_accessed=1_000_000, transcendentals=0),
    )(pin(tokens), pin(grad_out))


def kernel(
    scale_hbm,
    tok_ref,
    go_ref,
    row_a,
    row_b,
    col_a,
    col_b,
    wqkv_hbm,
    wout_hbm,
    gt_ref,
    gw_ref,
    scale_ref,
    wqkv_ref,
    wout_ref,
    sems,
    tx,
    gx,
    side,
    ends,
    qf,
    qr,
    kf,
    kr,
    khi,
    klo,
    vhi,
    vlo,
    qhi,
    qlo,
    ghi,
    glo,
    sbuf,
    dbuf,
    pbuf,
    dsbuf,
    gq,
    gk,
    gv,
    att,
):
    copies = [
        pltpu.make_async_copy(scale_hbm, scale_ref, sems.at[0]),
        pltpu.make_async_copy(wqkv_hbm, wqkv_ref, sems.at[1]),
        pltpu.make_async_copy(wout_hbm, wout_ref, sems.at[2]),
    ]
    for c in copies:
        c.start()
    rows, cols, d = tok_ref.shape
    tall, wide, _ = tx.shape
    qtall, qwide, _ = gx.shape
    per = d // HEADS
    q0 = 8 - REACH - 2
    own_k = 2 * REACH
    own_q = 8 - q0
    n_rows = rows * lax.axis_size(ROW_AXES)
    n_cols = cols * lax.axis_size("col")
    row_first = lax.axis_index(ROW_AXES) * rows
    col_first = lax.axis_index("col") * cols

    tx[:, 0:8, :] = jnp.zeros((tall, 8, d), F32)
    tx[:, 8 + cols : wide, :] = jnp.zeros((tall, wide - 8 - cols, d), F32)
    gx[:, 0:8, :] = jnp.zeros((qtall, 8, d), F32)
    left_k, right_k = 8 - own_k, 8 + cols
    left_q, right_q = own_q - REACH, own_q + cols
    tx[own_k : own_k + rows, 8 : 8 + cols, :] = tok_ref[...].astype(F32)
    gx[REACH : REACH + rows, own_q : own_q + cols, :] = go_ref[...].astype(F32)
    even_row = lax.axis_index("rowlo") % 2 == 0
    even_col = lax.axis_index("col") % 2 == 0
    seg, _, _, tok_at, go_at = piece_layout(rows)
    for even, at_k, at_q in ((~even_col, left_k, left_q), (even_col, right_k, right_q)):
        side[...] = jnp.where(even, col_a[...].astype(F32), col_b[...].astype(F32))
        for r in range(rows):
            tx[own_k + r, at_k : at_k + own_k, :] = side[tok_at[r] : tok_at[r] + own_k]
            gx[REACH + r, at_q : at_q + REACH, :] = side[go_at[r] : go_at[r] + REACH]
    cut = own_k * cols
    end = cut + REACH * cols
    for even, row_k, row_q in ((~even_row, 0, 0), (even_row, own_k + rows, REACH + rows)):
        ends[...] = jnp.where(even, row_a[...].astype(F32), row_b[...].astype(F32))
        tx[row_k : row_k + own_k, 8 : 8 + cols, :] = ends[0:cut].reshape(own_k, cols, d)
        gx[row_q : row_q + REACH, own_q : own_q + cols, :] = ends[cut:end].reshape(REACH, cols, d)
        first, last = ends[end : end + seg], ends[end + seg : end + 2 * seg]
        ends[end : end + seg] = jnp.where(even_col, last, first)
        ends[end + seg : end + 2 * seg] = jnp.where(even_col, first, last)
        for base, at_k, at_q in ((end, left_k, left_q), (end + seg, right_k, right_q)):
            for r in range(own_k):
                at = base + r * own_k
                tx[row_k + r, at_k : at_k + own_k, :] = ends[at : at + own_k]
            for r in range(REACH):
                at = base + own_k * own_k + r * REACH
                gx[row_q + r, at_q : at_q + REACH, :] = ends[at : at + REACH]

    lane_head = lax.broadcasted_iota(jnp.int32, (1, d), 1) // per
    ones = (
        lax.broadcasted_iota(jnp.int32, (d, d), 0) // per
        == lax.broadcasted_iota(jnp.int32, (d, d), 1) // per
    ).astype(BF16)

    def head_sum(x):
        hi, lo = split(x)
        return dot(hi, ones) + dot(lo, ones)

    for c in copies:
        c.wait()
    sl = jnp.zeros((1, d), F32)
    for h in range(HEADS):
        sl = jnp.where(lane_head == h, scale_ref[h], sl)
    head_lanes = [lane_head == h for h in range(HEADS)]

    step = tall // 4 if tall % 4 == 0 else 1
    for c in range(tall // step):
        at = slice(c * step, (c + 1) * step)
        x = tx[at].reshape(step * wide, d).astype(BF16)
        kv = dot(x, wqkv_ref[:, d:])
        k = kv[:, :d]
        rk = lax.rsqrt(head_sum(k * k) + 1e-06)
        k = k * rk
        kf[at] = k.reshape(step, wide, d)
        kr[at] = rk.reshape(step, wide, d)
        flat = slice(c * step * wide, (c + 1) * step * wide)
        khi[flat], klo[flat] = split(k)
        vhi[flat], vlo[flat] = split(kv[:, d:])
    nq = 2 * qwide
    step = qtall // 2
    step += step % 2
    for c in range(0, qtall, step):
        step = min(step, qtall - c)
        at = slice(c, c + step)
        x = tx[REACH + c : REACH + c + step, q0 : q0 + qwide, :].reshape(step * qwide, d)
        q = dot(x.astype(BF16), wqkv_ref[:, :d])
        rq = lax.rsqrt(head_sum(q * q) + 1e-06)
        q = q * rq
        qf[at] = q.reshape(step, qwide, d)
        qr[at] = rq.reshape(step, qwide, d)
        flat = slice(c * qwide, (c + step) * qwide)
        qhi[flat], qlo[flat] = split(q * (sl * LOG2E))
        g = dot(gx[at].reshape(step * qwide, d).astype(BF16), wout_ref[...], LAST)
        ghi[flat], glo[flat] = split(g)

    gk[...] = jnp.zeros_like(gk)
    gv[...] = jnp.zeros_like(gv)

    span = 2 + 2 * REACH
    nk = span * wide
    i = lax.broadcasted_iota(jnp.int32, (nq, nk), 0)
    j = lax.broadcasted_iota(jnp.int32, (nq, nk), 1)
    dr = j // wide - i // qwide
    dc = j % wide - i % qwide
    key_col = j % wide + (col_first - 8)
    near = (dr >= 0) & (dr <= 2 * REACH) & (dc >= 0) & (dc <= 2 * REACH)
    near = (near & (key_col >= 0) & (key_col < n_cols)).astype(F32)
    jr = lax.broadcasted_iota(jnp.int32, (1, nk), 1) // wide
    iq = lax.broadcasted_iota(jnp.int32, (nq, 1), 0)
    own_col = (iq % qwide >= own_q) & (iq % qwide < own_q + cols)

    def spread(x):
        zero = jnp.zeros_like(x)
        return jnp.concatenate([jnp.where(m, x, zero) for m in head_lanes], axis=0)

    def gather(x):
        out = x[0:nq]
        for h in range(1, HEADS):
            out = jnp.where(head_lanes[h], x[h * nq : (h + 1) * nq], out)
        return out

    def places(b):
        if isinstance(b, int):
            return slice(b * nq, (b + 1) * nq), slice(b * 2 * wide, b * 2 * wide + nk)
        return (
            pl.ds(pl.multiple_of(b * nq, nq), nq),
            pl.ds(pl.multiple_of(b * 2 * wide, 2 * wide), nk),
        )

    def scores(b):
        at, keys = places(b)
        q_hi, q_lo = spread(qhi[at]), spread(qlo[at])
        k_hi = khi[keys]
        sbuf[...] = dot(q_hi, k_hi, LAST) + dot(q_lo, k_hi, LAST) + dot(q_hi, klo[keys], LAST)
        g_hi, g_lo = spread(ghi[at]), spread(glo[at])
        v_hi = vhi[keys]
        dbuf[...] = dot(g_hi, v_hi, LAST) + dot(g_lo, v_hi, LAST) + dot(g_hi, vlo[keys], LAST)

    def softmax(b, total):
        key_row = jr + (row_first - 2 * REACH + 2 * b)
        mask = near * ((key_row >= 0) & (key_row < n_rows)).astype(F32)
        q_row = iq // qwide + 2 * b
        own = (own_col & (q_row >= REACH) & (q_row < REACH + rows)).astype(F32)
        out = []
        for h in range(HEADS):
            at = slice(h * nq, (h + 1) * nq)
            s, dp = sbuf[at], dbuf[at]
            e = jnp.exp2(s) * mask
            r = 1.0 / (jnp.sum(e, axis=1, keepdims=True) + 1e-30)
            p = e * r
            ds = p * (dp - jnp.sum(p * dp, axis=1, keepdims=True))
            out.append(total[h] + own * jnp.sum(ds * s, axis=1, keepdims=True))
            pbuf[at] = p.astype(BF16)
            dsbuf[at] = ds.astype(BF16)
        return tuple(out)

    def grads_of(b):
        at, keys = places(b)
        p, ds = pbuf[...], dsbuf[...]
        two = slice(2 * b, 2 * b + 2) if isinstance(b, int) else pl.ds(2 * b, 2)
        eight = slice(2 * b, 2 * b + span) if isinstance(b, int) else pl.ds(2 * b, span)
        att[two] = gather(dot(p, vhi[keys])).reshape(2, qwide, d)
        gq[two] = gather(dot(ds, khi[keys])).reshape(2, qwide, d)
        gk[eight] += dot(ds, spread(qhi[at]), FIRST).reshape(span, wide, d)
        gv[eight] += dot(p, spread(ghi[at]), FIRST).reshape(span, wide, d)

    bands = qtall // 2
    total = tuple(jnp.zeros((nq, 1), F32) for _ in range(HEADS))
    scores(0)
    total = softmax(0, total)
    scores(1)

    def steady(b, total):
        grads_of(b - 1)
        total = softmax(b, total)
        scores(b + 1)
        return total

    for b in range(1, bands - 1):
        total = steady(b, total)
    grads_of(bands - 2)
    total = softmax(bands - 1, total)
    grads_of(bands - 1)

    n = rows * cols
    at_k = (slice(own_k, own_k + rows), slice(8, 8 + cols))
    at_q = (slice(REACH, REACH + rows), slice(own_q, own_q + cols))

    def unit_back(unit, r, g):
        return r * (g - unit * head_sum(unit * g))

    g_q = unit_back(qf[at_q].reshape(n, d), qr[at_q].reshape(n, d), gq[at_q].reshape(n, d) * sl)
    g_k = unit_back(
        kf[at_k].reshape(n, d), kr[at_k].reshape(n, d), gk[at_k].reshape(n, d) * (1.0 / LOG2E)
    )
    g_v = gv[at_k].reshape(n, d)
    grads = jnp.concatenate([g_q.astype(BF16), g_k.astype(BF16), g_v.astype(BF16)], axis=1)
    gt_ref[...] = dot(grads, wqkv_ref[...], LAST).astype(BF16).reshape(rows, cols, d)
    wq = dot(tok_ref[...].reshape(n, d), grads, FIRST)
    wo = dot(att[at_q].reshape(n, d).astype(BF16), go_ref[...].reshape(n, d), FIRST)
    half = d // 2
    lane = lax.broadcasted_iota(jnp.int32, (8, 4 * d), 1)
    sums = jnp.zeros((8, 4 * d), F32)
    for h in range(HEADS):
        t = jnp.sum(total[h], axis=0, keepdims=True)
        t = t / (scale_ref[h] * LOG2E)
        sums = jnp.where(lane == h, t, sums)
    for c in range(2):
        gw_ref[c, 0:half, 0 : 3 * d] = wq[c * half : (c + 1) * half]
        gw_ref[c, 0:half, 3 * d :] = wo[c * half : (c + 1) * half]
        gw_ref[c, half:, :] = sums


def local_grads(scale, tokens, grad_out, row_a, row_b, col_a, col_b, w_qkv, w_out):
    rows, cols, d = tokens.shape
    tall = rows + 4 * REACH
    wide = -(-(cols + 4 * REACH + 2) // 16) * 16
    qtall = rows + 2 * REACH
    qwide = -(-(cols + 2 * REACH + 2) // 8) * 8
    nk = (2 + 2 * REACH) * wide
    vmem = pl.BlockSpec(memory_space=pltpu.VMEM)
    hbm = pl.BlockSpec(memory_space=pltpu.HBM)
    grid = pltpu.VMEM((tall, wide, d), F32)
    qgrid = pltpu.VMEM((qtall, qwide, d), F32)
    flat = pltpu.VMEM((tall * wide, d), BF16)
    qflat = pltpu.VMEM((qtall * qwide, d), BF16)
    tile = lambda dt: pltpu.VMEM((HEADS * 2 * qwide, nk), dt)
    return pl.pallas_call(
        kernel,
        out_shape=(
            jax.ShapeDtypeStruct((rows, cols, d), BF16),
            jax.ShapeDtypeStruct((2, d // 2 + 8, 4 * d), F32),
        ),
        in_specs=[hbm] + [vmem] * 6 + [hbm] * 2,
        out_specs=(vmem, vmem),
        scratch_shapes=[
            pltpu.SMEM((HEADS,), F32),
            pltpu.VMEM(w_qkv.shape, BF16),
            pltpu.VMEM(w_out.shape, BF16),
            pltpu.SemaphoreType.DMA((3,)),
            grid,
            qgrid,
            pltpu.VMEM(col_a.shape, F32),
            pltpu.VMEM(row_a.shape, F32),
            qgrid,
            qgrid,
            grid,
            grid,
            flat,
            flat,
            flat,
            flat,
            qflat,
            qflat,
            qflat,
            qflat,
            tile(F32),
            tile(F32),
            tile(BF16),
            tile(BF16),
            qgrid,
            grid,
            grid,
            qgrid,
        ],
        compiler_params=pltpu.CompilerParams(vmem_limit_bytes=32 * 1024 * 1024),
        cost_estimate=pl.CostEstimate(
            flops=8_000_000_000, bytes_accessed=4_000_000, transcendentals=600_000
        ),
    )(pin(scale), tokens, grad_out, row_a, row_b, col_a, col_b, pin(w_qkv), pin(w_out))


def finish(mine_ref, other_ref, wqkv_ref, wout_ref):
    half = mine_ref.shape[0]
    width = wqkv_ref.shape[1]
    first = lax.axis_index("rowlo") == 0
    mine, other = mine_ref[...].astype(F32), other_ref[...].astype(F32)
    upper = jnp.where(first, mine, other)
    lower = jnp.where(first, other, mine)
    wqkv_ref[0:half] = upper[:, :width]
    wout_ref[0:half] = upper[:, width:]
    wqkv_ref[half:] = lower[:, :width]
    wout_ref[half:] = lower[:, width:]


def finished(mine, other):
    half, width = mine.shape
    d = 2 * half
    vmem = pl.BlockSpec(memory_space=pltpu.VMEM)
    return pl.pallas_call(
        finish,
        out_shape=(
            jax.ShapeDtypeStruct((d, width - d), F32),
            jax.ShapeDtypeStruct((d, d), F32),
        ),
        in_specs=[vmem] * 2,
        out_specs=(vmem, vmem),
        compiler_params=pltpu.CompilerParams(vmem_limit_bytes=8 * 1024 * 1024),
        cost_estimate=pl.CostEstimate(flops=0, bytes_accessed=2_000_000, transcendentals=0),
    )(mine, other)


def swap_pairs(x, axis, first):
    pairs = []
    for i in range(first, lax.axis_size(axis) - 1, 2):
        pairs += [(i, i + 1), (i + 1, i)]
    return lax.ppermute(x, axis, pairs)


def shards(tokens, grad_out, w_qkv, w_out, scale):
    rows, cols, d = tokens.shape
    tokens, grad_out, col_a, col_b, row_a, row_b = packed(tokens, grad_out)
    col_b = swap_pairs(col_b, "col", 1)
    col_a = swap_pairs(col_a, "col", 0)
    seg, last, _, _, _ = piece_layout(rows)
    odd = lax.axis_index("rowlo") % 2

    def with_corners(row, at):
        return jnp.concatenate(
            [row] + [lax.dynamic_slice_in_dim(c, at, seg, 0) for c in (col_a, col_b)], axis=0
        )

    row_b = swap_pairs(with_corners(row_b, odd * last), ROW_AXES, 1)
    row_a = swap_pairs(with_corners(row_a, (1 - odd) * last), ROW_AXES, 0)

    grad_tokens, partial = local_grads(
        scale, tokens, grad_out, row_a, row_b, col_a, col_b, w_qkv, w_out
    )

    lo = lax.axis_index("rowlo")
    swap = [(0, 1), (1, 0)]
    kept = lax.dynamic_index_in_dim(partial, lo, 0, keepdims=False)
    sent = lax.dynamic_index_in_dim(partial, 1 - lo, 0, keepdims=False)
    kept = kept + lax.ppermute(sent, "rowlo", swap)
    half = d // 2
    n = lax.axis_size(SPREAD_AXES)
    pieces = half // n if half % n == 0 else 1
    part = kept[:half].reshape(n, pieces, -1)
    sums = kept[half, :HEADS]
    sums_hi = lax.reduce_precision(sums, 8, 7)
    sums = jnp.concatenate([sums_hi, sums - sums_hi, jnp.zeros((128 - 2 * HEADS,), F32)])
    part = jnp.concatenate(
        [part.astype(BF16), jnp.broadcast_to(sums.astype(BF16), (n, pieces, 128))], axis=2
    )
    part = lax.all_to_all(part, SPREAD_AXES, 0, 0, tiled=True).astype(F32)
    part = jnp.sum(part, axis=0)
    sums = part[0, -128:]
    grad_scale = sums[:HEADS] + sums[HEADS : 2 * HEADS]
    part = part[:, :-128].astype(BF16)
    mine = lax.all_to_all(
        jnp.broadcast_to(part[None], (n,) + part.shape), SPREAD_AXES, 0, 0, tiled=True
    ).reshape(half, 4 * d)
    other = lax.ppermute(mine, "rowlo", swap)
    grad_wqkv, grad_wout = finished(mine, other)
    return grad_tokens, grad_wqkv, grad_wout, grad_scale


def solution(mesh):
    n_row, n_col = mesh.devices.shape
    fine = Mesh(mesh.devices.reshape(n_row // 2, 2, n_col), ("rowhi", "rowlo", "col"))
    block = P(ROW_AXES, "col", None)
    return jax.shard_map(
        shards,
        mesh=fine,
        in_specs=(block, block, P(), P(), P()),
        out_specs=(block, P(), P(), P()),
        check_vma=False,
    )
```

```python
import math

import jax
import jax.numpy as jnp
from jax import lax
from jax.experimental import pallas as pl
from jax.experimental.pallas import tpu as pltpu
from jax.sharding import Mesh
from jax.sharding import PartitionSpec as P

HEADS = 4
REACH = 3
F32 = jnp.float32
BF16 = jnp.bfloat16
LAST = (((1,), (1,)), ((), ()))
FIRST = (((0,), (0,)), ((), ()))
LOG2E = math.log2(math.e)
ROW_AXES = ("rowhi", "rowlo")
SPREAD_AXES = ("rowhi", "col")


def dot(a, b, dims=(((1,), (0,)), ((), ()))):
    return lax.dot_general(a, b, dims, preferred_element_type=F32)


def split(x):
    hi = x.astype(BF16)
    return hi, (x - hi.astype(F32)).astype(BF16)


def pin(x):
    return pltpu.with_memory_space_constraint(x, pltpu.HBM)


def piece_layout(rows):
    wide = 2 * REACH
    seg = -(-(wide * wide + REACH * REACH) // 16) * 16
    mid_tok = (rows - 2 * wide) * wide
    mid = -(-(mid_tok + (rows - 2 * REACH) * REACH) // 16) * 16
    tok, go = [], []
    for r in range(rows):
        if r < wide:
            tok.append(r * wide)
        elif r < rows - wide:
            tok.append(seg + (r - wide) * wide)
        else:
            tok.append(seg + mid + (r - rows + wide) * wide)
        if r < REACH:
            go.append(wide * wide + r * REACH)
        elif r < rows - REACH:
            go.append(seg + mid_tok + (r - REACH) * REACH)
        else:
            go.append(seg + mid + wide * wide + (r - rows + REACH) * REACH)
    return seg, seg + mid, 2 * seg + mid, tok, go


def pack(tok_hbm, go_hbm, tok_ref, go_ref, col_a, col_b, row_a, row_b, tf, gf, first, last, sems):
    rows, cols, d = tok_ref.shape
    copies = [
        pltpu.make_async_copy(tok_hbm, tok_ref, sems.at[0]),
        pltpu.make_async_copy(go_hbm, go_ref, sems.at[1]),
    ]
    for c in copies:
        c.start()
    wide = 2 * REACH
    _, _, _, tok_at, go_at = piece_layout(rows)
    even_row = lax.axis_index("rowlo") % 2 == 0
    even_col = lax.axis_index("col") % 2 == 0
    first[...] = jnp.zeros_like(first)
    last[...] = jnp.zeros_like(last)
    for c in copies:
        c.wait()
    tf[...] = tok_ref[...].astype(F32)
    gf[...] = go_ref[...].astype(F32)
    for r in range(rows):
        first[tok_at[r] : tok_at[r] + wide] = tf[r, 0:wide, :]
        last[tok_at[r] : tok_at[r] + wide] = tf[r, cols - wide : cols, :]
        first[go_at[r] : go_at[r] + REACH] = gf[r, 0:REACH, :]
        last[go_at[r] : go_at[r] + REACH] = gf[r, cols - REACH : cols, :]
    lo, hi = first[...], last[...]
    col_a[...] = jnp.where(even_col, hi, lo).astype(BF16)
    col_b[...] = jnp.where(even_col, lo, hi).astype(BF16)
    cut = wide * cols
    end = cut + REACH * cols
    lo = tf[0:wide].reshape(cut, d)
    hi = tf[rows - wide : rows].reshape(cut, d)
    row_a[0:cut] = jnp.where(even_row, hi, lo).astype(BF16)
    row_b[0:cut] = jnp.where(even_row, lo, hi).astype(BF16)
    lo = gf[0:REACH].reshape(end - cut, d)
    hi = gf[rows - REACH : rows].reshape(end - cut, d)
    row_a[cut:end] = jnp.where(even_row, hi, lo).astype(BF16)
    row_b[cut:end] = jnp.where(even_row, lo, hi).astype(BF16)


def packed(tokens, grad_out):
    rows, cols, d = tokens.shape
    size = piece_layout(rows)[2]
    vmem = pl.BlockSpec(memory_space=pltpu.VMEM)
    col = jax.ShapeDtypeStruct((size, d), BF16)
    row = jax.ShapeDtypeStruct((3 * REACH * cols, d), BF16)
    whole = jax.ShapeDtypeStruct((rows, cols, d), BF16)
    block = pltpu.VMEM((rows, cols, d), F32)
    return pl.pallas_call(
        pack,
        out_shape=(whole, whole, col, col, row, row),
        in_specs=[pl.BlockSpec(memory_space=pltpu.HBM)] * 2,
        out_specs=(vmem,) * 6,
        scratch_shapes=[
            block,
            block,
            pltpu.VMEM((size, d), F32),
            pltpu.VMEM((size, d), F32),
            pltpu.SemaphoreType.DMA((2,)),
        ],
        compiler_params=pltpu.CompilerParams(vmem_limit_bytes=8 * 1024 * 1024),
        cost_estimate=pl.CostEstimate(flops=0, bytes_accessed=1_000_000, transcendentals=0),
    )(pin(tokens), pin(grad_out))


def unit(x, head_sum):
    r = lax.rsqrt(head_sum(x * x) + 1e-06)
    return x * r, r


def tools(d):
    per = d // HEADS
    lane_head = lax.broadcasted_iota(jnp.int32, (1, d), 1) // per
    heads = [lane_head == h for h in range(HEADS)]
    ones = (
        lax.broadcasted_iota(jnp.int32, (d, d), 0) // per
        == lax.broadcasted_iota(jnp.int32, (d, d), 1) // per
    ).astype(BF16)

    def head_sum(x):
        hi, lo = split(x)
        return dot(hi, ones) + dot(lo, ones)

    def spread(x):
        zero = jnp.zeros_like(x)
        return jnp.concatenate([jnp.where(m, x, zero) for m in heads], axis=0)

    def gather(x):
        n = x.shape[0] // HEADS
        out = x[0:n]
        for h in range(1, HEADS):
            out = jnp.where(heads[h], x[h * n : (h + 1) * n], out)
        return out

    return heads, head_sum, spread, gather


def near_mask(qwide, wide, cols):
    nq, nk = 2 * qwide, (2 + 2 * REACH) * wide
    i = lax.broadcasted_iota(jnp.int32, (nq, nk), 0)
    j = lax.broadcasted_iota(jnp.int32, (nq, nk), 1)
    dr = j // wide - i // qwide
    dc = j % wide - i % qwide
    key_col = j % wide + (lax.axis_index("col") * cols - 8)
    near = (dr >= 0) & (dr <= 2 * REACH) & (dc >= 0) & (dc <= 2 * REACH)
    near = near & (key_col >= 0) & (key_col < cols * lax.axis_size("col"))
    return near.astype(F32)


def run_bands(bands, sbuf, dbuf, pbuf, dsbuf, nq, spread):
    def scores(band):
        q_hi, q_lo = spread(band["q_hi"]()), spread(band["q_lo"]())
        k_hi = band["k_hi"]()
        sbuf[...] = dot(q_hi, k_hi, LAST) + dot(q_lo, k_hi, LAST) + dot(q_hi, band["k_lo"](), LAST)
        g_hi, g_lo = spread(band["g_hi"]()), spread(band["g_lo"]())
        v_hi = band["v_hi"]()
        dbuf[...] = dot(g_hi, v_hi, LAST) + dot(g_lo, v_hi, LAST) + dot(g_hi, band["v_lo"](), LAST)

    def softmax(band, total):
        mask, own = band["mask"](), band["own"]()
        out = []
        for h in range(HEADS):
            at = slice(h * nq, (h + 1) * nq)
            s, dp = sbuf[at], dbuf[at]
            e = jnp.exp2(s) * mask
            r = 1.0 / (jnp.sum(e, axis=1, keepdims=True) + 1e-30)
            p = e * r
            ds = p * (dp - jnp.sum(p * dp, axis=1, keepdims=True))
            if own is None:
                out.append(total[h])
            else:
                out.append(total[h] + own * jnp.sum(ds * s, axis=1, keepdims=True))
            pbuf[at] = p.astype(BF16)
            dsbuf[at] = ds.astype(BF16)
        return out

    total = [jnp.zeros((nq, 1), F32) for _ in range(HEADS)]
    count = len(bands)
    scores(bands[0])
    for b in range(count + 1):
        if b > 0:
            bands[b - 1]["grads"](pbuf, dsbuf)
        if b < count:
            total = softmax(bands[b], total)
        if b + 1 < count:
            scores(bands[b + 1])
    return [jnp.sum(t, axis=0, keepdims=True) for t in total]


def inner(
    scale_hbm,
    tok_ref,
    go_ref,
    col_a,
    col_b,
    wqkv_hbm,
    wout_hbm,
    sl_ref,
    wqkv_ref,
    wout_ref,
    khi,
    klo,
    vhi,
    vlo,
    kf,
    kr,
    qf,
    qr,
    ga_ref,
    gq,
    att,
    gk,
    gv,
    psum,
    scale_ref,
    sems,
    tx,
    gx,
    side,
    qhi,
    qlo,
    ghi,
    glo,
    sbuf,
    dbuf,
    pbuf,
    dsbuf,
):
    copies = [
        pltpu.make_async_copy(scale_hbm, scale_ref, sems.at[0]),
        pltpu.make_async_copy(wqkv_hbm, wqkv_ref, sems.at[1]),
        pltpu.make_async_copy(wout_hbm, wout_ref, sems.at[2]),
    ]
    for c in copies:
        c.start()
    rows, cols, d = tok_ref.shape
    _, wide, _ = tx.shape
    _, qwide, _ = gx.shape
    reach2 = 2 * REACH
    q0 = 8 - REACH - 2
    own_q = 8 - q0
    heads, head_sum, spread, gather = tools(d)

    tx[:, 0:8, :] = jnp.zeros((rows, 8, d), F32)
    tx[:, 8 + cols : wide, :] = jnp.zeros((rows, wide - 8 - cols, d), F32)
    gx[:, 0:8, :] = jnp.zeros((rows, 8, d), F32)
    tx[:, 8 : 8 + cols, :] = tok_ref[...].astype(F32)
    gx[:, own_q : own_q + cols, :] = go_ref[...].astype(F32)
    even_col = lax.axis_index("col") % 2 == 0
    _, _, _, tok_at, go_at = piece_layout(rows)
    for even, at_k, at_q in (
        (~even_col, 8 - reach2, own_q - REACH),
        (even_col, 8 + cols, own_q + cols),
    ):
        side[...] = jnp.where(even, col_a[...].astype(F32), col_b[...].astype(F32))
        for r in range(rows):
            tx[r, at_k : at_k + reach2, :] = side[tok_at[r] : tok_at[r] + reach2]
            gx[r, at_q : at_q + REACH, :] = side[go_at[r] : go_at[r] + REACH]

    for c in copies:
        c.wait()
    sl = jnp.zeros((1, d), F32)
    for h in range(HEADS):
        sl = jnp.where(heads[h], scale_ref[h], sl)
    sl_ref[...] = jnp.broadcast_to(sl, sl_ref.shape)

    step = rows // 2
    for c in range(0, rows, step):
        at = slice(c, c + step)
        x = tx[at].reshape(step * wide, d).astype(BF16)
        kv = dot(x, wqkv_ref[:, d:])
        k, rk = unit(kv[:, :d], head_sum)
        kf[at] = k.reshape(step, wide, d)
        kr[at] = rk.reshape(step, wide, d)
        flat = slice(c * wide, (c + step) * wide)
        khi[flat], klo[flat] = split(k)
        vhi[flat], vlo[flat] = split(kv[:, d:])
    x = tx[:, q0 : q0 + qwide, :].reshape(rows * qwide, d).astype(BF16)
    q, rq = unit(dot(x, wqkv_ref[:, :d]), head_sum)
    qf[...] = q.reshape(rows, qwide, d)
    qr[...] = rq.reshape(rows, qwide, d)
    g = dot(gx[...].reshape(rows * qwide, d).astype(BF16), wout_ref[...], LAST)
    lo, hi = REACH * qwide, (rows - REACH) * qwide
    qhi[...], qlo[...] = split(q[lo:hi] * (sl * LOG2E))
    ghi[...], glo[...] = split(g[lo:hi])
    ga_ref[0:REACH] = g[0:lo].reshape(REACH, qwide, d)
    ga_ref[REACH:] = g[hi:].reshape(REACH, qwide, d)
    gk[...] = jnp.zeros_like(gk)
    gv[...] = jnp.zeros_like(gv)

    nq = 2 * qwide
    span = 2 + reach2
    near = near_mask(qwide, wide, cols)
    iq = lax.broadcasted_iota(jnp.int32, (nq, 1), 0) % qwide
    own = ((iq >= own_q) & (iq < own_q + cols)).astype(F32)

    def band(b):
        at = slice(b * nq, (b + 1) * nq)
        keys = slice(b * 2 * wide, b * 2 * wide + span * wide)

        def grads(pbuf, dsbuf):
            p, ds = pbuf[...], dsbuf[...]
            att[2 * b : 2 * b + 2] = gather(dot(p, vhi[keys])).reshape(2, qwide, d)
            gq[2 * b : 2 * b + 2] = gather(dot(ds, khi[keys])).reshape(2, qwide, d)
            eight = slice(2 * b, 2 * b + span)
            gk[eight] += dot(ds, spread(qhi[at]), FIRST).reshape(span, wide, d)
            gv[eight] += dot(p, spread(ghi[at]), FIRST).reshape(span, wide, d)

        return {
            "q_hi": lambda: qhi[at],
            "q_lo": lambda: qlo[at],
            "g_hi": lambda: ghi[at],
            "g_lo": lambda: glo[at],
            "k_hi": lambda: khi[keys],
            "k_lo": lambda: klo[keys],
            "v_hi": lambda: vhi[keys],
            "v_lo": lambda: vlo[keys],
            "mask": lambda: near,
            "own": lambda: own,
            "grads": grads,
        }

    bands = [band(b) for b in range((rows - reach2) // 2)]
    total = run_bands(bands, sbuf, dbuf, pbuf, dsbuf, nq, spread)
    lane = lax.broadcasted_iota(jnp.int32, psum.shape, 1)
    sums = jnp.zeros(psum.shape, F32)
    for h in range(HEADS):
        sums = jnp.where(lane == h, total[h], sums)
    psum[...] = sums


def outer(
    tok_ref,
    go_ref,
    row_a,
    row_b,
    sl_ref,
    wqkv_ref,
    wout_ref,
    khi_in,
    klo_in,
    vhi_in,
    vlo_in,
    kf,
    kr,
    qf,
    qr,
    ga_in,
    gq_in,
    att_in,
    gk_in,
    gv_in,
    psum,
    grads_ref,
    gw_ref,
    tx,
    gx,
    ends,
    qe,
    ge,
    khi,
    klo,
    vhi,
    vlo,
    qhi,
    qlo,
    ghi,
    glo,
    sbuf,
    dbuf,
    pbuf,
    dsbuf,
    gq,
    att,
    gk,
    gv,
):
    rows, cols, d = tok_ref.shape
    _, wide, _ = tx.shape
    _, qwide, _ = gx.shape
    reach2 = 2 * REACH
    q0 = 8 - REACH - 2
    own_q = 8 - q0
    n_rows = rows * lax.axis_size(ROW_AXES)
    row_first = lax.axis_index(ROW_AXES) * rows
    heads, head_sum, spread, gather = tools(d)
    sl = sl_ref[0:1]

    left_k, right_k = 8 - reach2, 8 + cols
    left_q, right_q = own_q - REACH, own_q + cols
    tx[:, 0:8, :] = jnp.zeros((2 * reach2, 8, d), F32)
    tx[:, 8 + cols : wide, :] = jnp.zeros((2 * reach2, wide - 8 - cols, d), F32)
    gx[:, 0:8, :] = jnp.zeros((reach2, 8, d), F32)
    even_row = lax.axis_index("rowlo") % 2 == 0
    even_col = lax.axis_index("col") % 2 == 0
    seg = piece_layout(rows)[0]
    cut = reach2 * cols
    end = cut + REACH * cols
    for even, row_k, row_q in ((~even_row, 0, 0), (even_row, reach2, REACH)):
        ends[...] = jnp.where(even, row_a[...].astype(F32), row_b[...].astype(F32))
        tx[row_k : row_k + reach2, 8 : 8 + cols, :] = ends[0:cut].reshape(reach2, cols, d)
        gx[row_q : row_q + REACH, own_q : own_q + cols, :] = ends[cut:end].reshape(REACH, cols, d)
        first, last = ends[end : end + seg], ends[end + seg : end + 2 * seg]
        ends[end : end + seg] = jnp.where(even_col, last, first)
        ends[end + seg : end + 2 * seg] = jnp.where(even_col, first, last)
        for base, at_k, at_q in ((end, left_k, left_q), (end + seg, right_k, right_q)):
            for r in range(reach2):
                at = base + r * reach2
                tx[row_k + r, at_k : at_k + reach2, :] = ends[at : at + reach2]
            for r in range(REACH):
                at = base + reach2 * reach2 + r * REACH
                gx[row_q + r, at_q : at_q + REACH, :] = ends[at : at + REACH]

    m = reach2 * wide
    x = tx[...].reshape(2 * m, d).astype(BF16)
    kv = dot(x, wqkv_ref[:, d:])
    k, _ = unit(kv[:, :d], head_sum)
    for hi, lo, hi_in, lo_in, fresh in (
        (khi, klo, khi_in, klo_in, k),
        (vhi, vlo, vhi_in, vlo_in, kv[:, d:]),
    ):
        fresh_hi, fresh_lo = split(fresh)
        hi[0:m], lo[0:m] = fresh_hi[0:m], fresh_lo[0:m]
        hi[3 * m :], lo[3 * m :] = fresh_hi[m:], fresh_lo[m:]
        own_end = rows * wide
        for to, source in ((hi, hi_in), (lo, lo_in)):
            to[m : 2 * m] = source[0:m]
            to[2 * m : 3 * m] = source[own_end - m : own_end]
    x = tx[REACH : 3 * REACH, q0 : q0 + qwide, :].reshape(reach2 * qwide, d).astype(BF16)
    q, _ = unit(dot(x, wqkv_ref[:, :d]), head_sum)
    q = q.reshape(reach2, qwide, d)
    g = dot(gx[...].reshape(reach2 * qwide, d).astype(BF16), wout_ref[...], LAST)
    g = g.reshape(reach2, qwide, d)
    qe[0:REACH], qe[3 * REACH :] = q[0:REACH], q[REACH:]
    ge[0:REACH], ge[3 * REACH :] = g[0:REACH], g[REACH:]
    qe[REACH:reach2], qe[reach2 : 3 * REACH] = qf[0:REACH], qf[rows - REACH :]
    ge[REACH : 3 * REACH] = ga_in[...]
    flat = 2 * reach2 * qwide
    qhi[...], qlo[...] = split(qe[...].reshape(flat, d) * (sl * LOG2E))
    ghi[...], glo[...] = split(ge[...].reshape(flat, d))
    gk[...] = gk_in[...]
    gv[...] = gv_in[...]

    nq = 2 * qwide
    span = 2 + reach2
    nk = span * wide
    near = near_mask(qwide, wide, cols)
    jr = lax.broadcasted_iota(jnp.int32, (1, nk), 1) // wide
    iq = lax.broadcasted_iota(jnp.int32, (nq, 1), 0)
    own_col = (iq % qwide >= own_q) & (iq % qwide < own_q + cols)

    def band(b):
        top = b < REACH
        first = 2 * b if top else rows + 2 * (b - REACH)
        at = slice(b * nq, (b + 1) * nq)
        key_at = 2 * b if top else 2 * reach2 + 2 * (b - REACH)
        keys = slice(key_at * wide, key_at * wide + nk)
        mine = first + 1 >= REACH and first < rows + REACH
        skip = reach2 - first if top else 0
        count = span - skip if top else reach2 - 2 * (b - REACH)
        to = 0 if top else rows - count
        part = slice(skip * wide, (skip + count) * wide)

        def mask():
            key_row = jr + (row_first - reach2 + first)
            return near * ((key_row >= 0) & (key_row < n_rows)).astype(F32)

        def own():
            if not mine:
                return None
            q_row = iq // qwide + first
            return (own_col & (q_row >= REACH) & (q_row < REACH + rows)).astype(F32)

        def grads(pbuf, dsbuf):
            if mine:
                att[2 * b : 2 * b + 2] = gather(dot(pbuf[...], vhi[keys])).reshape(2, qwide, d)
                gq[2 * b : 2 * b + 2] = gather(dot(dsbuf[...], khi[keys])).reshape(2, qwide, d)
            p, ds = pbuf[:, part], dsbuf[:, part]
            own_rows = slice(to, to + count)
            gk[own_rows] += dot(ds, spread(qhi[at]), FIRST).reshape(count, wide, d)
            gv[own_rows] += dot(p, spread(ghi[at]), FIRST).reshape(count, wide, d)

        return {
            "q_hi": lambda: qhi[at],
            "q_lo": lambda: qlo[at],
            "g_hi": lambda: ghi[at],
            "g_lo": lambda: glo[at],
            "k_hi": lambda: khi[keys],
            "k_lo": lambda: klo[keys],
            "v_hi": lambda: vhi[keys],
            "v_lo": lambda: vlo[keys],
            "mask": mask,
            "own": own,
            "grads": grads,
        }

    total = run_bands([band(b) for b in range(reach2)], sbuf, dbuf, pbuf, dsbuf, nq, spread)

    n = rows * cols
    key_cols = slice(8, 8 + cols)
    query_cols = slice(own_q, own_q + cols)

    def own_queries(edge, middle):
        parts = [
            edge[REACH:reach2, query_cols, :],
            middle[:, query_cols, :],
            edge[reach2 : 3 * REACH, query_cols, :],
        ]
        return jnp.concatenate(parts, axis=0).reshape(n, d)

    def unit_back(u, r, g):
        return r * (g - u * head_sum(u * g))

    g_q = unit_back(
        qf[:, query_cols, :].reshape(n, d),
        qr[:, query_cols, :].reshape(n, d),
        own_queries(gq, gq_in) * sl,
    )
    g_k = unit_back(
        kf[:, key_cols, :].reshape(n, d),
        kr[:, key_cols, :].reshape(n, d),
        gk[:, key_cols, :].reshape(n, d) * (1.0 / LOG2E),
    )
    g_v = gv[:, key_cols, :].reshape(n, d)
    grads = jnp.concatenate([g_q.astype(BF16), g_k.astype(BF16), g_v.astype(BF16)], axis=1)
    grads_ref[...] = grads
    wq = dot(tok_ref[...].reshape(n, d), grads, FIRST)
    wo = dot(own_queries(att, att_in).astype(BF16), go_ref[...].reshape(n, d), FIRST)
    half = d // 2
    lane = lax.broadcasted_iota(jnp.int32, (8, 4 * d), 1)
    sums = jnp.zeros((8, 4 * d), F32)
    for h in range(HEADS):
        at = h * (d // HEADS)
        t = (total[h] + psum[0:1, h : h + 1]) / (sl[:, at : at + 1] * LOG2E)
        sums = jnp.where(lane == h, t, sums)
    for c in range(2):
        gw_ref[c, 0:half, 0 : 3 * d] = wq[c * half : (c + 1) * half]
        gw_ref[c, 0:half, 3 * d :] = wo[c * half : (c + 1) * half]
        gw_ref[c, half:, :] = sums


def sizes(rows, cols):
    wide = -(-(cols + 4 * REACH + 2) // 16) * 16
    qwide = -(-(cols + 2 * REACH + 2) // 8) * 8
    return wide, qwide


def call(body, out_shape, in_specs, scratch, flops):
    vmem = pl.BlockSpec(memory_space=pltpu.VMEM)
    return pl.pallas_call(
        body,
        out_shape=out_shape,
        in_specs=in_specs,
        out_specs=(vmem,) * len(out_shape),
        scratch_shapes=scratch,
        compiler_params=pltpu.CompilerParams(vmem_limit_bytes=24 * 1024 * 1024),
        cost_estimate=pl.CostEstimate(
            flops=flops, bytes_accessed=4_000_000, transcendentals=300_000
        ),
    )


def inner_grads(scale, tokens, grad_out, col_a, col_b, w_qkv, w_out):
    rows, cols, d = tokens.shape
    wide, qwide = sizes(rows, cols)
    f32 = lambda *s: jax.ShapeDtypeStruct(s, F32)
    bf16 = lambda *s: jax.ShapeDtypeStruct(s, BF16)
    middle = rows - 2 * REACH
    nk = (2 + 2 * REACH) * wide
    key, grid, qgrid = bf16(rows * wide, d), f32(rows, wide, d), f32(rows, qwide, d)
    mid = f32(middle, qwide, d)
    out_shape = (
        (f32(8, d), bf16(*w_qkv.shape), bf16(*w_out.shape))
        + (key,) * 4
        + (grid, grid, qgrid, qgrid, f32(2 * REACH, qwide, d), mid, mid, grid, grid, f32(8, 128))
    )
    vmem = pl.BlockSpec(memory_space=pltpu.VMEM)
    hbm = pl.BlockSpec(memory_space=pltpu.HBM)
    tile = lambda dt: pltpu.VMEM((HEADS * 2 * qwide, nk), dt)
    scratch = [
        pltpu.SMEM((HEADS,), F32),
        pltpu.SemaphoreType.DMA((3,)),
        pltpu.VMEM((rows, wide, d), F32),
        pltpu.VMEM((rows, qwide, d), F32),
        pltpu.VMEM(col_a.shape, F32),
    ]
    scratch += [pltpu.VMEM((middle * qwide, d), BF16)] * 4
    scratch += [tile(F32), tile(F32), tile(BF16), tile(BF16)]
    return call(inner, out_shape, [hbm] + [vmem] * 4 + [hbm] * 2, scratch, 3_000_000_000)(
        pin(scale), tokens, grad_out, col_a, col_b, pin(w_qkv), pin(w_out)
    )


def outer_grads(tokens, grad_out, row_a, row_b, state):
    rows, cols, d = tokens.shape
    wide, qwide = sizes(rows, cols)
    nk = (2 + 2 * REACH) * wide
    out_shape = (
        jax.ShapeDtypeStruct((rows * cols, 3 * d), BF16),
        jax.ShapeDtypeStruct((2, d // 2 + 8, 4 * d), F32),
    )
    edge = pltpu.VMEM((4 * REACH, qwide, d), F32)
    tile = lambda dt: pltpu.VMEM((HEADS * 2 * qwide, nk), dt)
    scratch = [
        pltpu.VMEM((4 * REACH, wide, d), F32),
        pltpu.VMEM((2 * REACH, qwide, d), F32),
        pltpu.VMEM(row_a.shape, F32),
        edge,
        edge,
    ]
    scratch += [pltpu.VMEM((8 * REACH * wide, d), BF16)] * 4
    scratch += [pltpu.VMEM((4 * REACH * qwide, d), BF16)] * 4
    scratch += [tile(F32), tile(F32), tile(BF16), tile(BF16), edge, edge]
    scratch += [pltpu.VMEM((rows, wide, d), F32)] * 2
    vmem = pl.BlockSpec(memory_space=pltpu.VMEM)
    args = (tokens, grad_out, row_a, row_b) + tuple(state)
    return call(outer, out_shape, [vmem] * len(args), scratch, 3_000_000_000)(*args)


def finish(mine_ref, other_ref, wqkv_ref, wout_ref):
    half = mine_ref.shape[0]
    width = wqkv_ref.shape[1]
    first = lax.axis_index("rowlo") == 0
    mine, other = mine_ref[...].astype(F32), other_ref[...].astype(F32)
    upper = jnp.where(first, mine, other)
    lower = jnp.where(first, other, mine)
    wqkv_ref[0:half] = upper[:, :width]
    wout_ref[0:half] = upper[:, width:]
    wqkv_ref[half:] = lower[:, :width]
    wout_ref[half:] = lower[:, width:]


def finished(mine, other):
    half, width = mine.shape
    d = 2 * half
    vmem = pl.BlockSpec(memory_space=pltpu.VMEM)
    return pl.pallas_call(
        finish,
        out_shape=(
            jax.ShapeDtypeStruct((d, width - d), F32),
            jax.ShapeDtypeStruct((d, d), F32),
        ),
        in_specs=[vmem] * 2,
        out_specs=(vmem, vmem),
        compiler_params=pltpu.CompilerParams(vmem_limit_bytes=8 * 1024 * 1024),
        cost_estimate=pl.CostEstimate(flops=0, bytes_accessed=2_000_000, transcendentals=0),
    )(mine, other)


def swap_pairs(x, axis, first):
    pairs = []
    for i in range(first, lax.axis_size(axis) - 1, 2):
        pairs += [(i, i + 1), (i + 1, i)]
    return lax.ppermute(x, axis, pairs)


def shards(tokens, grad_out, w_qkv, w_out, scale):
    rows, cols, d = tokens.shape
    tokens, grad_out, col_a, col_b, row_a, row_b = packed(tokens, grad_out)
    col_b = swap_pairs(col_b, "col", 1)
    col_a = swap_pairs(col_a, "col", 0)
    seg, last, _, _, _ = piece_layout(rows)
    odd = lax.axis_index("rowlo") % 2

    def with_corners(row, at):
        return jnp.concatenate(
            [row] + [lax.dynamic_slice_in_dim(c, at, seg, 0) for c in (col_a, col_b)], axis=0
        )

    row_b = swap_pairs(with_corners(row_b, odd * last), ROW_AXES, 1)
    row_a = swap_pairs(with_corners(row_a, (1 - odd) * last), ROW_AXES, 0)

    state = inner_grads(scale, tokens, grad_out, col_a, col_b, w_qkv, w_out)
    grads, partial = outer_grads(tokens, grad_out, row_a, row_b, state)
    grad_tokens = dot(grads, w_qkv, LAST).astype(BF16).reshape(rows, cols, d)

    lo = lax.axis_index("rowlo")
    swap = [(0, 1), (1, 0)]
    kept = lax.dynamic_index_in_dim(partial, lo, 0, keepdims=False)
    sent = lax.dynamic_index_in_dim(partial, 1 - lo, 0, keepdims=False)
    kept = kept + lax.ppermute(sent, "rowlo", swap)
    half = d // 2
    n = lax.axis_size(SPREAD_AXES)
    pieces = half // n if half % n == 0 else 1
    part = kept[:half].reshape(n, pieces, -1)
    sums = kept[half, :HEADS]
    sums_hi = lax.reduce_precision(sums, 8, 7)
    sums = jnp.concatenate([sums_hi, sums - sums_hi, jnp.zeros((128 - 2 * HEADS,), F32)])
    part = jnp.concatenate(
        [part.astype(BF16), jnp.broadcast_to(sums.astype(BF16), (n, pieces, 128))], axis=2
    )
    part = lax.all_to_all(part, SPREAD_AXES, 0, 0, tiled=True).astype(F32)
    part = jnp.sum(part, axis=0)
    sums = part[0, -128:]
    grad_scale = sums[:HEADS] + sums[HEADS : 2 * HEADS]
    part = part[:, :-128].astype(BF16)
    mine = lax.all_to_all(
        jnp.broadcast_to(part[None], (n,) + part.shape), SPREAD_AXES, 0, 0, tiled=True
    ).reshape(half, 4 * d)
    other = lax.ppermute(mine, "rowlo", swap)
    grad_wqkv, grad_wout = finished(mine, other)
    return grad_tokens, grad_wqkv, grad_wout, grad_scale


def solution(mesh):
    n_row, n_col = mesh.devices.shape
    fine = Mesh(mesh.devices.reshape(n_row // 2, 2, n_col), ("rowhi", "rowlo", "col"))
    block = P(ROW_AXES, "col", None)
    return jax.shard_map(
        shards,
        mesh=fine,
        in_specs=(block, block, P(), P(), P()),
        out_specs=(block, P(), P(), P()),
        check_vma=False,
    )
```

```python
import math

import jax
import jax.numpy as jnp
from jax import lax
from jax.experimental import pallas as pl
from jax.experimental.pallas import tpu as pltpu
from jax.sharding import Mesh
from jax.sharding import PartitionSpec as P

HEADS = 4
REACH = 3
F32 = jnp.float32
BF16 = jnp.bfloat16
LAST = (((1,), (1,)), ((), ()))
FIRST = (((0,), (0,)), ((), ()))
LOG2E = math.log2(math.e)
ROW_AXES = ("rowhi", "rowlo")
SPREAD_AXES = ("rowhi", "col")


def dot(a, b, dims=(((1,), (0,)), ((), ()))):
    return lax.dot_general(a, b, dims, preferred_element_type=F32)


def split(x):
    hi = x.astype(BF16)
    return hi, (x - hi.astype(F32)).astype(BF16)


def pin(x):
    return pltpu.with_memory_space_constraint(x, pltpu.HBM)


def piece_layout(rows):
    wide = 2 * REACH
    seg = -(-(wide * wide + REACH * REACH) // 16) * 16
    mid_tok = (rows - 2 * wide) * wide
    mid = -(-(mid_tok + (rows - 2 * REACH) * REACH) // 16) * 16
    tok, go = [], []
    for r in range(rows):
        if r < wide:
            tok.append(r * wide)
        elif r < rows - wide:
            tok.append(seg + (r - wide) * wide)
        else:
            tok.append(seg + mid + (r - rows + wide) * wide)
        if r < REACH:
            go.append(wide * wide + r * REACH)
        elif r < rows - REACH:
            go.append(seg + mid_tok + (r - REACH) * REACH)
        else:
            go.append(seg + mid + wide * wide + (r - rows + REACH) * REACH)
    return seg, seg + mid, 2 * seg + mid, tok, go


def pack(tok_hbm, go_hbm, tok_ref, go_ref, col_a, col_b, row_a, row_b, tf, gf, first, last, sems):
    rows, cols, d = tok_ref.shape
    copies = [
        pltpu.make_async_copy(tok_hbm, tok_ref, sems.at[0]),
        pltpu.make_async_copy(go_hbm, go_ref, sems.at[1]),
    ]
    for c in copies:
        c.start()
    wide = 2 * REACH
    _, _, _, tok_at, go_at = piece_layout(rows)
    even_row = lax.axis_index("rowlo") % 2 == 0
    even_col = lax.axis_index("col") % 2 == 0
    first[...] = jnp.zeros_like(first)
    last[...] = jnp.zeros_like(last)
    for c in copies:
        c.wait()
    tf[...] = tok_ref[...].astype(F32)
    gf[...] = go_ref[...].astype(F32)
    for r in range(rows):
        first[tok_at[r] : tok_at[r] + wide] = tf[r, 0:wide, :]
        last[tok_at[r] : tok_at[r] + wide] = tf[r, cols - wide : cols, :]
        first[go_at[r] : go_at[r] + REACH] = gf[r, 0:REACH, :]
        last[go_at[r] : go_at[r] + REACH] = gf[r, cols - REACH : cols, :]
    lo, hi = first[...], last[...]
    col_a[...] = jnp.where(even_col, hi, lo).astype(BF16)
    col_b[...] = jnp.where(even_col, lo, hi).astype(BF16)
    cut = wide * cols
    end = cut + REACH * cols
    lo = tf[0:wide].reshape(cut, d)
    hi = tf[rows - wide : rows].reshape(cut, d)
    row_a[0:cut] = jnp.where(even_row, hi, lo).astype(BF16)
    row_b[0:cut] = jnp.where(even_row, lo, hi).astype(BF16)
    lo = gf[0:REACH].reshape(end - cut, d)
    hi = gf[rows - REACH : rows].reshape(end - cut, d)
    row_a[cut:end] = jnp.where(even_row, hi, lo).astype(BF16)
    row_b[cut:end] = jnp.where(even_row, lo, hi).astype(BF16)


def packed(tokens, grad_out):
    rows, cols, d = tokens.shape
    size = piece_layout(rows)[2]
    vmem = pl.BlockSpec(memory_space=pltpu.VMEM)
    col = jax.ShapeDtypeStruct((size, d), BF16)
    row = jax.ShapeDtypeStruct((3 * REACH * cols, d), BF16)
    whole = jax.ShapeDtypeStruct((rows, cols, d), BF16)
    block = pltpu.VMEM((rows, cols, d), F32)
    return pl.pallas_call(
        pack,
        out_shape=(whole, whole, col, col, row, row),
        in_specs=[pl.BlockSpec(memory_space=pltpu.HBM)] * 2,
        out_specs=(vmem,) * 6,
        scratch_shapes=[
            block,
            block,
            pltpu.VMEM((size, d), F32),
            pltpu.VMEM((size, d), F32),
            pltpu.SemaphoreType.DMA((2,)),
        ],
        compiler_params=pltpu.CompilerParams(vmem_limit_bytes=8 * 1024 * 1024),
        cost_estimate=pl.CostEstimate(flops=0, bytes_accessed=1_000_000, transcendentals=0),
    )(pin(tokens), pin(grad_out))


def unit(x, head_sum):
    r = lax.rsqrt(head_sum(x * x) + 1e-06)
    return x * r, r


def tools(d):
    per = d // HEADS
    lane_head = lax.broadcasted_iota(jnp.int32, (1, d), 1) // per
    heads = [lane_head == h for h in range(HEADS)]
    ones = (
        lax.broadcasted_iota(jnp.int32, (d, d), 0) // per
        == lax.broadcasted_iota(jnp.int32, (d, d), 1) // per
    ).astype(BF16)

    def head_sum(x):
        hi, lo = split(x)
        return dot(hi, ones) + dot(lo, ones)

    def spread(x):
        zero = jnp.zeros_like(x)
        return jnp.concatenate([jnp.where(m, x, zero) for m in heads], axis=0)

    def gather(x):
        n = x.shape[0] // HEADS
        out = x[0:n]
        for h in range(1, HEADS):
            out = jnp.where(heads[h], x[h * n : (h + 1) * n], out)
        return out

    return heads, head_sum, spread, gather


def has_neighbours(axis):
    at = lax.axis_index(axis)
    return at > 0, at < lax.axis_size(axis) - 1


def near_mask(qwide, wide, cols):
    nq, nk = 2 * qwide, (2 + 2 * REACH) * wide
    i = lax.broadcasted_iota(jnp.int32, (nq, nk), 0)
    j = lax.broadcasted_iota(jnp.int32, (nq, nk), 1)
    dr = j // wide - i // qwide
    dc = j % wide - i % qwide
    key_col = j % wide + (lax.axis_index("col") * cols - 8)
    near = (dr >= 0) & (dr <= 2 * REACH) & (dc >= 0) & (dc <= 2 * REACH)
    near = near & (key_col >= 0) & (key_col < cols * lax.axis_size("col"))
    return near.astype(F32)


def run_bands(bands, sbuf, dbuf, pbuf, dsbuf, nq, spread):
    def scores(band):
        q_hi, q_lo = spread(band["q_hi"]()), spread(band["q_lo"]())
        k_hi = band["k_hi"]()
        sbuf[...] = dot(q_hi, k_hi, LAST) + dot(q_lo, k_hi, LAST) + dot(q_hi, band["k_lo"](), LAST)
        g_hi, g_lo = spread(band["g_hi"]()), spread(band["g_lo"]())
        v_hi = band["v_hi"]()
        dbuf[...] = dot(g_hi, v_hi, LAST) + dot(g_lo, v_hi, LAST) + dot(g_hi, band["v_lo"](), LAST)

    def softmax(band, total):
        mask, own = band["mask"](), band["own"]()
        out = []
        for h in range(HEADS):
            at = slice(h * nq, (h + 1) * nq)
            s, dp = sbuf[at], dbuf[at]
            e = jnp.exp2(s) * mask
            r = 1.0 / (jnp.sum(e, axis=1, keepdims=True) + 1e-30)
            p = e * r
            ds = p * (dp - jnp.sum(p * dp, axis=1, keepdims=True))
            if own is None:
                out.append(total[h])
            else:
                out.append(total[h] + own * jnp.sum(ds * s, axis=1, keepdims=True))
            pbuf[at] = p.astype(BF16)
            dsbuf[at] = ds.astype(BF16)
        return out

    total = [jnp.zeros((nq, 1), F32) for _ in range(HEADS)]
    count = len(bands)
    scores(bands[0])
    for b in range(count + 1):
        if b > 0:
            bands[b - 1]["grads"](pbuf, dsbuf)
        if b < count:
            total = softmax(bands[b], total)
        if b + 1 < count:
            scores(bands[b + 1])
    return [jnp.sum(t, axis=0, keepdims=True) for t in total]


def inner(
    scale_hbm,
    tok_ref,
    go_ref,
    col_a,
    col_b,
    wqkv_hbm,
    wout_hbm,
    sl_ref,
    wqkv_ref,
    wout_ref,
    khi,
    klo,
    vhi,
    vlo,
    kf,
    kr,
    qf,
    qr,
    ga_ref,
    gq,
    att,
    gk,
    gv,
    psum,
    scale_ref,
    sems,
    tx,
    gx,
    side,
    qhi,
    qlo,
    ghi,
    glo,
    sbuf,
    dbuf,
    pbuf,
    dsbuf,
):
    copies = [
        pltpu.make_async_copy(scale_hbm, scale_ref, sems.at[0]),
        pltpu.make_async_copy(wqkv_hbm, wqkv_ref, sems.at[1]),
        pltpu.make_async_copy(wout_hbm, wout_ref, sems.at[2]),
    ]
    for c in copies:
        c.start()
    rows, cols, d = tok_ref.shape
    _, wide, _ = tx.shape
    _, qwide, _ = gx.shape
    reach2 = 2 * REACH
    q0 = 8 - REACH - 2
    own_q = 8 - q0
    heads, head_sum, spread, gather = tools(d)

    tx[:, 0:8, :] = jnp.zeros((rows, 8, d), F32)
    tx[:, 8 + cols : wide, :] = jnp.zeros((rows, wide - 8 - cols, d), F32)
    gx[:, 0:8, :] = jnp.zeros((rows, 8, d), F32)
    tx[:, 8 : 8 + cols, :] = tok_ref[...].astype(F32)
    gx[:, own_q : own_q + cols, :] = go_ref[...].astype(F32)
    even_col = lax.axis_index("col") % 2 == 0
    _, _, _, tok_at, go_at = piece_layout(rows)
    has_left, has_right = has_neighbours("col")
    for even, valid, at_k, at_q in (
        (~even_col, has_left, 8 - reach2, own_q - REACH),
        (even_col, has_right, 8 + cols, own_q + cols),
    ):
        x = jnp.where(even, col_a[...].astype(F32), col_b[...].astype(F32))
        side[...] = jnp.where(valid, x, jnp.zeros_like(x))
        for r in range(rows):
            tx[r, at_k : at_k + reach2, :] = side[tok_at[r] : tok_at[r] + reach2]
            gx[r, at_q : at_q + REACH, :] = side[go_at[r] : go_at[r] + REACH]

    for c in copies:
        c.wait()
    sl = jnp.zeros((1, d), F32)
    for h in range(HEADS):
        sl = jnp.where(heads[h], scale_ref[h], sl)
    sl_ref[...] = jnp.broadcast_to(sl, sl_ref.shape)

    step = rows // 2
    for c in range(0, rows, step):
        at = slice(c, c + step)
        x = tx[at].reshape(step * wide, d).astype(BF16)
        kv = dot(x, wqkv_ref[:, d:])
        k, rk = unit(kv[:, :d], head_sum)
        kf[at] = k.reshape(step, wide, d)
        kr[at] = rk.reshape(step, wide, d)
        flat = slice(c * wide, (c + step) * wide)
        khi[flat], klo[flat] = split(k)
        vhi[flat], vlo[flat] = split(kv[:, d:])
    x = tx[:, q0 : q0 + qwide, :].reshape(rows * qwide, d).astype(BF16)
    q, rq = unit(dot(x, wqkv_ref[:, :d]), head_sum)
    qf[...] = q.reshape(rows, qwide, d)
    qr[...] = rq.reshape(rows, qwide, d)
    g = dot(gx[...].reshape(rows * qwide, d).astype(BF16), wout_ref[...], LAST)
    lo, hi = REACH * qwide, (rows - REACH) * qwide
    qhi[...], qlo[...] = split(q[lo:hi] * (sl * LOG2E))
    ghi[...], glo[...] = split(g[lo:hi])
    ga_ref[0:REACH] = g[0:lo].reshape(REACH, qwide, d)
    ga_ref[REACH:] = g[hi:].reshape(REACH, qwide, d)
    gk[...] = jnp.zeros_like(gk)
    gv[...] = jnp.zeros_like(gv)

    nq = 2 * qwide
    span = 2 + reach2
    near = near_mask(qwide, wide, cols)
    iq = lax.broadcasted_iota(jnp.int32, (nq, 1), 0) % qwide
    own = ((iq >= own_q) & (iq < own_q + cols)).astype(F32)

    def band(b):
        at = slice(b * nq, (b + 1) * nq)
        keys = slice(b * 2 * wide, b * 2 * wide + span * wide)

        def grads(pbuf, dsbuf):
            p, ds = pbuf[...], dsbuf[...]
            att[2 * b : 2 * b + 2] = gather(dot(p, vhi[keys])).reshape(2, qwide, d)
            gq[2 * b : 2 * b + 2] = gather(dot(ds, khi[keys])).reshape(2, qwide, d)
            eight = slice(2 * b, 2 * b + span)
            gk[eight] += dot(ds, spread(qhi[at]), FIRST).reshape(span, wide, d)
            gv[eight] += dot(p, spread(ghi[at]), FIRST).reshape(span, wide, d)

        return {
            "q_hi": lambda: qhi[at],
            "q_lo": lambda: qlo[at],
            "g_hi": lambda: ghi[at],
            "g_lo": lambda: glo[at],
            "k_hi": lambda: khi[keys],
            "k_lo": lambda: klo[keys],
            "v_hi": lambda: vhi[keys],
            "v_lo": lambda: vlo[keys],
            "mask": lambda: near,
            "own": lambda: own,
            "grads": grads,
        }

    bands = [band(b) for b in range((rows - reach2) // 2)]
    total = run_bands(bands, sbuf, dbuf, pbuf, dsbuf, nq, spread)
    lane = lax.broadcasted_iota(jnp.int32, psum.shape, 1)
    sums = jnp.zeros(psum.shape, F32)
    for h in range(HEADS):
        sums = jnp.where(lane == h, total[h], sums)
    psum[...] = sums


def outer(
    tok_ref,
    go_ref,
    row_a,
    row_b,
    sl_ref,
    wqkv_ref,
    wout_ref,
    khi_in,
    klo_in,
    vhi_in,
    vlo_in,
    kf,
    kr,
    qf,
    qr,
    ga_in,
    gq_in,
    att_in,
    gk_in,
    gv_in,
    psum,
    grads_ref,
    gw_ref,
    tx,
    gx,
    ends,
    qe,
    ge,
    khi,
    klo,
    vhi,
    vlo,
    qhi,
    qlo,
    ghi,
    glo,
    sbuf,
    dbuf,
    pbuf,
    dsbuf,
    gq,
    att,
    gk,
    gv,
):
    rows, cols, d = tok_ref.shape
    _, wide, _ = tx.shape
    _, qwide, _ = gx.shape
    reach2 = 2 * REACH
    q0 = 8 - REACH - 2
    own_q = 8 - q0
    n_rows = rows * lax.axis_size(ROW_AXES)
    row_first = lax.axis_index(ROW_AXES) * rows
    heads, head_sum, spread, gather = tools(d)
    sl = sl_ref[0:1]

    left_k, right_k = 8 - reach2, 8 + cols
    left_q, right_q = own_q - REACH, own_q + cols
    tx[:, 0:8, :] = jnp.zeros((2 * reach2, 8, d), F32)
    tx[:, 8 + cols : wide, :] = jnp.zeros((2 * reach2, wide - 8 - cols, d), F32)
    gx[:, 0:8, :] = jnp.zeros((reach2, 8, d), F32)
    even_row = lax.axis_index("rowlo") % 2 == 0
    even_col = lax.axis_index("col") % 2 == 0
    seg = piece_layout(rows)[0]
    cut = reach2 * cols
    end = cut + REACH * cols
    has_above, has_below = has_neighbours(ROW_AXES)
    has_left, has_right = has_neighbours("col")
    for even, valid, row_k, row_q in (
        (~even_row, has_above, 0, 0),
        (even_row, has_below, reach2, REACH),
    ):
        x = jnp.where(even, row_a[...].astype(F32), row_b[...].astype(F32))
        ends[...] = jnp.where(valid, x, jnp.zeros_like(x))
        tx[row_k : row_k + reach2, 8 : 8 + cols, :] = ends[0:cut].reshape(reach2, cols, d)
        gx[row_q : row_q + REACH, own_q : own_q + cols, :] = ends[cut:end].reshape(REACH, cols, d)
        first, last = ends[end : end + seg], ends[end + seg : end + 2 * seg]
        none = jnp.zeros_like(first)
        ends[end : end + seg] = jnp.where(has_left, jnp.where(even_col, last, first), none)
        ends[end + seg : end + 2 * seg] = jnp.where(has_right, jnp.where(even_col, first, last), none)
        for base, at_k, at_q in ((end, left_k, left_q), (end + seg, right_k, right_q)):
            for r in range(reach2):
                at = base + r * reach2
                tx[row_k + r, at_k : at_k + reach2, :] = ends[at : at + reach2]
            for r in range(REACH):
                at = base + reach2 * reach2 + r * REACH
                gx[row_q + r, at_q : at_q + REACH, :] = ends[at : at + REACH]

    m = reach2 * wide
    x = tx[...].reshape(2 * m, d).astype(BF16)
    kv = dot(x, wqkv_ref[:, d:])
    k, _ = unit(kv[:, :d], head_sum)
    for hi, lo, hi_in, lo_in, fresh in (
        (khi, klo, khi_in, klo_in, k),
        (vhi, vlo, vhi_in, vlo_in, kv[:, d:]),
    ):
        fresh_hi, fresh_lo = split(fresh)
        hi[0:m], lo[0:m] = fresh_hi[0:m], fresh_lo[0:m]
        hi[3 * m :], lo[3 * m :] = fresh_hi[m:], fresh_lo[m:]
        own_end = rows * wide
        for to, source in ((hi, hi_in), (lo, lo_in)):
            to[m : 2 * m] = source[0:m]
            to[2 * m : 3 * m] = source[own_end - m : own_end]
    x = tx[REACH : 3 * REACH, q0 : q0 + qwide, :].reshape(reach2 * qwide, d).astype(BF16)
    q, _ = unit(dot(x, wqkv_ref[:, :d]), head_sum)
    q = q.reshape(reach2, qwide, d)
    g = dot(gx[...].reshape(reach2 * qwide, d).astype(BF16), wout_ref[...], LAST)
    g = g.reshape(reach2, qwide, d)
    qe[0:REACH], qe[3 * REACH :] = q[0:REACH], q[REACH:]
    ge[0:REACH], ge[3 * REACH :] = g[0:REACH], g[REACH:]
    qe[REACH:reach2], qe[reach2 : 3 * REACH] = qf[0:REACH], qf[rows - REACH :]
    ge[REACH : 3 * REACH] = ga_in[...]
    flat = 2 * reach2 * qwide
    qhi[...], qlo[...] = split(qe[...].reshape(flat, d) * (sl * LOG2E))
    ghi[...], glo[...] = split(ge[...].reshape(flat, d))
    gk[...] = gk_in[...]
    gv[...] = gv_in[...]

    nq = 2 * qwide
    span = 2 + reach2
    nk = span * wide
    near = near_mask(qwide, wide, cols)
    jr = lax.broadcasted_iota(jnp.int32, (1, nk), 1) // wide
    iq = lax.broadcasted_iota(jnp.int32, (nq, 1), 0)
    own_col = (iq % qwide >= own_q) & (iq % qwide < own_q + cols)

    def band(b):
        top = b < REACH
        first = 2 * b if top else rows + 2 * (b - REACH)
        at = slice(b * nq, (b + 1) * nq)
        key_at = 2 * b if top else 2 * reach2 + 2 * (b - REACH)
        keys = slice(key_at * wide, key_at * wide + nk)
        mine = first + 1 >= REACH and first < rows + REACH
        skip = reach2 - first if top else 0
        count = span - skip if top else reach2 - 2 * (b - REACH)
        to = 0 if top else rows - count
        part = slice(skip * wide, (skip + count) * wide)

        def mask():
            key_row = jr + (row_first - reach2 + first)
            return near * ((key_row >= 0) & (key_row < n_rows)).astype(F32)

        def own():
            if not mine:
                return None
            q_row = iq // qwide + first
            return (own_col & (q_row >= REACH) & (q_row < REACH + rows)).astype(F32)

        def grads(pbuf, dsbuf):
            if mine:
                att[2 * b : 2 * b + 2] = gather(dot(pbuf[...], vhi[keys])).reshape(2, qwide, d)
                gq[2 * b : 2 * b + 2] = gather(dot(dsbuf[...], khi[keys])).reshape(2, qwide, d)
            p, ds = pbuf[:, part], dsbuf[:, part]
            own_rows = slice(to, to + count)
            gk[own_rows] += dot(ds, spread(qhi[at]), FIRST).reshape(count, wide, d)
            gv[own_rows] += dot(p, spread(ghi[at]), FIRST).reshape(count, wide, d)

        return {
            "q_hi": lambda: qhi[at],
            "q_lo": lambda: qlo[at],
            "g_hi": lambda: ghi[at],
            "g_lo": lambda: glo[at],
            "k_hi": lambda: khi[keys],
            "k_lo": lambda: klo[keys],
            "v_hi": lambda: vhi[keys],
            "v_lo": lambda: vlo[keys],
            "mask": mask,
            "own": own,
            "grads": grads,
        }

    total = run_bands([band(b) for b in range(reach2)], sbuf, dbuf, pbuf, dsbuf, nq, spread)

    n = rows * cols
    key_cols = slice(8, 8 + cols)
    query_cols = slice(own_q, own_q + cols)

    def own_queries(edge, middle):
        parts = [
            edge[REACH:reach2, query_cols, :],
            middle[:, query_cols, :],
            edge[reach2 : 3 * REACH, query_cols, :],
        ]
        return jnp.concatenate(parts, axis=0).reshape(n, d)

    def unit_back(u, r, g):
        return r * (g - u * head_sum(u * g))

    g_q = unit_back(
        qf[:, query_cols, :].reshape(n, d),
        qr[:, query_cols, :].reshape(n, d),
        own_queries(gq, gq_in) * sl,
    )
    g_k = unit_back(
        kf[:, key_cols, :].reshape(n, d),
        kr[:, key_cols, :].reshape(n, d),
        gk[:, key_cols, :].reshape(n, d) * (1.0 / LOG2E),
    )
    g_v = gv[:, key_cols, :].reshape(n, d)
    grads = jnp.concatenate([g_q.astype(BF16), g_k.astype(BF16), g_v.astype(BF16)], axis=1)
    grads_ref[...] = grads
    wq = dot(tok_ref[...].reshape(n, d), grads, FIRST)
    wo = dot(own_queries(att, att_in).astype(BF16), go_ref[...].reshape(n, d), FIRST)
    half = d // 2
    lane = lax.broadcasted_iota(jnp.int32, (8, 4 * d), 1)
    sums = jnp.zeros((8, 4 * d), F32)
    for h in range(HEADS):
        at = h * (d // HEADS)
        t = (total[h] + psum[0:1, h : h + 1]) / (sl[:, at : at + 1] * LOG2E)
        sums = jnp.where(lane == h, t, sums)
    for c in range(2):
        gw_ref[c, 0:half, 0 : 3 * d] = wq[c * half : (c + 1) * half]
        gw_ref[c, 0:half, 3 * d :] = wo[c * half : (c + 1) * half]
        gw_ref[c, half:, :] = sums


def sizes(rows, cols):
    wide = -(-(cols + 4 * REACH + 2) // 16) * 16
    qwide = -(-(cols + 2 * REACH + 2) // 8) * 8
    return wide, qwide


def call(body, out_shape, in_specs, scratch, flops):
    vmem = pl.BlockSpec(memory_space=pltpu.VMEM)
    return pl.pallas_call(
        body,
        out_shape=out_shape,
        in_specs=in_specs,
        out_specs=(vmem,) * len(out_shape),
        scratch_shapes=scratch,
        compiler_params=pltpu.CompilerParams(vmem_limit_bytes=24 * 1024 * 1024),
        cost_estimate=pl.CostEstimate(
            flops=flops, bytes_accessed=4_000_000, transcendentals=300_000
        ),
    )


def inner_grads(scale, tokens, grad_out, col_a, col_b, w_qkv, w_out):
    rows, cols, d = tokens.shape
    wide, qwide = sizes(rows, cols)
    f32 = lambda *s: jax.ShapeDtypeStruct(s, F32)
    bf16 = lambda *s: jax.ShapeDtypeStruct(s, BF16)
    middle = rows - 2 * REACH
    nk = (2 + 2 * REACH) * wide
    key, grid, qgrid = bf16(rows * wide, d), f32(rows, wide, d), f32(rows, qwide, d)
    mid = f32(middle, qwide, d)
    out_shape = (
        (f32(8, d), bf16(*w_qkv.shape), bf16(*w_out.shape))
        + (key,) * 4
        + (grid, grid, qgrid, qgrid, f32(2 * REACH, qwide, d), mid, mid, grid, grid, f32(8, 128))
    )
    vmem = pl.BlockSpec(memory_space=pltpu.VMEM)
    hbm = pl.BlockSpec(memory_space=pltpu.HBM)
    tile = lambda dt: pltpu.VMEM((HEADS * 2 * qwide, nk), dt)
    scratch = [
        pltpu.SMEM((HEADS,), F32),
        pltpu.SemaphoreType.DMA((3,)),
        pltpu.VMEM((rows, wide, d), F32),
        pltpu.VMEM((rows, qwide, d), F32),
        pltpu.VMEM(col_a.shape, F32),
    ]
    scratch += [pltpu.VMEM((middle * qwide, d), BF16)] * 4
    scratch += [tile(F32), tile(F32), tile(BF16), tile(BF16)]
    return call(inner, out_shape, [hbm] + [vmem] * 4 + [hbm] * 2, scratch, 3_000_000_000)(
        pin(scale), tokens, grad_out, col_a, col_b, pin(w_qkv), pin(w_out)
    )


def outer_grads(tokens, grad_out, row_a, row_b, state):
    rows, cols, d = tokens.shape
    wide, qwide = sizes(rows, cols)
    nk = (2 + 2 * REACH) * wide
    out_shape = (
        jax.ShapeDtypeStruct((rows * cols, 3 * d), BF16),
        jax.ShapeDtypeStruct((2, d // 2 + 8, 4 * d), F32),
    )
    edge = pltpu.VMEM((4 * REACH, qwide, d), F32)
    tile = lambda dt: pltpu.VMEM((HEADS * 2 * qwide, nk), dt)
    scratch = [
        pltpu.VMEM((4 * REACH, wide, d), F32),
        pltpu.VMEM((2 * REACH, qwide, d), F32),
        pltpu.VMEM(row_a.shape, F32),
        edge,
        edge,
    ]
    scratch += [pltpu.VMEM((8 * REACH * wide, d), BF16)] * 4
    scratch += [pltpu.VMEM((4 * REACH * qwide, d), BF16)] * 4
    scratch += [tile(F32), tile(F32), tile(BF16), tile(BF16), edge, edge]
    scratch += [pltpu.VMEM((rows, wide, d), F32)] * 2
    vmem = pl.BlockSpec(memory_space=pltpu.VMEM)
    args = (tokens, grad_out, row_a, row_b) + tuple(state)
    return call(outer, out_shape, [vmem] * len(args), scratch, 3_000_000_000)(*args)


def finish(mine_ref, other_ref, wqkv_ref, wout_ref):
    half = mine_ref.shape[0]
    width = wqkv_ref.shape[1]
    first = lax.axis_index("rowlo") == 0
    mine, other = mine_ref[...].astype(F32), other_ref[...].astype(F32)
    upper = jnp.where(first, mine, other)
    lower = jnp.where(first, other, mine)
    wqkv_ref[0:half] = upper[:, :width]
    wout_ref[0:half] = upper[:, width:]
    wqkv_ref[half:] = lower[:, :width]
    wout_ref[half:] = lower[:, width:]


def finished(mine, other):
    half, width = mine.shape
    d = 2 * half
    vmem = pl.BlockSpec(memory_space=pltpu.VMEM)
    return pl.pallas_call(
        finish,
        out_shape=(
            jax.ShapeDtypeStruct((d, width - d), F32),
            jax.ShapeDtypeStruct((d, d), F32),
        ),
        in_specs=[vmem] * 2,
        out_specs=(vmem, vmem),
        compiler_params=pltpu.CompilerParams(vmem_limit_bytes=8 * 1024 * 1024),
        cost_estimate=pl.CostEstimate(flops=0, bytes_accessed=2_000_000, transcendentals=0),
    )(mine, other)


def swap_pairs(x, axis, first):
    shape = (lax.axis_size(ROW_AXES), lax.axis_size("col"))
    pairs = []
    for r in range(shape[0]):
        for c in range(shape[1]):
            at = [r, c]
            to = at[axis] + (1 if (at[axis] - first) % 2 == 0 else -1)
            if 0 <= to < shape[axis]:
                at[axis] = to
            else:
                at[1 - axis] ^= 1
            pairs.append((r * shape[1] + c, at[0] * shape[1] + at[1]))
    return lax.ppermute(x, ROW_AXES + ("col",), pairs)


def shards(tokens, grad_out, w_qkv, w_out, scale):
    rows, cols, d = tokens.shape
    tokens, grad_out, col_a, col_b, row_a, row_b = packed(tokens, grad_out)
    col_b = swap_pairs(col_b, 1, 1)
    col_a = swap_pairs(col_a, 1, 0)
    seg, last, _, _, _ = piece_layout(rows)
    odd = lax.axis_index("rowlo") % 2

    def with_corners(row, at):
        return jnp.concatenate(
            [row] + [lax.dynamic_slice_in_dim(c, at, seg, 0) for c in (col_a, col_b)], axis=0
        )

    row_b = swap_pairs(with_corners(row_b, odd * last), 0, 1)
    row_a = swap_pairs(with_corners(row_a, (1 - odd) * last), 0, 0)

    state = inner_grads(scale, tokens, grad_out, col_a, col_b, w_qkv, w_out)
    grads, partial = outer_grads(tokens, grad_out, row_a, row_b, state)
    grad_tokens = dot(grads, w_qkv, LAST).astype(BF16).reshape(rows, cols, d)

    lo = lax.axis_index("rowlo")
    swap = [(0, 1), (1, 0)]
    kept = lax.dynamic_index_in_dim(partial, lo, 0, keepdims=False)
    sent = lax.dynamic_index_in_dim(partial, 1 - lo, 0, keepdims=False)
    kept = kept + lax.ppermute(sent, "rowlo", swap)
    half = d // 2
    n = lax.axis_size(SPREAD_AXES)
    pieces = half // n if half % n == 0 else 1
    part = kept[:half].reshape(n, pieces, -1)
    sums = kept[half, :HEADS]
    sums_hi = lax.reduce_precision(sums, 8, 7)
    sums = jnp.concatenate([sums_hi, sums - sums_hi, jnp.zeros((128 - 2 * HEADS,), F32)])
    part = jnp.concatenate(
        [part.astype(BF16), jnp.broadcast_to(sums.astype(BF16), (n, pieces, 128))], axis=2
    )
    part = lax.all_to_all(part, SPREAD_AXES, 0, 0, tiled=True).astype(F32)
    part = jnp.sum(part, axis=0)
    sums = part[0, -128:]
    grad_scale = sums[:HEADS] + sums[HEADS : 2 * HEADS]
    part = part[:, :-128].astype(BF16)
    mine = lax.all_to_all(
        jnp.broadcast_to(part[None], (n,) + part.shape), SPREAD_AXES, 0, 0, tiled=True
    ).reshape(half, 4 * d)
    other = lax.ppermute(mine, "rowlo", swap)
    grad_wqkv, grad_wout = finished(mine, other)
    return grad_tokens, grad_wqkv, grad_wout, grad_scale


def solution(mesh):
    n_row, n_col = mesh.devices.shape
    fine = Mesh(mesh.devices.reshape(n_row // 2, 2, n_col), ("rowhi", "rowlo", "col"))
    block = P(ROW_AXES, "col", None)
    return jax.shard_map(
        shards,
        mesh=fine,
        in_specs=(block, block, P(), P(), P()),
        out_specs=(block, P(), P(), P()),
        check_vma=False,
    )
```

```python
import functools
import math

import jax
import jax.numpy as jnp
from jax import lax
from jax.experimental import pallas as pl
from jax.experimental.pallas import tpu as pltpu
from jax.sharding import Mesh
from jax.sharding import PartitionSpec as P

HEADS = 4
REACH = 3
F32 = jnp.float32
BF16 = jnp.bfloat16
LAST = (((1,), (1,)), ((), ()))
FIRST = (((0,), (0,)), ((), ()))
LOG2E = math.log2(math.e)
ROW_AXES = ("rowhi", "rowlo")
SPREAD_AXES = ("rowhi", "col")


def dot(a, b, dims=(((1,), (0,)), ((), ()))):
    return lax.dot_general(a, b, dims, preferred_element_type=F32)


def split(x):
    hi = x.astype(BF16)
    return hi, (x - hi.astype(F32)).astype(BF16)


def pin(x):
    return pltpu.with_memory_space_constraint(x, pltpu.HBM)


def piece_layout(rows):
    wide = 2 * REACH
    seg = -(-(wide * wide + REACH * REACH) // 16) * 16
    mid_tok = (rows - 2 * wide) * wide
    mid = -(-(mid_tok + (rows - 2 * REACH) * REACH) // 8) * 8
    tok, go = [], []
    for r in range(rows):
        if r < wide:
            tok.append(r * wide)
        elif r < rows - wide:
            tok.append(seg + (r - wide) * wide)
        else:
            tok.append(seg + mid + (r - rows + wide) * wide)
        if r < REACH:
            go.append(wide * wide + r * REACH)
        elif r < rows - REACH:
            go.append(seg + mid_tok + (r - REACH) * REACH)
        else:
            go.append(seg + mid + wide * wide + (r - rows + REACH) * REACH)
    return seg, seg + mid, 2 * seg + mid, tok, go


def pack(tok_hbm, go_hbm, tok_ref, go_ref, col_a, col_b, row_a, row_b, tf, gf, first, last, sems):
    rows, cols, d = tok_ref.shape
    copies = [
        pltpu.make_async_copy(tok_hbm, tok_ref, sems.at[0]),
        pltpu.make_async_copy(go_hbm, go_ref, sems.at[1]),
    ]
    for c in copies:
        c.start()
    wide = 2 * REACH
    _, _, _, tok_at, go_at = piece_layout(rows)
    even_row = lax.axis_index("rowlo") % 2 == 0
    even_col = lax.axis_index("col") % 2 == 0
    first[...] = jnp.zeros_like(first)
    last[...] = jnp.zeros_like(last)
    for c in copies:
        c.wait()
    tf[...] = tok_ref[...].astype(F32)
    gf[...] = go_ref[...].astype(F32)
    for r in range(rows):
        first[tok_at[r] : tok_at[r] + wide] = tf[r, 0:wide, :]
        last[tok_at[r] : tok_at[r] + wide] = tf[r, cols - wide : cols, :]
        first[go_at[r] : go_at[r] + REACH] = gf[r, 0:REACH, :]
        last[go_at[r] : go_at[r] + REACH] = gf[r, cols - REACH : cols, :]
    lo, hi = first[...], last[...]
    col_a[...] = jnp.where(even_col, hi, lo).astype(BF16)
    col_b[...] = jnp.where(even_col, lo, hi).astype(BF16)
    cut = wide * cols
    end = cut + REACH * cols
    lo = tf[0:wide].reshape(cut, d)
    hi = tf[rows - wide : rows].reshape(cut, d)
    row_a[0:cut] = jnp.where(even_row, hi, lo).astype(BF16)
    row_b[0:cut] = jnp.where(even_row, lo, hi).astype(BF16)
    lo = gf[0:REACH].reshape(end - cut, d)
    hi = gf[rows - REACH : rows].reshape(end - cut, d)
    row_a[cut:end] = jnp.where(even_row, hi, lo).astype(BF16)
    row_b[cut:end] = jnp.where(even_row, lo, hi).astype(BF16)


def packed(tokens, grad_out):
    rows, cols, d = tokens.shape
    size = piece_layout(rows)[2]
    vmem = pl.BlockSpec(memory_space=pltpu.VMEM)
    col = jax.ShapeDtypeStruct((size, d), BF16)
    row = jax.ShapeDtypeStruct((3 * REACH * cols, d), BF16)
    whole = jax.ShapeDtypeStruct((rows, cols, d), BF16)
    block = pltpu.VMEM((rows, cols, d), F32)
    return pl.pallas_call(
        pack,
        out_shape=(whole, whole, col, col, row, row),
        in_specs=[pl.BlockSpec(memory_space=pltpu.HBM)] * 2,
        out_specs=(vmem,) * 6,
        scratch_shapes=[
            block,
            block,
            pltpu.VMEM((size, d), F32),
            pltpu.VMEM((size, d), F32),
            pltpu.SemaphoreType.DMA((2,)),
        ],
        compiler_params=pltpu.CompilerParams(vmem_limit_bytes=8 * 1024 * 1024),
        cost_estimate=pl.CostEstimate(flops=0, bytes_accessed=1_000_000, transcendentals=0),
    )(pin(tokens), pin(grad_out))


def unit(x, head_sum):
    r = lax.rsqrt(head_sum(x * x) + 1e-06)
    return x * r, r


def tools(d):
    per = d // HEADS
    lane_head = lax.broadcasted_iota(jnp.int32, (1, d), 1) // per
    heads = [lane_head == h for h in range(HEADS)]
    ones = (
        lax.broadcasted_iota(jnp.int32, (d, d), 0) // per
        == lax.broadcasted_iota(jnp.int32, (d, d), 1) // per
    ).astype(BF16)

    def head_sum(x):
        hi, lo = split(x)
        return dot(hi, ones) + dot(lo, ones)

    def spread(x):
        zero = jnp.zeros_like(x)
        return jnp.concatenate([jnp.where(m, x, zero) for m in heads], axis=0)

    def gather(x):
        n = x.shape[0] // HEADS
        out = x[0:n]
        for h in range(1, HEADS):
            out = jnp.where(heads[h], x[h * n : (h + 1) * n], out)
        return out

    return heads, head_sum, spread, gather


def has_neighbours(axis):
    at = lax.axis_index(axis)
    return at > 0, at < lax.axis_size(axis) - 1


def near_mask(qwide, wide, cols):
    nq, nk = 2 * qwide, (2 + 2 * REACH) * wide
    i = lax.broadcasted_iota(jnp.int32, (nq, nk), 0)
    j = lax.broadcasted_iota(jnp.int32, (nq, nk), 1)
    dr = j // wide - i // qwide
    dc = j % wide - i % qwide
    key_col = j % wide + (lax.axis_index("col") * cols - 8)
    near = (dr >= 0) & (dr <= 2 * REACH) & (dc >= 0) & (dc <= 2 * REACH)
    near = near & (key_col >= 0) & (key_col < cols * lax.axis_size("col"))
    return near.astype(F32)


def run_bands(bands, sbuf, dbuf, pbuf, dsbuf, nq, spread):
    def scores(band):
        q_hi, q_lo = spread(band["q_hi"]()), spread(band["q_lo"]())
        k_hi = band["k_hi"]()
        sbuf[...] = dot(q_hi, k_hi, LAST) + dot(q_lo, k_hi, LAST) + dot(q_hi, band["k_lo"](), LAST)
        g_hi, g_lo = spread(band["g_hi"]()), spread(band["g_lo"]())
        v_hi = band["v_hi"]()
        dbuf[...] = dot(g_hi, v_hi, LAST) + dot(g_lo, v_hi, LAST) + dot(g_hi, band["v_lo"](), LAST)

    def softmax(band, total):
        mask, own = band["mask"](), band["own"]()
        out = []
        for h in range(HEADS):
            at = slice(h * nq, (h + 1) * nq)
            s, dp = sbuf[at], dbuf[at]
            e = jnp.exp2(s) * mask
            r = 1.0 / (jnp.sum(e, axis=1, keepdims=True) + 1e-30)
            p = e * r
            ds = p * (dp - jnp.sum(p * dp, axis=1, keepdims=True))
            if own is None:
                out.append(total[h])
            else:
                out.append(total[h] + own * jnp.sum(ds * s, axis=1, keepdims=True))
            pbuf[at] = p.astype(BF16)
            dsbuf[at] = ds.astype(BF16)
        return out

    total = [jnp.zeros((nq, 1), F32) for _ in range(HEADS)]
    count = len(bands)
    scores(bands[0])
    for b in range(count + 1):
        if b > 0:
            bands[b - 1]["grads"](pbuf, dsbuf)
        if b < count:
            total = softmax(bands[b], total)
        if b + 1 < count:
            scores(bands[b + 1])
    return [jnp.sum(t, axis=0, keepdims=True) for t in total]


def inner(
    scale_hbm,
    tok_ref,
    go_ref,
    col_a,
    col_b,
    wqkv_hbm,
    wout_hbm,
    sl_ref,
    wqkv_ref,
    wout_ref,
    khi,
    klo,
    vhi,
    vlo,
    kf,
    kr,
    qf,
    qr,
    ga_ref,
    gq,
    att,
    gk,
    gv,
    psum,
    scale_ref,
    sems,
    tx,
    gx,
    side,
    qhi,
    qlo,
    ghi,
    glo,
    sbuf,
    dbuf,
    pbuf,
    dsbuf,
):
    copies = [
        pltpu.make_async_copy(scale_hbm, scale_ref, sems.at[0]),
        pltpu.make_async_copy(wqkv_hbm, wqkv_ref, sems.at[1]),
        pltpu.make_async_copy(wout_hbm, wout_ref, sems.at[2]),
    ]
    for c in copies:
        c.start()
    rows, cols, d = tok_ref.shape
    _, wide, _ = tx.shape
    _, qwide, _ = gx.shape
    reach2 = 2 * REACH
    q0 = 8 - REACH - 2
    own_q = 8 - q0
    heads, head_sum, spread, gather = tools(d)

    tx[:, 0:8, :] = jnp.zeros((rows, 8, d), F32)
    tx[:, 8 + cols : wide, :] = jnp.zeros((rows, wide - 8 - cols, d), F32)
    gx[:, 0:8, :] = jnp.zeros((rows, 8, d), F32)
    tx[:, 8 : 8 + cols, :] = tok_ref[...].astype(F32)
    gx[:, own_q : own_q + cols, :] = go_ref[...].astype(F32)
    even_col = lax.axis_index("col") % 2 == 0
    _, _, _, tok_at, go_at = piece_layout(rows)
    has_left, has_right = has_neighbours("col")
    for even, valid, at_k, at_q in (
        (~even_col, has_left, 8 - reach2, own_q - REACH),
        (even_col, has_right, 8 + cols, own_q + cols),
    ):
        x = jnp.where(even, col_a[...].astype(F32), col_b[...].astype(F32))
        side[...] = jnp.where(valid, x, jnp.zeros_like(x))
        for r in range(rows):
            tx[r, at_k : at_k + reach2, :] = side[tok_at[r] : tok_at[r] + reach2]
            gx[r, at_q : at_q + REACH, :] = side[go_at[r] : go_at[r] + REACH]

    for c in copies:
        c.wait()
    sl = jnp.zeros((1, d), F32)
    for h in range(HEADS):
        sl = jnp.where(heads[h], scale_ref[h], sl)
    sl_ref[...] = jnp.broadcast_to(sl, sl_ref.shape)

    step = rows // 2
    for c in range(0, rows, step):
        at = slice(c, c + step)
        x = tx[at].reshape(step * wide, d).astype(BF16)
        kv = dot(x, wqkv_ref[:, d:])
        k, rk = unit(kv[:, :d], head_sum)
        kf[at] = k.reshape(step, wide, d)
        kr[at] = rk.reshape(step, wide, d)
        flat = slice(c * wide, (c + step) * wide)
        khi[flat], klo[flat] = split(k)
        vhi[flat], vlo[flat] = split(kv[:, d:])
    x = tx[:, q0 : q0 + qwide, :].reshape(rows * qwide, d).astype(BF16)
    q, rq = unit(dot(x, wqkv_ref[:, :d]), head_sum)
    qf[...] = q.reshape(rows, qwide, d)
    qr[...] = rq.reshape(rows, qwide, d)
    g = dot(gx[...].reshape(rows * qwide, d).astype(BF16), wout_ref[...], LAST)
    lo, hi = REACH * qwide, (rows - REACH) * qwide
    qhi[...], qlo[...] = split(q[lo:hi] * (sl * LOG2E))
    ghi[...], glo[...] = split(g[lo:hi])
    ga_ref[0:REACH] = g[0:lo].reshape(REACH, qwide, d)
    ga_ref[REACH:] = g[hi:].reshape(REACH, qwide, d)
    gk[...] = jnp.zeros_like(gk)
    gv[...] = jnp.zeros_like(gv)

    nq = 2 * qwide
    span = 2 + reach2
    near = near_mask(qwide, wide, cols)
    iq = lax.broadcasted_iota(jnp.int32, (nq, 1), 0) % qwide
    own = ((iq >= own_q) & (iq < own_q + cols)).astype(F32)

    def band(b):
        at = slice(b * nq, (b + 1) * nq)
        keys = slice(b * 2 * wide, b * 2 * wide + span * wide)

        def grads(pbuf, dsbuf):
            p, ds = pbuf[...], dsbuf[...]
            att[2 * b : 2 * b + 2] = gather(dot(p, vhi[keys])).reshape(2, qwide, d)
            gq[2 * b : 2 * b + 2] = gather(dot(ds, khi[keys])).reshape(2, qwide, d)
            eight = slice(2 * b, 2 * b + span)
            gk[eight] += dot(ds, spread(qhi[at]), FIRST).reshape(span, wide, d)
            gv[eight] += dot(p, spread(ghi[at]), FIRST).reshape(span, wide, d)

        return {
            "q_hi": lambda: qhi[at],
            "q_lo": lambda: qlo[at],
            "g_hi": lambda: ghi[at],
            "g_lo": lambda: glo[at],
            "k_hi": lambda: khi[keys],
            "k_lo": lambda: klo[keys],
            "v_hi": lambda: vhi[keys],
            "v_lo": lambda: vlo[keys],
            "mask": lambda: near,
            "own": lambda: own,
            "grads": grads,
        }

    bands = [band(b) for b in range((rows - reach2) // 2)]
    total = run_bands(bands, sbuf, dbuf, pbuf, dsbuf, nq, spread)
    lane = lax.broadcasted_iota(jnp.int32, psum.shape, 1)
    sums = jnp.zeros(psum.shape, F32)
    for h in range(HEADS):
        sums = jnp.where(lane == h, total[h], sums)
    psum[...] = sums


def outer(
    tok_ref,
    go_ref,
    row_a,
    row_b,
    sl_ref,
    wqkv_ref,
    wout_ref,
    khi_in,
    klo_in,
    vhi_in,
    vlo_in,
    kf,
    kr,
    qf,
    qr,
    ga_in,
    gq_in,
    att_in,
    gk_in,
    gv_in,
    psum,
    grads_ref,
    kept_ref,
    sent_ref,
    tx,
    gx,
    ends,
    qe,
    ge,
    khi,
    klo,
    vhi,
    vlo,
    qhi,
    qlo,
    ghi,
    glo,
    sbuf,
    dbuf,
    pbuf,
    dsbuf,
    gq,
    att,
    gk,
    gv,
):
    rows, cols, d = tok_ref.shape
    _, wide, _ = tx.shape
    _, qwide, _ = gx.shape
    reach2 = 2 * REACH
    q0 = 8 - REACH - 2
    own_q = 8 - q0
    n_rows = rows * lax.axis_size(ROW_AXES)
    row_first = lax.axis_index(ROW_AXES) * rows
    heads, head_sum, spread, gather = tools(d)
    sl = sl_ref[0:1]

    left_k, right_k = 8 - reach2, 8 + cols
    left_q, right_q = own_q - REACH, own_q + cols
    tx[:, 0:8, :] = jnp.zeros((2 * reach2, 8, d), F32)
    tx[:, 8 + cols : wide, :] = jnp.zeros((2 * reach2, wide - 8 - cols, d), F32)
    gx[:, 0:8, :] = jnp.zeros((reach2, 8, d), F32)
    even_row = lax.axis_index("rowlo") % 2 == 0
    even_col = lax.axis_index("col") % 2 == 0
    seg = piece_layout(rows)[0]
    cut = reach2 * cols
    end = cut + REACH * cols
    has_above, has_below = has_neighbours(ROW_AXES)
    has_left, has_right = has_neighbours("col")
    for even, valid, row_k, row_q in (
        (~even_row, has_above, 0, 0),
        (even_row, has_below, reach2, REACH),
    ):
        x = jnp.where(even, row_a[...].astype(F32), row_b[...].astype(F32))
        ends[...] = jnp.where(valid, x, jnp.zeros_like(x))
        tx[row_k : row_k + reach2, 8 : 8 + cols, :] = ends[0:cut].reshape(reach2, cols, d)
        gx[row_q : row_q + REACH, own_q : own_q + cols, :] = ends[cut:end].reshape(REACH, cols, d)
        first, last = ends[end : end + seg], ends[end + seg : end + 2 * seg]
        none = jnp.zeros_like(first)
        ends[end : end + seg] = jnp.where(has_left, jnp.where(even_col, last, first), none)
        ends[end + seg : end + 2 * seg] = jnp.where(has_right, jnp.where(even_col, first, last), none)
        for base, at_k, at_q in ((end, left_k, left_q), (end + seg, right_k, right_q)):
            for r in range(reach2):
                at = base + r * reach2
                tx[row_k + r, at_k : at_k + reach2, :] = ends[at : at + reach2]
            for r in range(REACH):
                at = base + reach2 * reach2 + r * REACH
                gx[row_q + r, at_q : at_q + REACH, :] = ends[at : at + REACH]

    m = reach2 * wide
    x = tx[...].reshape(2 * m, d).astype(BF16)
    kv = dot(x, wqkv_ref[:, d:])
    k, _ = unit(kv[:, :d], head_sum)
    for hi, lo, hi_in, lo_in, fresh in (
        (khi, klo, khi_in, klo_in, k),
        (vhi, vlo, vhi_in, vlo_in, kv[:, d:]),
    ):
        fresh_hi, fresh_lo = split(fresh)
        hi[0:m], lo[0:m] = fresh_hi[0:m], fresh_lo[0:m]
        hi[3 * m :], lo[3 * m :] = fresh_hi[m:], fresh_lo[m:]
        own_end = rows * wide
        for to, source in ((hi, hi_in), (lo, lo_in)):
            to[m : 2 * m] = source[0:m]
            to[2 * m : 3 * m] = source[own_end - m : own_end]
    x = tx[REACH : 3 * REACH, q0 : q0 + qwide, :].reshape(reach2 * qwide, d).astype(BF16)
    q, _ = unit(dot(x, wqkv_ref[:, :d]), head_sum)
    q = q.reshape(reach2, qwide, d)
    g = dot(gx[...].reshape(reach2 * qwide, d).astype(BF16), wout_ref[...], LAST)
    g = g.reshape(reach2, qwide, d)
    qe[0:REACH], qe[3 * REACH :] = q[0:REACH], q[REACH:]
    ge[0:REACH], ge[3 * REACH :] = g[0:REACH], g[REACH:]
    qe[REACH:reach2], qe[reach2 : 3 * REACH] = qf[0:REACH], qf[rows - REACH :]
    ge[REACH : 3 * REACH] = ga_in[...]
    flat = 2 * reach2 * qwide
    qhi[...], qlo[...] = split(qe[...].reshape(flat, d) * (sl * LOG2E))
    ghi[...], glo[...] = split(ge[...].reshape(flat, d))
    gk[...] = gk_in[...]
    gv[...] = gv_in[...]

    nq = 2 * qwide
    span = 2 + reach2
    nk = span * wide
    near = near_mask(qwide, wide, cols)
    jr = lax.broadcasted_iota(jnp.int32, (1, nk), 1) // wide
    iq = lax.broadcasted_iota(jnp.int32, (nq, 1), 0)
    own_col = (iq % qwide >= own_q) & (iq % qwide < own_q + cols)

    def band(b):
        top = b < REACH
        first = 2 * b if top else rows + 2 * (b - REACH)
        at = slice(b * nq, (b + 1) * nq)
        key_at = 2 * b if top else 2 * reach2 + 2 * (b - REACH)
        keys = slice(key_at * wide, key_at * wide + nk)
        mine = first + 1 >= REACH and first < rows + REACH
        skip = reach2 - first if top else 0
        count = span - skip if top else reach2 - 2 * (b - REACH)
        to = 0 if top else rows - count
        part = slice(skip * wide, (skip + count) * wide)

        def mask():
            key_row = jr + (row_first - reach2 + first)
            return near * ((key_row >= 0) & (key_row < n_rows)).astype(F32)

        def own():
            if not mine:
                return None
            q_row = iq // qwide + first
            return (own_col & (q_row >= REACH) & (q_row < REACH + rows)).astype(F32)

        def grads(pbuf, dsbuf):
            if mine:
                att[2 * b : 2 * b + 2] = gather(dot(pbuf[...], vhi[keys])).reshape(2, qwide, d)
                gq[2 * b : 2 * b + 2] = gather(dot(dsbuf[...], khi[keys])).reshape(2, qwide, d)
            p, ds = pbuf[:, part], dsbuf[:, part]
            own_rows = slice(to, to + count)
            gk[own_rows] += dot(ds, spread(qhi[at]), FIRST).reshape(count, wide, d)
            gv[own_rows] += dot(p, spread(ghi[at]), FIRST).reshape(count, wide, d)

        return {
            "q_hi": lambda: qhi[at],
            "q_lo": lambda: qlo[at],
            "g_hi": lambda: ghi[at],
            "g_lo": lambda: glo[at],
            "k_hi": lambda: khi[keys],
            "k_lo": lambda: klo[keys],
            "v_hi": lambda: vhi[keys],
            "v_lo": lambda: vlo[keys],
            "mask": mask,
            "own": own,
            "grads": grads,
        }

    total = run_bands([band(b) for b in range(reach2)], sbuf, dbuf, pbuf, dsbuf, nq, spread)

    n = rows * cols
    key_cols = slice(8, 8 + cols)
    query_cols = slice(own_q, own_q + cols)

    def own_queries(edge, middle):
        parts = [
            edge[REACH:reach2, query_cols, :],
            middle[:, query_cols, :],
            edge[reach2 : 3 * REACH, query_cols, :],
        ]
        return jnp.concatenate(parts, axis=0).reshape(n, d)

    def unit_back(u, r, g):
        return r * (g - u * head_sum(u * g))

    g_q = unit_back(
        qf[:, query_cols, :].reshape(n, d),
        qr[:, query_cols, :].reshape(n, d),
        own_queries(gq, gq_in) * sl,
    )
    g_k = unit_back(
        kf[:, key_cols, :].reshape(n, d),
        kr[:, key_cols, :].reshape(n, d),
        gk[:, key_cols, :].reshape(n, d) * (1.0 / LOG2E),
    )
    g_v = gv[:, key_cols, :].reshape(n, d)
    grads = jnp.concatenate([g_q.astype(BF16), g_k.astype(BF16), g_v.astype(BF16)], axis=1)
    grads_ref[...] = grads
    wq = dot(tok_ref[...].reshape(n, d), grads, FIRST)
    wo = dot(own_queries(att, att_in).astype(BF16), go_ref[...].reshape(n, d), FIRST)
    half = d // 2
    lane = lax.broadcasted_iota(jnp.int32, (8, 4 * d), 1)
    kept, sent = jnp.zeros((8, 4 * d), F32), jnp.zeros((8, 4 * d), F32)
    for h in range(HEADS):
        at = h * (d // HEADS)
        t = (total[h] + psum[0:1, h : h + 1]) / (sl[:, at : at + 1] * LOG2E)
        hi = t.astype(BF16).astype(F32)
        kept = jnp.where(lane == h, t, kept)
        sent = jnp.where(lane == h, hi, sent)
        sent = jnp.where(lane == HEADS + h, t - hi, sent)
    first = lax.axis_index("rowlo") == 0
    for x, at in ((wq, slice(0, 3 * d)), (wo, slice(3 * d, 4 * d))):
        kept_ref[0:half, at] = jnp.where(first, x[:half], x[half:])
        sent_ref[0:half, at] = jnp.where(first, x[half:], x[:half]).astype(BF16)
    kept_ref[half:, :] = kept
    sent_ref[half:, :] = sent.astype(BF16)


def sizes(rows, cols):
    wide = -(-(cols + 4 * REACH + 2) // 16) * 16
    qwide = -(-(cols + 2 * REACH + 2) // 8) * 8
    return wide, qwide


def call(body, out_shape, in_specs, scratch, flops):
    vmem = pl.BlockSpec(memory_space=pltpu.VMEM)
    return pl.pallas_call(
        body,
        out_shape=out_shape,
        in_specs=in_specs,
        out_specs=(vmem,) * len(out_shape),
        scratch_shapes=scratch,
        compiler_params=pltpu.CompilerParams(vmem_limit_bytes=24 * 1024 * 1024),
        cost_estimate=pl.CostEstimate(
            flops=flops, bytes_accessed=4_000_000, transcendentals=300_000
        ),
    )


def inner_grads(scale, tokens, grad_out, col_a, col_b, w_qkv, w_out):
    rows, cols, d = tokens.shape
    wide, qwide = sizes(rows, cols)
    f32 = lambda *s: jax.ShapeDtypeStruct(s, F32)
    bf16 = lambda *s: jax.ShapeDtypeStruct(s, BF16)
    middle = rows - 2 * REACH
    nk = (2 + 2 * REACH) * wide
    key, grid, qgrid = bf16(rows * wide, d), f32(rows, wide, d), f32(rows, qwide, d)
    mid = f32(middle, qwide, d)
    out_shape = (
        (f32(8, d), bf16(*w_qkv.shape), bf16(*w_out.shape))
        + (key,) * 4
        + (grid, grid, qgrid, qgrid, f32(2 * REACH, qwide, d), mid, mid, grid, grid, f32(8, 128))
    )
    vmem = pl.BlockSpec(memory_space=pltpu.VMEM)
    hbm = pl.BlockSpec(memory_space=pltpu.HBM)
    tile = lambda dt: pltpu.VMEM((HEADS * 2 * qwide, nk), dt)
    scratch = [
        pltpu.SMEM((HEADS,), F32),
        pltpu.SemaphoreType.DMA((3,)),
        pltpu.VMEM((rows, wide, d), F32),
        pltpu.VMEM((rows, qwide, d), F32),
        pltpu.VMEM(col_a.shape, F32),
    ]
    scratch += [pltpu.VMEM((middle * qwide, d), BF16)] * 4
    scratch += [tile(F32), tile(F32), tile(BF16), tile(BF16)]
    return call(inner, out_shape, [hbm] + [vmem] * 4 + [hbm] * 2, scratch, 3_000_000_000)(
        pin(scale), tokens, grad_out, col_a, col_b, pin(w_qkv), pin(w_out)
    )


def outer_grads(tokens, grad_out, row_a, row_b, state):
    rows, cols, d = tokens.shape
    wide, qwide = sizes(rows, cols)
    nk = (2 + 2 * REACH) * wide
    out_shape = (
        jax.ShapeDtypeStruct((rows * cols, 3 * d), BF16),
        jax.ShapeDtypeStruct((d // 2 + 8, 4 * d), F32),
        jax.ShapeDtypeStruct((d // 2 + 8, 4 * d), BF16),
    )
    edge = pltpu.VMEM((4 * REACH, qwide, d), F32)
    tile = lambda dt: pltpu.VMEM((HEADS * 2 * qwide, nk), dt)
    scratch = [
        pltpu.VMEM((4 * REACH, wide, d), F32),
        pltpu.VMEM((2 * REACH, qwide, d), F32),
        pltpu.VMEM(row_a.shape, F32),
        edge,
        edge,
    ]
    scratch += [pltpu.VMEM((8 * REACH * wide, d), BF16)] * 4
    scratch += [pltpu.VMEM((4 * REACH * qwide, d), BF16)] * 4
    scratch += [tile(F32), tile(F32), tile(BF16), tile(BF16), edge, edge]
    scratch += [pltpu.VMEM((rows, wide, d), F32)] * 2
    vmem = pl.BlockSpec(memory_space=pltpu.VMEM)
    args = (tokens, grad_out, row_a, row_b) + tuple(state)
    return call(outer, out_shape, [vmem] * len(args), scratch, 3_000_000_000)(*args)


def put_half(piece_ref, *refs, other):
    *_, wqkv_hbm, wout_hbm, wqkv, wout, sems = refs
    half = piece_ref.shape[0]
    width = wqkv.shape[1]
    lo = lax.axis_index("rowlo")
    lo = 1 - lo if other else lo
    rows = pl.ds(pl.multiple_of(lo * half, half), half)
    wqkv[...] = piece_ref[:, :width].astype(F32)
    first = pltpu.make_async_copy(wqkv, wqkv_hbm.at[rows], sems.at[0])
    first.start()
    wout[...] = piece_ref[:, width:].astype(F32)
    second = pltpu.make_async_copy(wout, wout_hbm.at[rows], sems.at[1])
    second.start()
    first.wait()
    second.wait()


def put(piece, into, other):
    half, width = piece.shape
    d = 2 * half
    hbm = pl.BlockSpec(memory_space=pltpu.HBM)
    return pl.pallas_call(
        functools.partial(put_half, other=other),
        out_shape=(
            jax.ShapeDtypeStruct((d, width - d), F32),
            jax.ShapeDtypeStruct((d, d), F32),
        ),
        in_specs=[pl.BlockSpec(memory_space=pltpu.VMEM)] + [hbm] * len(into),
        out_specs=(hbm, hbm),
        scratch_shapes=[
            pltpu.VMEM((half, width - d), F32),
            pltpu.VMEM((half, d), F32),
            pltpu.SemaphoreType.DMA((2,)),
        ],
        input_output_aliases={1: 0, 2: 1} if into else {},
        compiler_params=pltpu.CompilerParams(vmem_limit_bytes=8 * 1024 * 1024),
        cost_estimate=pl.CostEstimate(flops=0, bytes_accessed=2_000_000, transcendentals=0),
    )(piece, *into)


def swap_pairs(x, axis, first):
    shape = (lax.axis_size(ROW_AXES), lax.axis_size("col"))
    pairs = []
    for r in range(shape[0]):
        for c in range(shape[1]):
            at = [r, c]
            to = at[axis] + (1 if (at[axis] - first) % 2 == 0 else -1)
            if 0 <= to < shape[axis]:
                at[axis] = to
            else:
                at[1 - axis] ^= 1
            pairs.append((r * shape[1] + c, at[0] * shape[1] + at[1]))
    return lax.ppermute(x, ROW_AXES + ("col",), pairs)


def shards(tokens, grad_out, w_qkv, w_out, scale):
    rows, cols, d = tokens.shape
    tokens, grad_out, col_a, col_b, row_a, row_b = packed(tokens, grad_out)
    col_b = swap_pairs(col_b, 1, 1)
    col_a = swap_pairs(col_a, 1, 0)
    seg, last, _, _, _ = piece_layout(rows)
    odd = lax.axis_index("rowlo") % 2

    def with_corners(row, at):
        return jnp.concatenate(
            [row] + [lax.dynamic_slice_in_dim(c, at, seg, 0) for c in (col_a, col_b)], axis=0
        )

    row_b = swap_pairs(with_corners(row_b, odd * last), 0, 1)
    row_a = swap_pairs(with_corners(row_a, (1 - odd) * last), 0, 0)

    state = inner_grads(scale, tokens, grad_out, col_a, col_b, w_qkv, w_out)
    grads, kept, sent = outer_grads(tokens, grad_out, row_a, row_b, state)
    grad_tokens = dot(grads, w_qkv, LAST).astype(BF16).reshape(rows, cols, d)

    swap = [(0, 1), (1, 0)]
    kept = kept + lax.ppermute(sent, "rowlo", swap).astype(F32)
    kept, grad_tokens = lax.optimization_barrier((kept, grad_tokens))
    half = d // 2
    n = lax.axis_size(SPREAD_AXES)
    pieces = half // n if half % n == 0 else 1
    part = kept[:half].reshape(n, pieces, -1)
    sums = kept[half, :HEADS] + kept[half, HEADS : 2 * HEADS]
    sums_hi = lax.reduce_precision(sums, 8, 7)
    sums = jnp.concatenate([sums_hi, sums - sums_hi, jnp.zeros((128 - 2 * HEADS,), F32)])
    part = jnp.concatenate(
        [part.astype(BF16), jnp.broadcast_to(sums.astype(BF16), (n, pieces, 128))], axis=2
    )
    part = lax.all_to_all(part, SPREAD_AXES, 0, 0, tiled=True).astype(F32)
    part = jnp.sum(part, axis=0)
    sums = part[0, -128:]
    grad_scale = sums[:HEADS] + sums[HEADS : 2 * HEADS]
    part = part[:, :-128].astype(BF16)
    mine = lax.all_to_all(
        jnp.broadcast_to(part[None], (n,) + part.shape), SPREAD_AXES, 0, 0, tiled=True
    ).reshape(half, 4 * d)
    other = lax.ppermute(mine, "rowlo", swap)
    grad_wqkv, grad_wout = put(other, put(mine, (), False), True)
    return grad_tokens, grad_wqkv, grad_wout, grad_scale


def solution(mesh):
    n_row, n_col = mesh.devices.shape
    fine = Mesh(mesh.devices.reshape(n_row // 2, 2, n_col), ("rowhi", "rowlo", "col"))
    block = P(ROW_AXES, "col", None)
    return jax.shard_map(
        shards,
        mesh=fine,
        in_specs=(block, block, P(), P(), P()),
        out_specs=(block, P(), P(), P()),
        check_vma=False,
    )
```

```python
import functools
import math

import jax
import jax.numpy as jnp
from jax import lax
from jax.experimental import pallas as pl
from jax.experimental.pallas import tpu as pltpu
from jax.sharding import Mesh
from jax.sharding import PartitionSpec as P

HEADS = 4
REACH = 3
F32 = jnp.float32
BF16 = jnp.bfloat16
LAST = (((1,), (1,)), ((), ()))
FIRST = (((0,), (0,)), ((), ()))
LOG2E = math.log2(math.e)
ROW_AXES = ("rowhi", "rowlo")
SPREAD_AXES = ("rowhi", "col")


def dot(a, b, dims=(((1,), (0,)), ((), ()))):
    return lax.dot_general(a, b, dims, preferred_element_type=F32)


def split(x):
    hi = x.astype(BF16)
    return hi, (x - hi.astype(F32)).astype(BF16)


def pin(x):
    return pltpu.with_memory_space_constraint(x, pltpu.HBM)


def piece_layout(rows):
    wide = 2 * REACH
    seg = -(-(wide * wide + REACH * REACH) // 16) * 16
    mid_tok = (rows - 2 * wide) * wide
    mid = -(-(mid_tok + (rows - 2 * REACH) * REACH) // 8) * 8
    tok, go = [], []
    for r in range(rows):
        if r < wide:
            tok.append(r * wide)
        elif r < rows - wide:
            tok.append(seg + (r - wide) * wide)
        else:
            tok.append(seg + mid + (r - rows + wide) * wide)
        if r < REACH:
            go.append(wide * wide + r * REACH)
        elif r < rows - REACH:
            go.append(seg + mid_tok + (r - REACH) * REACH)
        else:
            go.append(seg + mid + wide * wide + (r - rows + REACH) * REACH)
    return seg, seg + mid, 2 * seg + mid, tok, go


def pack(tok_hbm, go_hbm, tok_ref, go_ref, col_a, col_b, row_a, row_b, tf, gf, first, last, sems):
    rows, cols, d = tok_ref.shape
    copies = [
        pltpu.make_async_copy(tok_hbm, tok_ref, sems.at[0]),
        pltpu.make_async_copy(go_hbm, go_ref, sems.at[1]),
    ]
    for c in copies:
        c.start()
    wide = 2 * REACH
    _, _, _, tok_at, go_at = piece_layout(rows)
    even_row = lax.axis_index("rowlo") % 2 == 0
    even_col = lax.axis_index("col") % 2 == 0
    first[...] = jnp.zeros_like(first)
    last[...] = jnp.zeros_like(last)
    for c in copies:
        c.wait()
    tf[...] = tok_ref[...].astype(F32)
    gf[...] = go_ref[...].astype(F32)
    for r in range(rows):
        first[tok_at[r] : tok_at[r] + wide] = tf[r, 0:wide, :]
        last[tok_at[r] : tok_at[r] + wide] = tf[r, cols - wide : cols, :]
        first[go_at[r] : go_at[r] + REACH] = gf[r, 0:REACH, :]
        last[go_at[r] : go_at[r] + REACH] = gf[r, cols - REACH : cols, :]
    lo, hi = first[...], last[...]
    col_a[...] = jnp.where(even_col, hi, lo).astype(BF16)
    col_b[...] = jnp.where(even_col, lo, hi).astype(BF16)
    cut = wide * cols
    end = cut + REACH * cols
    lo = tf[0:wide].reshape(cut, d)
    hi = tf[rows - wide : rows].reshape(cut, d)
    row_a[0:cut] = jnp.where(even_row, hi, lo).astype(BF16)
    row_b[0:cut] = jnp.where(even_row, lo, hi).astype(BF16)
    lo = gf[0:REACH].reshape(end - cut, d)
    hi = gf[rows - REACH : rows].reshape(end - cut, d)
    row_a[cut:end] = jnp.where(even_row, hi, lo).astype(BF16)
    row_b[cut:end] = jnp.where(even_row, lo, hi).astype(BF16)


def packed(tokens, grad_out):
    rows, cols, d = tokens.shape
    size = piece_layout(rows)[2]
    vmem = pl.BlockSpec(memory_space=pltpu.VMEM)
    col = jax.ShapeDtypeStruct((size, d), BF16)
    row = jax.ShapeDtypeStruct((3 * REACH * cols, d), BF16)
    whole = jax.ShapeDtypeStruct((rows, cols, d), BF16)
    block = pltpu.VMEM((rows, cols, d), F32)
    return pl.pallas_call(
        pack,
        out_shape=(whole, whole, col, col, row, row),
        in_specs=[pl.BlockSpec(memory_space=pltpu.HBM)] * 2,
        out_specs=(vmem,) * 6,
        scratch_shapes=[
            block,
            block,
            pltpu.VMEM((size, d), F32),
            pltpu.VMEM((size, d), F32),
            pltpu.SemaphoreType.DMA((2,)),
        ],
        compiler_params=pltpu.CompilerParams(vmem_limit_bytes=8 * 1024 * 1024),
        cost_estimate=pl.CostEstimate(flops=0, bytes_accessed=1_000_000, transcendentals=0),
    )(pin(tokens), pin(grad_out))


def unit(x, head_sum):
    r = lax.rsqrt(head_sum(x * x) + 1e-06)
    return x * r, r


def tools(d):
    per = d // HEADS
    lane_head = lax.broadcasted_iota(jnp.int32, (1, d), 1) // per
    heads = [lane_head == h for h in range(HEADS)]
    ones = (
        lax.broadcasted_iota(jnp.int32, (d, d), 0) // per
        == lax.broadcasted_iota(jnp.int32, (d, d), 1) // per
    ).astype(BF16)

    def head_sum(x):
        hi, lo = split(x)
        return dot(hi, ones) + dot(lo, ones)

    def spread(x):
        zero = jnp.zeros_like(x)
        return jnp.concatenate([jnp.where(m, x, zero) for m in heads], axis=0)

    def gather(x):
        n = x.shape[0] // HEADS
        out = x[0:n]
        for h in range(1, HEADS):
            out = jnp.where(heads[h], x[h * n : (h + 1) * n], out)
        return out

    return heads, head_sum, spread, gather


def has_neighbours(axis):
    at = lax.axis_index(axis)
    return at > 0, at < lax.axis_size(axis) - 1


def near_mask(qwide, wide, cols):
    nq, nk = 2 * qwide, (2 + 2 * REACH) * wide
    i = lax.broadcasted_iota(jnp.int32, (nq, nk), 0)
    j = lax.broadcasted_iota(jnp.int32, (nq, nk), 1)
    dr = j // wide - i // qwide
    dc = j % wide - i % qwide
    key_col = j % wide + (lax.axis_index("col") * cols - 8)
    near = (dr >= 0) & (dr <= 2 * REACH) & (dc >= 0) & (dc <= 2 * REACH)
    near = near & (key_col >= 0) & (key_col < cols * lax.axis_size("col"))
    return near.astype(F32)


def run_bands(bands, sbuf, dbuf, pbuf, dsbuf, nq, spread):
    def scores(band):
        q_hi, q_lo = spread(band["q_hi"]()), spread(band["q_lo"]())
        k_hi = band["k_hi"]()
        sbuf[...] = dot(q_hi, k_hi, LAST) + dot(q_lo, k_hi, LAST) + dot(q_hi, band["k_lo"](), LAST)
        g_hi, g_lo = spread(band["g_hi"]()), spread(band["g_lo"]())
        v_hi = band["v_hi"]()
        dbuf[...] = dot(g_hi, v_hi, LAST) + dot(g_lo, v_hi, LAST) + dot(g_hi, band["v_lo"](), LAST)

    def softmax(band, total):
        mask, own = band["mask"](), band["own"]()
        out = []
        for h in range(HEADS):
            at = slice(h * nq, (h + 1) * nq)
            s, dp = sbuf[at], dbuf[at]
            e = jnp.exp2(s) * mask
            r = 1.0 / (jnp.sum(e, axis=1, keepdims=True) + 1e-30)
            p = e * r
            ds = p * (dp - jnp.sum(p * dp, axis=1, keepdims=True))
            if own is None:
                out.append(total[h])
            else:
                out.append(total[h] + own * jnp.sum(ds * s, axis=1, keepdims=True))
            pbuf[at] = p.astype(BF16)
            dsbuf[at] = ds.astype(BF16)
        return out

    total = [jnp.zeros((nq, 1), F32) for _ in range(HEADS)]
    count = len(bands)
    scores(bands[0])
    for b in range(count + 1):
        if b > 0:
            bands[b - 1]["grads"](pbuf, dsbuf)
        if b < count:
            total = softmax(bands[b], total)
        if b + 1 < count:
            scores(bands[b + 1])
    return [jnp.sum(t, axis=0, keepdims=True) for t in total]


def own(
    scale_hbm,
    tok_ref,
    go_ref,
    wqkv_hbm,
    wout_hbm,
    sl_ref,
    wqkv_ref,
    wout_ref,
    k_ref,
    rk_ref,
    v_ref,
    q_ref,
    rq_ref,
    ga_ref,
    scale_ref,
    sems,
):
    copies = [
        pltpu.make_async_copy(scale_hbm, scale_ref, sems.at[0]),
        pltpu.make_async_copy(wqkv_hbm, wqkv_ref, sems.at[1]),
        pltpu.make_async_copy(wout_hbm, wout_ref, sems.at[2]),
    ]
    for c in copies:
        c.start()
    rows, cols, d = tok_ref.shape
    n = rows * cols
    heads, head_sum, _, _ = tools(d)
    for c in copies:
        c.wait()
    sl = jnp.zeros((1, d), F32)
    for h in range(HEADS):
        sl = jnp.where(heads[h], scale_ref[h], sl)
    sl_ref[...] = jnp.broadcast_to(sl, sl_ref.shape)
    qkv = dot(tok_ref[...].reshape(n, d), wqkv_ref[...])
    q_ref[...], rq_ref[...] = unit(qkv[:, :d], head_sum)
    k_ref[...], rk_ref[...] = unit(qkv[:, d : 2 * d], head_sum)
    v_ref[...] = qkv[:, 2 * d :]
    ga_ref[...] = dot(go_ref[...].reshape(n, d), wout_ref[...], LAST)


def inner(
    col_a,
    col_b,
    sl_ref,
    wqkv_ref,
    wout_ref,
    k_own,
    v_own,
    q_own,
    ga_own,
    khi,
    klo,
    vhi,
    vlo,
    qe_ref,
    ge_ref,
    gq,
    att,
    gk,
    gv,
    psum,
    ts,
    gs,
    side,
    kg,
    vg,
    qs,
    gas,
    qg,
    gg,
    qhi,
    qlo,
    ghi,
    glo,
    sbuf,
    dbuf,
    pbuf,
    dsbuf,
):
    rows, wide, d = kg.shape
    _, qwide, _ = qg.shape
    cols = k_own.shape[0] // rows
    reach2 = 2 * REACH
    q0 = 8 - REACH - 2
    own_q = 8 - q0
    heads, head_sum, spread, gather = tools(d)
    sl = sl_ref[0:1]

    ts[...] = jnp.zeros_like(ts)
    gs[...] = jnp.zeros_like(gs)
    even_col = lax.axis_index("col") % 2 == 0
    _, _, _, tok_at, go_at = piece_layout(rows)
    has_left, has_right = has_neighbours("col")
    for i, even, valid, at_k, at_g in (
        (0, ~even_col, has_left, 8 - reach2, 8 - REACH),
        (1, even_col, has_right, 0, 0),
    ):
        x = jnp.where(even, col_a[...].astype(F32), col_b[...].astype(F32))
        side[...] = jnp.where(valid, x, jnp.zeros_like(x))
        for r in range(rows):
            ts[i, r, at_k : at_k + reach2, :] = side[tok_at[r] : tok_at[r] + reach2]
            gs[i, r, at_g : at_g + REACH, :] = side[go_at[r] : go_at[r] + REACH]
    m = 2 * rows * 8
    qkv = dot(ts[...].reshape(m, d).astype(BF16), wqkv_ref[...])
    q, _ = unit(qkv[:, :d], head_sum)
    k, _ = unit(qkv[:, d : 2 * d], head_sum)
    qs[...] = q.reshape(2, rows, 8, d)
    gas[...] = dot(gs[...].reshape(m, d).astype(BF16), wout_ref[...], LAST).reshape(2, rows, 8, d)
    for grid, sides, mine in ((kg, k, k_own), (vg, qkv[:, 2 * d :], v_own)):
        grid[:, 0:8, :] = sides[: m // 2].reshape(rows, 8, d)
        grid[:, 8 : 8 + cols, :] = mine[...].reshape(rows, cols, d)
        grid[:, 8 + cols : 16 + cols, :] = sides[m // 2 :].reshape(rows, 8, d)
        if wide > 16 + cols:
            grid[:, 16 + cols :, :] = jnp.zeros((rows, wide - 16 - cols, d), F32)
    for grid, sides, mine in ((qg, qs, q_own), (gg, gas, ga_own)):
        grid[:, 0:own_q, :] = sides[0, :, q0:8, :]
        grid[:, own_q : own_q + cols, :] = mine[...].reshape(rows, cols, d)
        grid[:, own_q + cols : qwide, :] = sides[1, :, 0 : qwide - own_q - cols, :]
    khi[...], klo[...] = split(kg[...].reshape(rows * wide, d))
    vhi[...], vlo[...] = split(vg[...].reshape(rows * wide, d))
    mid = (rows - reach2) * qwide
    middle = slice(REACH, rows - REACH)
    qhi[...], qlo[...] = split(qg[middle].reshape(mid, d) * (sl * LOG2E))
    ghi[...], glo[...] = split(gg[middle].reshape(mid, d))
    for edge, grid in ((qe_ref, qg), (ge_ref, gg)):
        edge[0:REACH] = grid[0:REACH]
        edge[REACH:] = grid[rows - REACH :]
    gk[...] = jnp.zeros_like(gk)
    gv[...] = jnp.zeros_like(gv)

    nq = 2 * qwide
    span = 2 + reach2
    near = near_mask(qwide, wide, cols)
    iq = lax.broadcasted_iota(jnp.int32, (nq, 1), 0) % qwide
    own_col = ((iq >= own_q) & (iq < own_q + cols)).astype(F32)

    def band(b):
        at = slice(b * nq, (b + 1) * nq)
        keys = slice(b * 2 * wide, b * 2 * wide + span * wide)

        def grads(pbuf, dsbuf):
            p, ds = pbuf[...], dsbuf[...]
            att[2 * b : 2 * b + 2] = gather(dot(p, vhi[keys])).reshape(2, qwide, d)
            gq[2 * b : 2 * b + 2] = gather(dot(ds, khi[keys])).reshape(2, qwide, d)
            eight = slice(2 * b, 2 * b + span)
            gk[eight] += dot(ds, spread(qhi[at]), FIRST).reshape(span, wide, d)
            gv[eight] += dot(p, spread(ghi[at]), FIRST).reshape(span, wide, d)

        return {
            "q_hi": lambda: qhi[at],
            "q_lo": lambda: qlo[at],
            "g_hi": lambda: ghi[at],
            "g_lo": lambda: glo[at],
            "k_hi": lambda: khi[keys],
            "k_lo": lambda: klo[keys],
            "v_hi": lambda: vhi[keys],
            "v_lo": lambda: vlo[keys],
            "mask": lambda: near,
            "own": lambda: own_col,
            "grads": grads,
        }

    bands = [band(b) for b in range((rows - reach2) // 2)]
    total = run_bands(bands, sbuf, dbuf, pbuf, dsbuf, nq, spread)
    lane = lax.broadcasted_iota(jnp.int32, psum.shape, 1)
    sums = jnp.zeros(psum.shape, F32)
    for h in range(HEADS):
        sums = jnp.where(lane == h, total[h], sums)
    psum[...] = sums


def outer(
    tok_ref,
    go_ref,
    row_a,
    row_b,
    sl_ref,
    wqkv_ref,
    wout_ref,
    khi_in,
    klo_in,
    vhi_in,
    vlo_in,
    k_own,
    rk_own,
    q_own,
    rq_own,
    qe_in,
    ge_in,
    gq_in,
    att_in,
    gk_in,
    gv_in,
    psum,
    grads_ref,
    kept_ref,
    sent_ref,
    tx,
    gx,
    ends,
    qe,
    ge,
    khi,
    klo,
    vhi,
    vlo,
    qhi,
    qlo,
    ghi,
    glo,
    sbuf,
    dbuf,
    pbuf,
    dsbuf,
    gq,
    att,
    gk,
    gv,
):
    rows, cols, d = tok_ref.shape
    _, wide, _ = tx.shape
    _, qwide, _ = gx.shape
    reach2 = 2 * REACH
    q0 = 8 - REACH - 2
    own_q = 8 - q0
    n_rows = rows * lax.axis_size(ROW_AXES)
    row_first = lax.axis_index(ROW_AXES) * rows
    heads, head_sum, spread, gather = tools(d)
    sl = sl_ref[0:1]

    left_k, right_k = 8 - reach2, 8 + cols
    left_q, right_q = own_q - REACH, own_q + cols
    tx[:, 0:8, :] = jnp.zeros((2 * reach2, 8, d), F32)
    tx[:, 8 + cols : wide, :] = jnp.zeros((2 * reach2, wide - 8 - cols, d), F32)
    gx[:, 0:8, :] = jnp.zeros((reach2, 8, d), F32)
    even_row = lax.axis_index("rowlo") % 2 == 0
    even_col = lax.axis_index("col") % 2 == 0
    seg = piece_layout(rows)[0]
    cut = reach2 * cols
    end = cut + REACH * cols
    has_above, has_below = has_neighbours(ROW_AXES)
    has_left, has_right = has_neighbours("col")
    for even, valid, row_k, row_q in (
        (~even_row, has_above, 0, 0),
        (even_row, has_below, reach2, REACH),
    ):
        x = jnp.where(even, row_a[...].astype(F32), row_b[...].astype(F32))
        ends[...] = jnp.where(valid, x, jnp.zeros_like(x))
        tx[row_k : row_k + reach2, 8 : 8 + cols, :] = ends[0:cut].reshape(reach2, cols, d)
        gx[row_q : row_q + REACH, own_q : own_q + cols, :] = ends[cut:end].reshape(REACH, cols, d)
        first, last = ends[end : end + seg], ends[end + seg : end + 2 * seg]
        none = jnp.zeros_like(first)
        ends[end : end + seg] = jnp.where(has_left, jnp.where(even_col, last, first), none)
        ends[end + seg : end + 2 * seg] = jnp.where(has_right, jnp.where(even_col, first, last), none)
        for base, at_k, at_q in ((end, left_k, left_q), (end + seg, right_k, right_q)):
            for r in range(reach2):
                at = base + r * reach2
                tx[row_k + r, at_k : at_k + reach2, :] = ends[at : at + reach2]
            for r in range(REACH):
                at = base + reach2 * reach2 + r * REACH
                gx[row_q + r, at_q : at_q + REACH, :] = ends[at : at + REACH]

    m = reach2 * wide
    x = tx[...].reshape(2 * m, d).astype(BF16)
    kv = dot(x, wqkv_ref[:, d:])
    k, _ = unit(kv[:, :d], head_sum)
    for hi, lo, hi_in, lo_in, fresh in (
        (khi, klo, khi_in, klo_in, k),
        (vhi, vlo, vhi_in, vlo_in, kv[:, d:]),
    ):
        fresh_hi, fresh_lo = split(fresh)
        hi[0:m], lo[0:m] = fresh_hi[0:m], fresh_lo[0:m]
        hi[3 * m :], lo[3 * m :] = fresh_hi[m:], fresh_lo[m:]
        own_end = rows * wide
        for to, source in ((hi, hi_in), (lo, lo_in)):
            to[m : 2 * m] = source[0:m]
            to[2 * m : 3 * m] = source[own_end - m : own_end]
    x = tx[REACH : 3 * REACH, q0 : q0 + qwide, :].reshape(reach2 * qwide, d).astype(BF16)
    q, _ = unit(dot(x, wqkv_ref[:, :d]), head_sum)
    q = q.reshape(reach2, qwide, d)
    g = dot(gx[...].reshape(reach2 * qwide, d).astype(BF16), wout_ref[...], LAST)
    g = g.reshape(reach2, qwide, d)
    qe[0:REACH], qe[3 * REACH :] = q[0:REACH], q[REACH:]
    ge[0:REACH], ge[3 * REACH :] = g[0:REACH], g[REACH:]
    qe[REACH : 3 * REACH] = qe_in[...]
    ge[REACH : 3 * REACH] = ge_in[...]
    flat = 2 * reach2 * qwide
    qhi[...], qlo[...] = split(qe[...].reshape(flat, d) * (sl * LOG2E))
    ghi[...], glo[...] = split(ge[...].reshape(flat, d))
    gk[...] = gk_in[...]
    gv[...] = gv_in[...]

    nq = 2 * qwide
    span = 2 + reach2
    nk = span * wide
    near = near_mask(qwide, wide, cols)
    jr = lax.broadcasted_iota(jnp.int32, (1, nk), 1) // wide
    iq = lax.broadcasted_iota(jnp.int32, (nq, 1), 0)
    own_col = (iq % qwide >= own_q) & (iq % qwide < own_q + cols)

    def band(b):
        top = b < REACH
        first = 2 * b if top else rows + 2 * (b - REACH)
        at = slice(b * nq, (b + 1) * nq)
        key_at = 2 * b if top else 2 * reach2 + 2 * (b - REACH)
        keys = slice(key_at * wide, key_at * wide + nk)
        mine = first + 1 >= REACH and first < rows + REACH
        skip = reach2 - first if top else 0
        count = span - skip if top else reach2 - 2 * (b - REACH)
        to = 0 if top else rows - count
        part = slice(skip * wide, (skip + count) * wide)

        def mask():
            key_row = jr + (row_first - reach2 + first)
            return near * ((key_row >= 0) & (key_row < n_rows)).astype(F32)

        def own():
            if not mine:
                return None
            q_row = iq // qwide + first
            return (own_col & (q_row >= REACH) & (q_row < REACH + rows)).astype(F32)

        def grads(pbuf, dsbuf):
            if mine:
                att[2 * b : 2 * b + 2] = gather(dot(pbuf[...], vhi[keys])).reshape(2, qwide, d)
                gq[2 * b : 2 * b + 2] = gather(dot(dsbuf[...], khi[keys])).reshape(2, qwide, d)
            p, ds = pbuf[:, part], dsbuf[:, part]
            own_rows = slice(to, to + count)
            gk[own_rows] += dot(ds, spread(qhi[at]), FIRST).reshape(count, wide, d)
            gv[own_rows] += dot(p, spread(ghi[at]), FIRST).reshape(count, wide, d)

        return {
            "q_hi": lambda: qhi[at],
            "q_lo": lambda: qlo[at],
            "g_hi": lambda: ghi[at],
            "g_lo": lambda: glo[at],
            "k_hi": lambda: khi[keys],
            "k_lo": lambda: klo[keys],
            "v_hi": lambda: vhi[keys],
            "v_lo": lambda: vlo[keys],
            "mask": mask,
            "own": own,
            "grads": grads,
        }

    total = run_bands([band(b) for b in range(reach2)], sbuf, dbuf, pbuf, dsbuf, nq, spread)

    n = rows * cols
    key_cols = slice(8, 8 + cols)
    query_cols = slice(own_q, own_q + cols)

    def own_queries(edge, middle):
        parts = [
            edge[REACH:reach2, query_cols, :],
            middle[:, query_cols, :],
            edge[reach2 : 3 * REACH, query_cols, :],
        ]
        return jnp.concatenate(parts, axis=0).reshape(n, d)

    def unit_back(u, r, g):
        return r * (g - u * head_sum(u * g))

    g_q = unit_back(q_own[...], rq_own[...], own_queries(gq, gq_in) * sl)
    g_k = unit_back(k_own[...], rk_own[...], gk[:, key_cols, :].reshape(n, d) * (1.0 / LOG2E))
    g_v = gv[:, key_cols, :].reshape(n, d)
    grads = jnp.concatenate([g_q.astype(BF16), g_k.astype(BF16), g_v.astype(BF16)], axis=1)
    grads_ref[...] = grads
    wq = dot(tok_ref[...].reshape(n, d), grads, FIRST)
    wo = dot(own_queries(att, att_in).astype(BF16), go_ref[...].reshape(n, d), FIRST)
    half = d // 2
    lane = lax.broadcasted_iota(jnp.int32, (8, 4 * d), 1)
    kept, sent = jnp.zeros((8, 4 * d), F32), jnp.zeros((8, 4 * d), F32)
    for h in range(HEADS):
        at = h * (d // HEADS)
        t = (total[h] + psum[0:1, h : h + 1]) / (sl[:, at : at + 1] * LOG2E)
        hi = t.astype(BF16).astype(F32)
        kept = jnp.where(lane == h, t, kept)
        sent = jnp.where(lane == h, hi, sent)
        sent = jnp.where(lane == HEADS + h, t - hi, sent)
    first = lax.axis_index("rowlo") == 0
    for x, at in ((wq, slice(0, 3 * d)), (wo, slice(3 * d, 4 * d))):
        kept_ref[0:half, at] = jnp.where(first, x[:half], x[half:])
        sent_ref[0:half, at] = jnp.where(first, x[half:], x[:half]).astype(BF16)
    kept_ref[half:, :] = kept
    sent_ref[half:, :] = sent.astype(BF16)


def sizes(rows, cols):
    wide = -(-(cols + 4 * REACH + 2) // 16) * 16
    qwide = -(-(cols + 2 * REACH + 2) // 8) * 8
    return wide, qwide


def call(body, out_shape, in_specs, scratch, flops):
    vmem = pl.BlockSpec(memory_space=pltpu.VMEM)
    return pl.pallas_call(
        body,
        out_shape=out_shape,
        in_specs=in_specs,
        out_specs=(vmem,) * len(out_shape),
        scratch_shapes=scratch,
        compiler_params=pltpu.CompilerParams(vmem_limit_bytes=24 * 1024 * 1024),
        cost_estimate=pl.CostEstimate(
            flops=flops, bytes_accessed=4_000_000, transcendentals=300_000
        ),
    )


def own_parts(scale, tokens, grad_out, w_qkv, w_out):
    rows, cols, d = tokens.shape
    f32 = lambda *s: jax.ShapeDtypeStruct(s, F32)
    bf16 = lambda *s: jax.ShapeDtypeStruct(s, BF16)
    out_shape = (f32(8, d), bf16(*w_qkv.shape), bf16(*w_out.shape)) + (f32(rows * cols, d),) * 6
    vmem = pl.BlockSpec(memory_space=pltpu.VMEM)
    hbm = pl.BlockSpec(memory_space=pltpu.HBM)
    scratch = [pltpu.SMEM((HEADS,), F32), pltpu.SemaphoreType.DMA((3,))]
    return call(own, out_shape, [hbm, vmem, vmem, hbm, hbm], scratch, 500_000_000)(
        pin(scale), tokens, grad_out, pin(w_qkv), pin(w_out)
    )


def inner_grads(rows, cols, col_a, col_b, *parts):
    d = col_a.shape[1]
    wide, qwide = sizes(rows, cols)
    f32 = lambda *s: jax.ShapeDtypeStruct(s, F32)
    middle = rows - 2 * REACH
    nk = (2 + 2 * REACH) * wide
    key = jax.ShapeDtypeStruct((rows * wide, d), BF16)
    edge, mid, grid = f32(2 * REACH, qwide, d), f32(middle, qwide, d), f32(rows, wide, d)
    out_shape = (key,) * 4 + (edge, edge, mid, mid, grid, grid, f32(8, 128))
    vmem = pl.BlockSpec(memory_space=pltpu.VMEM)
    tile = lambda dt: pltpu.VMEM((HEADS * 2 * qwide, nk), dt)
    sides = pltpu.VMEM((2, rows, 8, d), F32)
    scratch = [sides, sides, pltpu.VMEM(col_a.shape, F32)]
    scratch += [pltpu.VMEM((rows, wide, d), F32)] * 2 + [sides, sides]
    scratch += [pltpu.VMEM((rows, qwide, d), F32)] * 2
    scratch += [pltpu.VMEM((middle * qwide, d), BF16)] * 4
    scratch += [tile(F32), tile(F32), tile(BF16), tile(BF16)]
    args = (col_a, col_b) + parts
    return call(inner, out_shape, [vmem] * len(args), scratch, 3_000_000_000)(*args)


def outer_grads(tokens, grad_out, row_a, row_b, state):
    rows, cols, d = tokens.shape
    wide, qwide = sizes(rows, cols)
    nk = (2 + 2 * REACH) * wide
    out_shape = (
        jax.ShapeDtypeStruct((rows * cols, 3 * d), BF16),
        jax.ShapeDtypeStruct((d // 2 + 8, 4 * d), F32),
        jax.ShapeDtypeStruct((d // 2 + 8, 4 * d), BF16),
    )
    edge = pltpu.VMEM((4 * REACH, qwide, d), F32)
    tile = lambda dt: pltpu.VMEM((HEADS * 2 * qwide, nk), dt)
    scratch = [
        pltpu.VMEM((4 * REACH, wide, d), F32),
        pltpu.VMEM((2 * REACH, qwide, d), F32),
        pltpu.VMEM(row_a.shape, F32),
        edge,
        edge,
    ]
    scratch += [pltpu.VMEM((8 * REACH * wide, d), BF16)] * 4
    scratch += [pltpu.VMEM((4 * REACH * qwide, d), BF16)] * 4
    scratch += [tile(F32), tile(F32), tile(BF16), tile(BF16), edge, edge]
    scratch += [pltpu.VMEM((rows, wide, d), F32)] * 2
    vmem = pl.BlockSpec(memory_space=pltpu.VMEM)
    args = (tokens, grad_out, row_a, row_b) + tuple(state)
    return call(outer, out_shape, [vmem] * len(args), scratch, 3_000_000_000)(*args)


def put_half(piece_ref, *refs, other):
    *_, wqkv_hbm, wout_hbm, wqkv, wout, sems = refs
    half = piece_ref.shape[0]
    width = wqkv.shape[1]
    lo = lax.axis_index("rowlo")
    lo = 1 - lo if other else lo
    rows = pl.ds(pl.multiple_of(lo * half, half), half)
    wqkv[...] = piece_ref[:, :width].astype(F32)
    first = pltpu.make_async_copy(wqkv, wqkv_hbm.at[rows], sems.at[0])
    first.start()
    wout[...] = piece_ref[:, width:].astype(F32)
    second = pltpu.make_async_copy(wout, wout_hbm.at[rows], sems.at[1])
    second.start()
    first.wait()
    second.wait()


def put(piece, into, other):
    half, width = piece.shape
    d = 2 * half
    hbm = pl.BlockSpec(memory_space=pltpu.HBM)
    return pl.pallas_call(
        functools.partial(put_half, other=other),
        out_shape=(
            jax.ShapeDtypeStruct((d, width - d), F32),
            jax.ShapeDtypeStruct((d, d), F32),
        ),
        in_specs=[pl.BlockSpec(memory_space=pltpu.VMEM)] + [hbm] * len(into),
        out_specs=(hbm, hbm),
        scratch_shapes=[
            pltpu.VMEM((half, width - d), F32),
            pltpu.VMEM((half, d), F32),
            pltpu.SemaphoreType.DMA((2,)),
        ],
        input_output_aliases={1: 0, 2: 1} if into else {},
        compiler_params=pltpu.CompilerParams(vmem_limit_bytes=8 * 1024 * 1024),
        cost_estimate=pl.CostEstimate(flops=0, bytes_accessed=2_000_000, transcendentals=0),
    )(piece, *into)


def swap_pairs(x, axis, first):
    shape = (lax.axis_size(ROW_AXES), lax.axis_size("col"))
    pairs = []
    for r in range(shape[0]):
        for c in range(shape[1]):
            at = [r, c]
            to = at[axis] + (1 if (at[axis] - first) % 2 == 0 else -1)
            if 0 <= to < shape[axis]:
                at[axis] = to
            else:
                at[1 - axis] ^= 1
            pairs.append((r * shape[1] + c, at[0] * shape[1] + at[1]))
    return lax.ppermute(x, ROW_AXES + ("col",), pairs)


def shards(tokens, grad_out, w_qkv, w_out, scale):
    rows, cols, d = tokens.shape
    tokens, grad_out, col_a, col_b, row_a, row_b = packed(tokens, grad_out)
    col_b = swap_pairs(col_b, 1, 1)
    col_a = swap_pairs(col_a, 1, 0)
    seg, last, _, _, _ = piece_layout(rows)
    odd = lax.axis_index("rowlo") % 2

    def with_corners(row, at):
        return jnp.concatenate(
            [row] + [lax.dynamic_slice_in_dim(c, at, seg, 0) for c in (col_a, col_b)], axis=0
        )

    row_b = swap_pairs(with_corners(row_b, odd * last), 0, 1)
    row_a = swap_pairs(with_corners(row_a, (1 - odd) * last), 0, 0)

    sl, wqkv_in, wout_in, k, rk, v, q, rq, ga = own_parts(scale, tokens, grad_out, w_qkv, w_out)
    state = inner_grads(rows, cols, col_a, col_b, sl, wqkv_in, wout_in, k, v, q, ga)
    state = (sl, wqkv_in, wout_in) + state[:4] + (k, rk, q, rq) + state[4:]
    grads, kept, sent = outer_grads(tokens, grad_out, row_a, row_b, state)
    grad_tokens = dot(grads, w_qkv, LAST).astype(BF16).reshape(rows, cols, d)

    swap = [(0, 1), (1, 0)]
    kept = kept + lax.ppermute(sent, "rowlo", swap).astype(F32)
    kept, grad_tokens = lax.optimization_barrier((kept, grad_tokens))
    half = d // 2
    n = lax.axis_size(SPREAD_AXES)
    pieces = half // n if half % n == 0 else 1
    part = kept[:half].reshape(n, pieces, -1)
    sums = kept[half, :HEADS] + kept[half, HEADS : 2 * HEADS]
    sums_hi = lax.reduce_precision(sums, 8, 7)
    sums = jnp.concatenate([sums_hi, sums - sums_hi, jnp.zeros((128 - 2 * HEADS,), F32)])
    part = jnp.concatenate(
        [part.astype(BF16), jnp.broadcast_to(sums.astype(BF16), (n, pieces, 128))], axis=2
    )
    part = lax.all_to_all(part, SPREAD_AXES, 0, 0, tiled=True).astype(F32)
    part = jnp.sum(part, axis=0)
    sums = part[0, -128:]
    grad_scale = sums[:HEADS] + sums[HEADS : 2 * HEADS]
    part = part[:, :-128].astype(BF16)
    mine = lax.all_to_all(
        jnp.broadcast_to(part[None], (n,) + part.shape), SPREAD_AXES, 0, 0, tiled=True
    ).reshape(half, 4 * d)
    other = lax.ppermute(mine, "rowlo", swap)
    grad_wqkv, grad_wout = put(other, put(mine, (), False), True)
    return grad_tokens, grad_wqkv, grad_wout, grad_scale


def solution(mesh):
    n_row, n_col = mesh.devices.shape
    fine = Mesh(mesh.devices.reshape(n_row // 2, 2, n_col), ("rowhi", "rowlo", "col"))
    block = P(ROW_AXES, "col", None)
    return jax.shard_map(
        shards,
        mesh=fine,
        in_specs=(block, block, P(), P(), P()),
        out_specs=(block, P(), P(), P()),
        check_vma=False,
    )
```

```python
import functools
import math

import jax
import jax.numpy as jnp
from jax import lax
from jax.experimental import pallas as pl
from jax.experimental.pallas import tpu as pltpu
from jax.sharding import Mesh
from jax.sharding import PartitionSpec as P

HEADS = 4
REACH = 3
F32 = jnp.float32
BF16 = jnp.bfloat16
LAST = (((1,), (1,)), ((), ()))
FIRST = (((0,), (0,)), ((), ()))
LOG2E = math.log2(math.e)
ROW_AXES = ("rowhi", "rowlo")
SPREAD_AXES = ("rowhi", "col")


def dot(a, b, dims=(((1,), (0,)), ((), ()))):
    return lax.dot_general(a, b, dims, preferred_element_type=F32)


def split(x):
    hi = x.astype(BF16)
    return hi, (x - hi.astype(F32)).astype(BF16)


def pin(x):
    return pltpu.with_memory_space_constraint(x, pltpu.HBM)


def piece_layout(rows):
    wide = 2 * REACH
    seg = -(-(wide * wide + REACH * REACH) // 16) * 16
    mid_tok = (rows - 2 * wide) * wide
    mid = -(-(mid_tok + (rows - 2 * REACH) * REACH) // 8) * 8
    tok, go = [], []
    for r in range(rows):
        if r < wide:
            tok.append(r * wide)
        elif r < rows - wide:
            tok.append(seg + (r - wide) * wide)
        else:
            tok.append(seg + mid + (r - rows + wide) * wide)
        if r < REACH:
            go.append(wide * wide + r * REACH)
        elif r < rows - REACH:
            go.append(seg + mid_tok + (r - REACH) * REACH)
        else:
            go.append(seg + mid + wide * wide + (r - rows + REACH) * REACH)
    return seg, seg + mid, 2 * seg + mid, tok, go


def pack(tok_hbm, go_hbm, tok_ref, go_ref, col_a, col_b, row_a, row_b, tf, gf, first, last, sems):
    rows, cols, d = tok_ref.shape
    copies = [
        pltpu.make_async_copy(tok_hbm, tok_ref, sems.at[0]),
        pltpu.make_async_copy(go_hbm, go_ref, sems.at[1]),
    ]
    for c in copies:
        c.start()
    wide = 2 * REACH
    _, _, _, tok_at, go_at = piece_layout(rows)
    even_row = lax.axis_index("rowlo") % 2 == 0
    even_col = lax.axis_index("col") % 2 == 0
    first[...] = jnp.zeros_like(first)
    last[...] = jnp.zeros_like(last)
    for c in copies:
        c.wait()
    tf[...] = tok_ref[...].astype(F32)
    gf[...] = go_ref[...].astype(F32)
    for r in range(rows):
        first[tok_at[r] : tok_at[r] + wide] = tf[r, 0:wide, :]
        last[tok_at[r] : tok_at[r] + wide] = tf[r, cols - wide : cols, :]
        first[go_at[r] : go_at[r] + REACH] = gf[r, 0:REACH, :]
        last[go_at[r] : go_at[r] + REACH] = gf[r, cols - REACH : cols, :]
    lo, hi = first[...], last[...]
    col_a[...] = jnp.where(even_col, hi, lo).astype(BF16)
    col_b[...] = jnp.where(even_col, lo, hi).astype(BF16)
    cut = wide * cols
    end = cut + REACH * cols
    lo = tf[0:wide].reshape(cut, d)
    hi = tf[rows - wide : rows].reshape(cut, d)
    row_a[0:cut] = jnp.where(even_row, hi, lo).astype(BF16)
    row_b[0:cut] = jnp.where(even_row, lo, hi).astype(BF16)
    lo = gf[0:REACH].reshape(end - cut, d)
    hi = gf[rows - REACH : rows].reshape(end - cut, d)
    row_a[cut:end] = jnp.where(even_row, hi, lo).astype(BF16)
    row_b[cut:end] = jnp.where(even_row, lo, hi).astype(BF16)


def packed(tokens, grad_out):
    rows, cols, d = tokens.shape
    size = piece_layout(rows)[2]
    vmem = pl.BlockSpec(memory_space=pltpu.VMEM)
    col = jax.ShapeDtypeStruct((size, d), BF16)
    row = jax.ShapeDtypeStruct((3 * REACH * cols, d), BF16)
    whole = jax.ShapeDtypeStruct((rows, cols, d), BF16)
    block = pltpu.VMEM((rows, cols, d), F32)
    return pl.pallas_call(
        pack,
        out_shape=(whole, whole, col, col, row, row),
        in_specs=[pl.BlockSpec(memory_space=pltpu.HBM)] * 2,
        out_specs=(vmem,) * 6,
        scratch_shapes=[
            block,
            block,
            pltpu.VMEM((size, d), F32),
            pltpu.VMEM((size, d), F32),
            pltpu.SemaphoreType.DMA((2,)),
        ],
        compiler_params=pltpu.CompilerParams(vmem_limit_bytes=8 * 1024 * 1024),
        cost_estimate=pl.CostEstimate(flops=0, bytes_accessed=1_000_000, transcendentals=0),
    )(pin(tokens), pin(grad_out))


def unit(x, head_sum):
    r = lax.rsqrt(head_sum(x * x) + 1e-06)
    return x * r, r


def tools(d):
    per = d // HEADS
    lane_head = lax.broadcasted_iota(jnp.int32, (1, d), 1) // per
    heads = [lane_head == h for h in range(HEADS)]
    ones = (
        lax.broadcasted_iota(jnp.int32, (d, d), 0) // per
        == lax.broadcasted_iota(jnp.int32, (d, d), 1) // per
    ).astype(BF16)

    def head_sum(x):
        return dot(x.astype(BF16), ones)

    def spread(x):
        zero = jnp.zeros_like(x)
        return jnp.concatenate([jnp.where(m, x, zero) for m in heads], axis=0)

    def gather(x):
        n = x.shape[0] // HEADS
        out = x[0:n]
        for h in range(1, HEADS):
            out = jnp.where(heads[h], x[h * n : (h + 1) * n], out)
        return out

    return heads, head_sum, spread, gather


def has_neighbours(axis):
    at = lax.axis_index(axis)
    return at > 0, at < lax.axis_size(axis) - 1


def near_mask(qwide, wide, cols):
    nq, nk = 2 * qwide, (2 + 2 * REACH) * wide
    i = lax.broadcasted_iota(jnp.int32, (nq, nk), 0)
    j = lax.broadcasted_iota(jnp.int32, (nq, nk), 1)
    dr = j // wide - i // qwide
    dc = j % wide - i % qwide
    key_col = j % wide + (lax.axis_index("col") * cols - 8)
    near = (dr >= 0) & (dr <= 2 * REACH) & (dc >= 0) & (dc <= 2 * REACH)
    near = near & (key_col >= 0) & (key_col < cols * lax.axis_size("col"))
    return near.astype(F32)


def run_bands(bands, sbuf, dbuf, pbuf, dsbuf, nq, spread):
    def scores(band):
        q_hi, q_lo = spread(band["q_hi"]()), spread(band["q_lo"]())
        k_hi = band["k_hi"]()
        sbuf[...] = dot(q_hi, k_hi, LAST) + dot(q_lo, k_hi, LAST) + dot(q_hi, band["k_lo"](), LAST)
        g_hi, g_lo = spread(band["g_hi"]()), spread(band["g_lo"]())
        v_hi = band["v_hi"]()
        dbuf[...] = dot(g_hi, v_hi, LAST) + dot(g_lo, v_hi, LAST) + dot(g_hi, band["v_lo"](), LAST)

    def softmax(band, total):
        mask, own = band["mask"](), band["own"]()
        out = []
        for h in range(HEADS):
            at = slice(h * nq, (h + 1) * nq)
            s, dp = sbuf[at], dbuf[at]
            e = jnp.exp2(s) * mask
            r = 1.0 / (jnp.sum(e, axis=1, keepdims=True) + 1e-30)
            p = e * r
            ds = p * (dp - jnp.sum(p * dp, axis=1, keepdims=True))
            if own is None:
                out.append(total[h])
            else:
                out.append(total[h] + own * jnp.sum(ds * s, axis=1, keepdims=True))
            pbuf[at] = p.astype(BF16)
            dsbuf[at] = ds.astype(BF16)
        return out

    total = [jnp.zeros((nq, 1), F32) for _ in range(HEADS)]
    count = len(bands)
    scores(bands[0])
    for b in range(count + 1):
        if b > 0:
            bands[b - 1]["grads"](pbuf, dsbuf)
        if b < count:
            total = softmax(bands[b], total)
        if b + 1 < count:
            scores(bands[b + 1])
    return [jnp.sum(t, axis=0, keepdims=True) for t in total]


def own(
    scale_hbm,
    tok_ref,
    go_ref,
    wqkv_hbm,
    wout_hbm,
    sl_ref,
    wqkv_ref,
    wout_ref,
    k_ref,
    rk_ref,
    v_ref,
    q_ref,
    rq_ref,
    ga_ref,
    scale_ref,
    sems,
):
    copies = [
        pltpu.make_async_copy(scale_hbm, scale_ref, sems.at[0]),
        pltpu.make_async_copy(wqkv_hbm, wqkv_ref, sems.at[1]),
        pltpu.make_async_copy(wout_hbm, wout_ref, sems.at[2]),
    ]
    for c in copies:
        c.start()
    rows, cols, d = tok_ref.shape
    n = rows * cols
    heads, head_sum, _, _ = tools(d)
    for c in copies:
        c.wait()
    sl = jnp.zeros((1, d), F32)
    for h in range(HEADS):
        sl = jnp.where(heads[h], scale_ref[h], sl)
    sl_ref[...] = jnp.broadcast_to(sl, sl_ref.shape)
    qkv = dot(tok_ref[...].reshape(n, d), wqkv_ref[...])
    q_ref[...], rq_ref[...] = unit(qkv[:, :d], head_sum)
    k_ref[...], rk_ref[...] = unit(qkv[:, d : 2 * d], head_sum)
    v_ref[...] = qkv[:, 2 * d :]
    ga_ref[...] = dot(go_ref[...].reshape(n, d), wout_ref[...], LAST)


def inner(
    col_a,
    col_b,
    sl_ref,
    wqkv_ref,
    wout_ref,
    k_own,
    v_own,
    q_own,
    ga_own,
    khi,
    klo,
    vhi,
    vlo,
    qe_ref,
    ge_ref,
    gq,
    att,
    gk,
    gv,
    psum,
    ts,
    gs,
    side,
    kg,
    vg,
    qs,
    gas,
    qg,
    gg,
    qhi,
    qlo,
    ghi,
    glo,
    sbuf,
    dbuf,
    pbuf,
    dsbuf,
):
    rows, wide, d = kg.shape
    _, qwide, _ = qg.shape
    cols = k_own.shape[0] // rows
    reach2 = 2 * REACH
    q0 = 8 - REACH - 2
    own_q = 8 - q0
    heads, head_sum, spread, gather = tools(d)
    sl = sl_ref[0:1]

    ts[...] = jnp.zeros_like(ts)
    gs[...] = jnp.zeros_like(gs)
    even_col = lax.axis_index("col") % 2 == 0
    _, _, _, tok_at, go_at = piece_layout(rows)
    has_left, has_right = has_neighbours("col")
    for i, even, valid, at_k, at_g in (
        (0, ~even_col, has_left, 8 - reach2, 8 - REACH),
        (1, even_col, has_right, 0, 0),
    ):
        x = jnp.where(even, col_a[...].astype(F32), col_b[...].astype(F32))
        side[...] = jnp.where(valid, x, jnp.zeros_like(x))
        for r in range(rows):
            ts[i, r, at_k : at_k + reach2, :] = side[tok_at[r] : tok_at[r] + reach2]
            gs[i, r, at_g : at_g + REACH, :] = side[go_at[r] : go_at[r] + REACH]
    m = 2 * rows * 8
    qkv = dot(ts[...].reshape(m, d).astype(BF16), wqkv_ref[...])
    q, _ = unit(qkv[:, :d], head_sum)
    k, _ = unit(qkv[:, d : 2 * d], head_sum)
    qs[...] = q.reshape(2, rows, 8, d)
    gas[...] = dot(gs[...].reshape(m, d).astype(BF16), wout_ref[...], LAST).reshape(2, rows, 8, d)
    for grid, sides, mine in ((kg, k, k_own), (vg, qkv[:, 2 * d :], v_own)):
        grid[:, 0:8, :] = sides[: m // 2].reshape(rows, 8, d)
        grid[:, 8 : 8 + cols, :] = mine[...].reshape(rows, cols, d)
        grid[:, 8 + cols : 16 + cols, :] = sides[m // 2 :].reshape(rows, 8, d)
        if wide > 16 + cols:
            grid[:, 16 + cols :, :] = jnp.zeros((rows, wide - 16 - cols, d), F32)
    for grid, sides, mine in ((qg, qs, q_own), (gg, gas, ga_own)):
        grid[:, 0:own_q, :] = sides[0, :, q0:8, :]
        grid[:, own_q : own_q + cols, :] = mine[...].reshape(rows, cols, d)
        grid[:, own_q + cols : qwide, :] = sides[1, :, 0 : qwide - own_q - cols, :]
    khi[...], klo[...] = split(kg[...].reshape(rows * wide, d))
    vhi[...], vlo[...] = split(vg[...].reshape(rows * wide, d))
    mid = (rows - reach2) * qwide
    middle = slice(REACH, rows - REACH)
    qhi[...], qlo[...] = split(qg[middle].reshape(mid, d) * (sl * LOG2E))
    ghi[...], glo[...] = split(gg[middle].reshape(mid, d))
    for edge, grid in ((qe_ref, qg), (ge_ref, gg)):
        edge[0:REACH] = grid[0:REACH]
        edge[REACH:] = grid[rows - REACH :]
    gk[...] = jnp.zeros_like(gk)
    gv[...] = jnp.zeros_like(gv)

    nq = 2 * qwide
    span = 2 + reach2
    near = near_mask(qwide, wide, cols)
    iq = lax.broadcasted_iota(jnp.int32, (nq, 1), 0) % qwide
    own_col = ((iq >= own_q) & (iq < own_q + cols)).astype(F32)

    def band(b):
        at = slice(b * nq, (b + 1) * nq)
        keys = slice(b * 2 * wide, b * 2 * wide + span * wide)

        def grads(pbuf, dsbuf):
            p, ds = pbuf[...], dsbuf[...]
            att[2 * b : 2 * b + 2] = gather(dot(p, vhi[keys])).reshape(2, qwide, d)
            gq[2 * b : 2 * b + 2] = gather(dot(ds, khi[keys])).reshape(2, qwide, d)
            eight = slice(2 * b, 2 * b + span)
            gk[eight] += dot(ds, spread(qhi[at]), FIRST).reshape(span, wide, d)
            gv[eight] += dot(p, spread(ghi[at]), FIRST).reshape(span, wide, d)

        return {
            "q_hi": lambda: qhi[at],
            "q_lo": lambda: qlo[at],
            "g_hi": lambda: ghi[at],
            "g_lo": lambda: glo[at],
            "k_hi": lambda: khi[keys],
            "k_lo": lambda: klo[keys],
            "v_hi": lambda: vhi[keys],
            "v_lo": lambda: vlo[keys],
            "mask": lambda: near,
            "own": lambda: own_col,
            "grads": grads,
        }

    bands = [band(b) for b in range((rows - reach2) // 2)]
    total = run_bands(bands, sbuf, dbuf, pbuf, dsbuf, nq, spread)
    lane = lax.broadcasted_iota(jnp.int32, psum.shape, 1)
    sums = jnp.zeros(psum.shape, F32)
    for h in range(HEADS):
        sums = jnp.where(lane == h, total[h], sums)
    psum[...] = sums


def outer(
    tok_ref,
    go_ref,
    row_a,
    row_b,
    corner_a,
    corner_b,
    sl_ref,
    wqkv_ref,
    wout_ref,
    khi_in,
    klo_in,
    vhi_in,
    vlo_in,
    k_own,
    rk_own,
    q_own,
    rq_own,
    qe_in,
    ge_in,
    gq_in,
    att_in,
    gk_in,
    gv_in,
    psum,
    grads_ref,
    kept_ref,
    sent_ref,
    tx,
    gx,
    ends,
    qe,
    ge,
    khi,
    klo,
    vhi,
    vlo,
    qhi,
    qlo,
    ghi,
    glo,
    sbuf,
    dbuf,
    pbuf,
    dsbuf,
    gq,
    att,
    gk,
    gv,
):
    rows, cols, d = tok_ref.shape
    _, wide, _ = tx.shape
    _, qwide, _ = gx.shape
    reach2 = 2 * REACH
    q0 = 8 - REACH - 2
    own_q = 8 - q0
    n_rows = rows * lax.axis_size(ROW_AXES)
    row_first = lax.axis_index(ROW_AXES) * rows
    heads, head_sum, spread, gather = tools(d)
    sl = sl_ref[0:1]

    left_k, right_k = 8 - reach2, 8 + cols
    left_q, right_q = own_q - REACH, own_q + cols
    tx[:, 0:8, :] = jnp.zeros((2 * reach2, 8, d), F32)
    tx[:, 8 + cols : wide, :] = jnp.zeros((2 * reach2, wide - 8 - cols, d), F32)
    gx[:, 0:8, :] = jnp.zeros((reach2, 8, d), F32)
    even_row = lax.axis_index("rowlo") % 2 == 0
    even_col = lax.axis_index("col") % 2 == 0
    seg = piece_layout(rows)[0]
    cut = reach2 * cols
    end = cut + REACH * cols
    has_above, has_below = has_neighbours(ROW_AXES)
    has_left, has_right = has_neighbours("col")
    for even, valid, row_k, row_q in (
        (~even_row, has_above, 0, 0),
        (even_row, has_below, reach2, REACH),
    ):
        x = jnp.where(even, row_a[...].astype(F32), row_b[...].astype(F32))
        ends[0:end] = jnp.where(valid, x, jnp.zeros_like(x))
        x = jnp.where(even, corner_a[...].astype(F32), corner_b[...].astype(F32))
        ends[end : end + 2 * seg] = jnp.where(valid, x, jnp.zeros_like(x))
        tx[row_k : row_k + reach2, 8 : 8 + cols, :] = ends[0:cut].reshape(reach2, cols, d)
        gx[row_q : row_q + REACH, own_q : own_q + cols, :] = ends[cut:end].reshape(REACH, cols, d)
        first, last = ends[end : end + seg], ends[end + seg : end + 2 * seg]
        none = jnp.zeros_like(first)
        ends[end : end + seg] = jnp.where(has_left, jnp.where(even_col, last, first), none)
        ends[end + seg : end + 2 * seg] = jnp.where(has_right, jnp.where(even_col, first, last), none)
        for base, at_k, at_q in ((end, left_k, left_q), (end + seg, right_k, right_q)):
            for r in range(reach2):
                at = base + r * reach2
                tx[row_k + r, at_k : at_k + reach2, :] = ends[at : at + reach2]
            for r in range(REACH):
                at = base + reach2 * reach2 + r * REACH
                gx[row_q + r, at_q : at_q + REACH, :] = ends[at : at + REACH]

    m = reach2 * wide
    x = tx[...].reshape(2 * m, d).astype(BF16)
    kv = dot(x, wqkv_ref[:, d:])
    k, _ = unit(kv[:, :d], head_sum)
    for hi, lo, hi_in, lo_in, fresh in (
        (khi, klo, khi_in, klo_in, k),
        (vhi, vlo, vhi_in, vlo_in, kv[:, d:]),
    ):
        fresh_hi, fresh_lo = split(fresh)
        hi[0:m], lo[0:m] = fresh_hi[0:m], fresh_lo[0:m]
        hi[3 * m :], lo[3 * m :] = fresh_hi[m:], fresh_lo[m:]
        own_end = rows * wide
        for to, source in ((hi, hi_in), (lo, lo_in)):
            to[m : 2 * m] = source[0:m]
            to[2 * m : 3 * m] = source[own_end - m : own_end]
    x = tx[REACH : 3 * REACH, q0 : q0 + qwide, :].reshape(reach2 * qwide, d).astype(BF16)
    q, _ = unit(dot(x, wqkv_ref[:, :d]), head_sum)
    q = q.reshape(reach2, qwide, d)
    g = dot(gx[...].reshape(reach2 * qwide, d).astype(BF16), wout_ref[...], LAST)
    g = g.reshape(reach2, qwide, d)
    qe[0:REACH], qe[3 * REACH :] = q[0:REACH], q[REACH:]
    ge[0:REACH], ge[3 * REACH :] = g[0:REACH], g[REACH:]
    qe[REACH : 3 * REACH] = qe_in[...]
    ge[REACH : 3 * REACH] = ge_in[...]
    flat = 2 * reach2 * qwide
    qhi[...], qlo[...] = split(qe[...].reshape(flat, d) * (sl * LOG2E))
    ghi[...], glo[...] = split(ge[...].reshape(flat, d))
    gk[...] = gk_in[...]
    gv[...] = gv_in[...]

    nq = 2 * qwide
    span = 2 + reach2
    nk = span * wide
    near = near_mask(qwide, wide, cols)
    jr = lax.broadcasted_iota(jnp.int32, (1, nk), 1) // wide
    iq = lax.broadcasted_iota(jnp.int32, (nq, 1), 0)
    own_col = (iq % qwide >= own_q) & (iq % qwide < own_q + cols)

    def band(b):
        top = b < REACH
        first = 2 * b if top else rows + 2 * (b - REACH)
        at = slice(b * nq, (b + 1) * nq)
        key_at = 2 * b if top else 2 * reach2 + 2 * (b - REACH)
        keys = slice(key_at * wide, key_at * wide + nk)
        mine = first + 1 >= REACH and first < rows + REACH
        skip = reach2 - first if top else 0
        count = span - skip if top else reach2 - 2 * (b - REACH)
        to = 0 if top else rows - count
        part = slice(skip * wide, (skip + count) * wide)

        def mask():
            key_row = jr + (row_first - reach2 + first)
            return near * ((key_row >= 0) & (key_row < n_rows)).astype(F32)

        def own():
            if not mine:
                return None
            q_row = iq // qwide + first
            return (own_col & (q_row >= REACH) & (q_row < REACH + rows)).astype(F32)

        def grads(pbuf, dsbuf):
            if mine:
                att[2 * b : 2 * b + 2] = gather(dot(pbuf[...], vhi[keys])).reshape(2, qwide, d)
                gq[2 * b : 2 * b + 2] = gather(dot(dsbuf[...], khi[keys])).reshape(2, qwide, d)
            p, ds = pbuf[:, part], dsbuf[:, part]
            own_rows = slice(to, to + count)
            gk[own_rows] += dot(ds, spread(qhi[at]), FIRST).reshape(count, wide, d)
            gv[own_rows] += dot(p, spread(ghi[at]), FIRST).reshape(count, wide, d)

        return {
            "q_hi": lambda: qhi[at],
            "q_lo": lambda: qlo[at],
            "g_hi": lambda: ghi[at],
            "g_lo": lambda: glo[at],
            "k_hi": lambda: khi[keys],
            "k_lo": lambda: klo[keys],
            "v_hi": lambda: vhi[keys],
            "v_lo": lambda: vlo[keys],
            "mask": mask,
            "own": own,
            "grads": grads,
        }

    total = run_bands([band(b) for b in range(reach2)], sbuf, dbuf, pbuf, dsbuf, nq, spread)

    n = rows * cols
    key_cols = slice(8, 8 + cols)
    query_cols = slice(own_q, own_q + cols)

    def own_queries(edge, middle):
        parts = [
            edge[REACH:reach2, query_cols, :],
            middle[:, query_cols, :],
            edge[reach2 : 3 * REACH, query_cols, :],
        ]
        return jnp.concatenate(parts, axis=0).reshape(n, d)

    def unit_back(u, r, g):
        return r * (g - u * head_sum(u * g))

    g_q = unit_back(q_own[...], rq_own[...], own_queries(gq, gq_in) * sl)
    g_k = unit_back(k_own[...], rk_own[...], gk[:, key_cols, :].reshape(n, d) * (1.0 / LOG2E))
    g_v = gv[:, key_cols, :].reshape(n, d)
    grads = jnp.concatenate([g_q.astype(BF16), g_k.astype(BF16), g_v.astype(BF16)], axis=1)
    grads_ref[...] = grads
    wq = dot(tok_ref[...].reshape(n, d), grads, FIRST)
    wo = dot(own_queries(att, att_in).astype(BF16), go_ref[...].reshape(n, d), FIRST)
    half = d // 2
    lane = lax.broadcasted_iota(jnp.int32, (8, 4 * d), 1)
    kept, sent = jnp.zeros((8, 4 * d), F32), jnp.zeros((8, 4 * d), F32)
    for h in range(HEADS):
        at = h * (d // HEADS)
        t = (total[h] + psum[0:1, h : h + 1]) / (sl[:, at : at + 1] * LOG2E)
        hi = t.astype(BF16).astype(F32)
        kept = jnp.where(lane == h, t, kept)
        sent = jnp.where(lane == h, hi, sent)
        sent = jnp.where(lane == HEADS + h, t - hi, sent)
    first = lax.axis_index("rowlo") == 0
    for x, at in ((wq, slice(0, 3 * d)), (wo, slice(3 * d, 4 * d))):
        kept_ref[0:half, at] = jnp.where(first, x[:half], x[half:])
        sent_ref[0:half, at] = jnp.where(first, x[half:], x[:half]).astype(BF16)
    kept_ref[half:, :] = kept
    sent_ref[half:, :] = sent.astype(BF16)


def sizes(rows, cols):
    wide = -(-(cols + 4 * REACH + 2) // 16) * 16
    qwide = -(-(cols + 2 * REACH + 2) // 8) * 8
    return wide, qwide


def call(body, out_shape, in_specs, scratch, flops):
    vmem = pl.BlockSpec(memory_space=pltpu.VMEM)
    return pl.pallas_call(
        body,
        out_shape=out_shape,
        in_specs=in_specs,
        out_specs=(vmem,) * len(out_shape),
        scratch_shapes=scratch,
        compiler_params=pltpu.CompilerParams(vmem_limit_bytes=24 * 1024 * 1024),
        cost_estimate=pl.CostEstimate(
            flops=flops, bytes_accessed=4_000_000, transcendentals=300_000
        ),
    )


def own_parts(scale, tokens, grad_out, w_qkv, w_out):
    rows, cols, d = tokens.shape
    f32 = lambda *s: jax.ShapeDtypeStruct(s, F32)
    bf16 = lambda *s: jax.ShapeDtypeStruct(s, BF16)
    out_shape = (f32(8, d), bf16(*w_qkv.shape), bf16(*w_out.shape)) + (f32(rows * cols, d),) * 6
    vmem = pl.BlockSpec(memory_space=pltpu.VMEM)
    hbm = pl.BlockSpec(memory_space=pltpu.HBM)
    scratch = [pltpu.SMEM((HEADS,), F32), pltpu.SemaphoreType.DMA((3,))]
    return call(own, out_shape, [hbm, vmem, vmem, hbm, hbm], scratch, 500_000_000)(
        pin(scale), tokens, grad_out, pin(w_qkv), pin(w_out)
    )


def inner_grads(rows, cols, col_a, col_b, *parts):
    d = col_a.shape[1]
    wide, qwide = sizes(rows, cols)
    f32 = lambda *s: jax.ShapeDtypeStruct(s, F32)
    middle = rows - 2 * REACH
    nk = (2 + 2 * REACH) * wide
    key = jax.ShapeDtypeStruct((rows * wide, d), BF16)
    edge, mid, grid = f32(2 * REACH, qwide, d), f32(middle, qwide, d), f32(rows, wide, d)
    out_shape = (key,) * 4 + (edge, edge, mid, mid, grid, grid, f32(8, 128))
    vmem = pl.BlockSpec(memory_space=pltpu.VMEM)
    tile = lambda dt: pltpu.VMEM((HEADS * 2 * qwide, nk), dt)
    sides = pltpu.VMEM((2, rows, 8, d), F32)
    scratch = [sides, sides, pltpu.VMEM(col_a.shape, F32)]
    scratch += [pltpu.VMEM((rows, wide, d), F32)] * 2 + [sides, sides]
    scratch += [pltpu.VMEM((rows, qwide, d), F32)] * 2
    scratch += [pltpu.VMEM((middle * qwide, d), BF16)] * 4
    scratch += [tile(F32), tile(F32), tile(BF16), tile(BF16)]
    args = (col_a, col_b) + parts
    return call(inner, out_shape, [vmem] * len(args), scratch, 3_000_000_000)(*args)


def outer_grads(tokens, grad_out, edges, state):
    rows, cols, d = tokens.shape
    wide, qwide = sizes(rows, cols)
    nk = (2 + 2 * REACH) * wide
    out_shape = (
        jax.ShapeDtypeStruct((rows * cols, 3 * d), BF16),
        jax.ShapeDtypeStruct((d // 2 + 8, 4 * d), F32),
        jax.ShapeDtypeStruct((d // 2 + 8, 4 * d), BF16),
    )
    edge = pltpu.VMEM((4 * REACH, qwide, d), F32)
    tile = lambda dt: pltpu.VMEM((HEADS * 2 * qwide, nk), dt)
    scratch = [
        pltpu.VMEM((4 * REACH, wide, d), F32),
        pltpu.VMEM((2 * REACH, qwide, d), F32),
        pltpu.VMEM((edges[0].shape[0] + edges[2].shape[0], d), F32),
        edge,
        edge,
    ]
    scratch += [pltpu.VMEM((8 * REACH * wide, d), BF16)] * 4
    scratch += [pltpu.VMEM((4 * REACH * qwide, d), BF16)] * 4
    scratch += [tile(F32), tile(F32), tile(BF16), tile(BF16), edge, edge]
    scratch += [pltpu.VMEM((rows, wide, d), F32)] * 2
    vmem = pl.BlockSpec(memory_space=pltpu.VMEM)
    args = (tokens, grad_out) + tuple(edges) + tuple(state)
    return call(outer, out_shape, [vmem] * len(args), scratch, 3_000_000_000)(*args)


def put_half(piece_ref, *refs, other):
    *_, wqkv_hbm, wout_hbm, wqkv, wout, sems = refs
    half = piece_ref.shape[0]
    width = wqkv.shape[1]
    lo = lax.axis_index("rowlo")
    lo = 1 - lo if other else lo
    rows = pl.ds(pl.multiple_of(lo * half, half), half)
    wqkv[...] = piece_ref[:, :width].astype(F32)
    first = pltpu.make_async_copy(wqkv, wqkv_hbm.at[rows], sems.at[0])
    first.start()
    wout[...] = piece_ref[:, width:].astype(F32)
    second = pltpu.make_async_copy(wout, wout_hbm.at[rows], sems.at[1])
    second.start()
    first.wait()
    second.wait()


def put(piece, into, other):
    half, width = piece.shape
    d = 2 * half
    hbm = pl.BlockSpec(memory_space=pltpu.HBM)
    return pl.pallas_call(
        functools.partial(put_half, other=other),
        out_shape=(
            jax.ShapeDtypeStruct((d, width - d), F32),
            jax.ShapeDtypeStruct((d, d), F32),
        ),
        in_specs=[pl.BlockSpec(memory_space=pltpu.VMEM)] + [hbm] * len(into),
        out_specs=(hbm, hbm),
        scratch_shapes=[
            pltpu.VMEM((half, width - d), F32),
            pltpu.VMEM((half, d), F32),
            pltpu.SemaphoreType.DMA((2,)),
        ],
        input_output_aliases={1: 0, 2: 1} if into else {},
        compiler_params=pltpu.CompilerParams(vmem_limit_bytes=8 * 1024 * 1024),
        cost_estimate=pl.CostEstimate(flops=0, bytes_accessed=2_000_000, transcendentals=0),
    )(piece, *into)


def swap_pairs(x, axis, first):
    shape = (lax.axis_size(ROW_AXES), lax.axis_size("col"))
    pairs = []
    for r in range(shape[0]):
        for c in range(shape[1]):
            at = [r, c]
            to = at[axis] + (1 if (at[axis] - first) % 2 == 0 else -1)
            if 0 <= to < shape[axis]:
                at[axis] = to
            else:
                at[1 - axis] ^= 1
            pairs.append((r * shape[1] + c, at[0] * shape[1] + at[1]))
    return lax.ppermute(x, ROW_AXES + ("col",), pairs)


def shards(tokens, grad_out, w_qkv, w_out, scale):
    rows, cols, d = tokens.shape
    tokens, grad_out, col_a, col_b, row_a, row_b = packed(tokens, grad_out)
    col_b = swap_pairs(col_b, 1, 1)
    col_a = swap_pairs(col_a, 1, 0)
    row_b = swap_pairs(row_b, 0, 1)
    row_a = swap_pairs(row_a, 0, 0)
    seg, last, _, _, _ = piece_layout(rows)
    odd = lax.axis_index("rowlo") % 2

    def corners(at):
        return jnp.concatenate(
            [lax.dynamic_slice_in_dim(c, at, seg, 0) for c in (col_a, col_b)], axis=0
        )

    corner_b = swap_pairs(corners(odd * last), 0, 1)
    corner_a = swap_pairs(corners((1 - odd) * last), 0, 0)

    sl, wqkv_in, wout_in, k, rk, v, q, rq, ga = own_parts(scale, tokens, grad_out, w_qkv, w_out)
    state = inner_grads(rows, cols, col_a, col_b, sl, wqkv_in, wout_in, k, v, q, ga)
    state = (sl, wqkv_in, wout_in) + state[:4] + (k, rk, q, rq) + state[4:]
    grads, kept, sent = outer_grads(tokens, grad_out, (row_a, row_b, corner_a, corner_b), state)
    grad_tokens = dot(grads, w_qkv, LAST).astype(BF16).reshape(rows, cols, d)

    swap = [(0, 1), (1, 0)]
    kept = kept + lax.ppermute(sent, "rowlo", swap).astype(F32)
    kept, grad_tokens = lax.optimization_barrier((kept, grad_tokens))
    half = d // 2
    n = lax.axis_size(SPREAD_AXES)
    pieces = half // n if half % n == 0 else 1
    part = kept[:half].reshape(n, pieces, -1)
    sums = kept[half, :HEADS] + kept[half, HEADS : 2 * HEADS]
    sums_hi = lax.reduce_precision(sums, 8, 7)
    sums = jnp.concatenate([sums_hi, sums - sums_hi, jnp.zeros((128 - 2 * HEADS,), F32)])
    part = jnp.concatenate(
        [part.astype(BF16), jnp.broadcast_to(sums.astype(BF16), (n, pieces, 128))], axis=2
    )
    part = lax.all_to_all(part, SPREAD_AXES, 0, 0, tiled=True).astype(F32)
    part = jnp.sum(part, axis=0)
    sums = part[0, -128:]
    grad_scale = sums[:HEADS] + sums[HEADS : 2 * HEADS]
    part = part[:, :-128].astype(BF16)
    mine = lax.all_to_all(
        jnp.broadcast_to(part[None], (n,) + part.shape), SPREAD_AXES, 0, 0, tiled=True
    ).reshape(half, 4 * d)
    other = lax.ppermute(mine, "rowlo", swap)
    grad_wqkv, grad_wout = put(other, put(mine, (), False), True)
    return grad_tokens, grad_wqkv, grad_wout, grad_scale


def solution(mesh):
    n_row, n_col = mesh.devices.shape
    fine = Mesh(mesh.devices.reshape(n_row // 2, 2, n_col), ("rowhi", "rowlo", "col"))
    block = P(ROW_AXES, "col", None)
    return jax.shard_map(
        shards,
        mesh=fine,
        in_specs=(block, block, P(), P(), P()),
        out_specs=(block, P(), P(), P()),
        check_vma=False,
    )
```

```python
import functools
import math

import jax
import jax.numpy as jnp
from jax import lax
from jax.experimental import pallas as pl
from jax.experimental.pallas import tpu as pltpu
from jax.sharding import Mesh
from jax.sharding import PartitionSpec as P

HEADS = 4
REACH = 3
F32 = jnp.float32
BF16 = jnp.bfloat16
LAST = (((1,), (1,)), ((), ()))
FIRST = (((0,), (0,)), ((), ()))
LOG2E = math.log2(math.e)
ROW_AXES = ("rowhi", "rowlo")
SPREAD_AXES = ("rowhi", "col")


def dot(a, b, dims=(((1,), (0,)), ((), ()))):
    return lax.dot_general(a, b, dims, preferred_element_type=F32)


def split(x):
    hi = x.astype(BF16)
    return hi, (x - hi.astype(F32)).astype(BF16)


def pin(x):
    return pltpu.with_memory_space_constraint(x, pltpu.HBM)


def piece_layout(rows):
    wide = 2 * REACH
    used = wide * wide + REACH * REACH
    seg = -(-used // 16) * 16
    more = (seg - used) // REACH
    mid_tok = (rows - 2 * wide) * wide
    mid = -(-(mid_tok + (rows - 2 * REACH - 2 * more) * REACH) // 8) * 8
    tok, go = [], []
    for r in range(rows):
        if r < wide:
            tok.append(r * wide)
        elif r < rows - wide:
            tok.append(seg + (r - wide) * wide)
        else:
            tok.append(seg + mid + (r - rows + wide) * wide)
        if r < REACH + more:
            go.append(wide * wide + r * REACH)
        elif r < rows - REACH - more:
            go.append(seg + mid_tok + (r - REACH - more) * REACH)
        elif r < rows - REACH:
            go.append(seg + mid + used + (r - rows + REACH + more) * REACH)
        else:
            go.append(seg + mid + wide * wide + (r - rows + REACH) * REACH)
    return seg, seg + mid, 2 * seg + mid, tok, go


def pack(tok_hbm, go_hbm, tok_ref, go_ref, col_a, col_b, row_a, row_b, tf, gf, first, last, sems):
    rows, cols, d = tok_ref.shape
    copies = [
        pltpu.make_async_copy(tok_hbm, tok_ref, sems.at[0]),
        pltpu.make_async_copy(go_hbm, go_ref, sems.at[1]),
    ]
    for c in copies:
        c.start()
    wide = 2 * REACH
    _, _, _, tok_at, go_at = piece_layout(rows)
    even_row = lax.axis_index("rowlo") % 2 == 0
    even_col = lax.axis_index("col") % 2 == 0
    first[...] = jnp.zeros_like(first)
    last[...] = jnp.zeros_like(last)
    for c in copies:
        c.wait()
    tf[...] = tok_ref[...].astype(F32)
    gf[...] = go_ref[...].astype(F32)
    for r in range(rows):
        first[tok_at[r] : tok_at[r] + wide] = tf[r, 0:wide, :]
        last[tok_at[r] : tok_at[r] + wide] = tf[r, cols - wide : cols, :]
        first[go_at[r] : go_at[r] + REACH] = gf[r, 0:REACH, :]
        last[go_at[r] : go_at[r] + REACH] = gf[r, cols - REACH : cols, :]
    lo, hi = first[...], last[...]
    col_a[...] = jnp.where(even_col, hi, lo).astype(BF16)
    col_b[...] = jnp.where(even_col, lo, hi).astype(BF16)
    cut = wide * cols
    end = cut + REACH * cols
    lo = tf[0:wide].reshape(cut, d)
    hi = tf[rows - wide : rows].reshape(cut, d)
    row_a[0:cut] = jnp.where(even_row, hi, lo).astype(BF16)
    row_b[0:cut] = jnp.where(even_row, lo, hi).astype(BF16)
    lo = gf[0:REACH].reshape(end - cut, d)
    hi = gf[rows - REACH : rows].reshape(end - cut, d)
    row_a[cut:end] = jnp.where(even_row, hi, lo).astype(BF16)
    row_b[cut:end] = jnp.where(even_row, lo, hi).astype(BF16)


def packed(tokens, grad_out):
    rows, cols, d = tokens.shape
    size = piece_layout(rows)[2]
    vmem = pl.BlockSpec(memory_space=pltpu.VMEM)
    col = jax.ShapeDtypeStruct((size, d), BF16)
    row = jax.ShapeDtypeStruct((3 * REACH * cols, d), BF16)
    whole = jax.ShapeDtypeStruct((rows, cols, d), BF16)
    block = pltpu.VMEM((rows, cols, d), F32)
    return pl.pallas_call(
        pack,
        out_shape=(whole, whole, col, col, row, row),
        in_specs=[pl.BlockSpec(memory_space=pltpu.HBM)] * 2,
        out_specs=(vmem,) * 6,
        scratch_shapes=[
            block,
            block,
            pltpu.VMEM((size, d), F32),
            pltpu.VMEM((size, d), F32),
            pltpu.SemaphoreType.DMA((2,)),
        ],
        compiler_params=pltpu.CompilerParams(vmem_limit_bytes=8 * 1024 * 1024),
        cost_estimate=pl.CostEstimate(flops=0, bytes_accessed=1_000_000, transcendentals=0),
    )(pin(tokens), pin(grad_out))


def unit(x, head_sum):
    r = lax.rsqrt(head_sum(x * x) + 1e-06)
    return x * r, r


def tools(d):
    per = d // HEADS
    lane_head = lax.broadcasted_iota(jnp.int32, (1, d), 1) // per
    heads = [lane_head == h for h in range(HEADS)]
    ones = (
        lax.broadcasted_iota(jnp.int32, (d, d), 0) // per
        == lax.broadcasted_iota(jnp.int32, (d, d), 1) // per
    ).astype(BF16)

    def head_sum(x):
        return dot(x.astype(BF16), ones)

    def spread(x):
        zero = jnp.zeros_like(x)
        return jnp.concatenate([jnp.where(m, x, zero) for m in heads], axis=0)

    def gather(x):
        n = x.shape[0] // HEADS
        out = x[0:n]
        for h in range(1, HEADS):
            out = jnp.where(heads[h], x[h * n : (h + 1) * n], out)
        return out

    return heads, head_sum, spread, gather


def has_neighbours(axis):
    at = lax.axis_index(axis)
    return at > 0, at < lax.axis_size(axis) - 1


def near_mask(qwide, wide, cols):
    nq, nk = 2 * qwide, (2 + 2 * REACH) * wide
    i = lax.broadcasted_iota(jnp.int32, (nq, nk), 0)
    j = lax.broadcasted_iota(jnp.int32, (nq, nk), 1)
    dr = j // wide - i // qwide
    dc = j % wide - i % qwide
    key_col = j % wide + (lax.axis_index("col") * cols - 8)
    near = (dr >= 0) & (dr <= 2 * REACH) & (dc >= 0) & (dc <= 2 * REACH)
    near = near & (key_col >= 0) & (key_col < cols * lax.axis_size("col"))
    return near.astype(F32)


def run_bands(bands, sbuf, dbuf, pbuf, dsbuf, nq, spread):
    def scores(band):
        q_hi, q_lo = spread(band["q_hi"]()), spread(band["q_lo"]())
        k_hi = band["k_hi"]()
        sbuf[...] = dot(q_hi, k_hi, LAST) + dot(q_lo, k_hi, LAST) + dot(q_hi, band["k_lo"](), LAST)
        g_hi, g_lo = spread(band["g_hi"]()), spread(band["g_lo"]())
        v_hi = band["v_hi"]()
        dbuf[...] = dot(g_hi, v_hi, LAST) + dot(g_lo, v_hi, LAST) + dot(g_hi, band["v_lo"](), LAST)

    def softmax(band, total):
        mask, own = band["mask"](), band["own"]()
        out = []
        for h in range(HEADS):
            at = slice(h * nq, (h + 1) * nq)
            s, dp = sbuf[at], dbuf[at]
            e = jnp.exp2(s) * mask
            r = 1.0 / (jnp.sum(e, axis=1, keepdims=True) + 1e-30)
            p = e * r
            ds = p * (dp - jnp.sum(p * dp, axis=1, keepdims=True))
            if own is None:
                out.append(total[h])
            else:
                out.append(total[h] + own * jnp.sum(ds * s, axis=1, keepdims=True))
            pbuf[at] = p.astype(BF16)
            dsbuf[at] = ds.astype(BF16)
        return out

    total = [jnp.zeros((nq, 1), F32) for _ in range(HEADS)]
    count = len(bands)
    scores(bands[0])
    for b in range(count + 1):
        if b > 0:
            bands[b - 1]["grads"](pbuf, dsbuf)
        if b < count:
            total = softmax(bands[b], total)
        if b + 1 < count:
            scores(bands[b + 1])
    return [jnp.sum(t, axis=0, keepdims=True) for t in total]


def own(
    scale_hbm,
    tok_ref,
    go_ref,
    wqkv_hbm,
    wout_hbm,
    sl_ref,
    wqkv_ref,
    wout_ref,
    k_ref,
    rk_ref,
    v_ref,
    q_ref,
    rq_ref,
    ga_ref,
    near_ref,
    scale_ref,
    sems,
):
    copies = [
        pltpu.make_async_copy(scale_hbm, scale_ref, sems.at[0]),
        pltpu.make_async_copy(wqkv_hbm, wqkv_ref, sems.at[1]),
        pltpu.make_async_copy(wout_hbm, wout_ref, sems.at[2]),
    ]
    for c in copies:
        c.start()
    rows, cols, d = tok_ref.shape
    n = rows * cols
    heads, head_sum, _, _ = tools(d)
    wide, qwide = sizes(rows, cols)
    near_ref[...] = near_mask(qwide, wide, cols)
    for c in copies:
        c.wait()
    sl = jnp.zeros((1, d), F32)
    for h in range(HEADS):
        sl = jnp.where(heads[h], scale_ref[h], sl)
    sl_ref[...] = jnp.broadcast_to(sl, sl_ref.shape)
    qkv = dot(tok_ref[...].reshape(n, d), wqkv_ref[...])
    q_ref[...], rq_ref[...] = unit(qkv[:, :d], head_sum)
    k_ref[...], rk_ref[...] = unit(qkv[:, d : 2 * d], head_sum)
    v_ref[...] = qkv[:, 2 * d :]
    ga_ref[...] = dot(go_ref[...].reshape(n, d), wout_ref[...], LAST)


def inner(
    col_a,
    col_b,
    sl_ref,
    wqkv_ref,
    wout_ref,
    k_own,
    v_own,
    q_own,
    ga_own,
    near_ref,
    khi,
    klo,
    vhi,
    vlo,
    qe_ref,
    ge_ref,
    gq,
    att,
    gk,
    gv,
    psum,
    ts,
    gs,
    side,
    kg,
    vg,
    qs,
    gas,
    qg,
    gg,
    qhi,
    qlo,
    ghi,
    glo,
    sbuf,
    dbuf,
    pbuf,
    dsbuf,
):
    rows, wide, d = kg.shape
    _, qwide, _ = qg.shape
    cols = k_own.shape[0] // rows
    reach2 = 2 * REACH
    q0 = 8 - REACH - 2
    own_q = 8 - q0
    heads, head_sum, spread, gather = tools(d)
    sl = sl_ref[0:1]

    ts[...] = jnp.zeros_like(ts)
    gs[...] = jnp.zeros_like(gs)
    even_col = lax.axis_index("col") % 2 == 0
    _, _, _, tok_at, go_at = piece_layout(rows)
    has_left, has_right = has_neighbours("col")
    for i, even, valid, at_k, at_g in (
        (0, ~even_col, has_left, 8 - reach2, 8 - REACH),
        (1, even_col, has_right, 0, 0),
    ):
        x = jnp.where(even, col_a[...].astype(F32), col_b[...].astype(F32))
        side[...] = jnp.where(valid, x, jnp.zeros_like(x))
        for r in range(rows):
            ts[i, r, at_k : at_k + reach2, :] = side[tok_at[r] : tok_at[r] + reach2]
            gs[i, r, at_g : at_g + REACH, :] = side[go_at[r] : go_at[r] + REACH]
    m = 2 * rows * 8
    qkv = dot(ts[...].reshape(m, d).astype(BF16), wqkv_ref[...])
    q, _ = unit(qkv[:, :d], head_sum)
    k, _ = unit(qkv[:, d : 2 * d], head_sum)
    qs[...] = q.reshape(2, rows, 8, d)
    gas[...] = dot(gs[...].reshape(m, d).astype(BF16), wout_ref[...], LAST).reshape(2, rows, 8, d)
    for grid, sides, mine in ((kg, k, k_own), (vg, qkv[:, 2 * d :], v_own)):
        grid[:, 0:8, :] = sides[: m // 2].reshape(rows, 8, d)
        grid[:, 8 : 8 + cols, :] = mine[...].reshape(rows, cols, d)
        grid[:, 8 + cols : 16 + cols, :] = sides[m // 2 :].reshape(rows, 8, d)
        if wide > 16 + cols:
            grid[:, 16 + cols :, :] = jnp.zeros((rows, wide - 16 - cols, d), F32)
    for grid, sides, mine in ((qg, qs, q_own), (gg, gas, ga_own)):
        grid[:, 0:own_q, :] = sides[0, :, q0:8, :]
        grid[:, own_q : own_q + cols, :] = mine[...].reshape(rows, cols, d)
        grid[:, own_q + cols : qwide, :] = sides[1, :, 0 : qwide - own_q - cols, :]
    khi[...], klo[...] = split(kg[...].reshape(rows * wide, d))
    vhi[...], vlo[...] = split(vg[...].reshape(rows * wide, d))
    mid = (rows - reach2) * qwide
    middle = slice(REACH, rows - REACH)
    qhi[...], qlo[...] = split(qg[middle].reshape(mid, d) * (sl * LOG2E))
    ghi[...], glo[...] = split(gg[middle].reshape(mid, d))
    for edge, grid in ((qe_ref, qg), (ge_ref, gg)):
        edge[0:REACH] = grid[0:REACH]
        edge[REACH:] = grid[rows - REACH :]
    gk[...] = jnp.zeros_like(gk)
    gv[...] = jnp.zeros_like(gv)

    nq = 2 * qwide
    span = 2 + reach2
    near = near_ref[...]
    iq = lax.broadcasted_iota(jnp.int32, (nq, 1), 0) % qwide
    own_col = ((iq >= own_q) & (iq < own_q + cols)).astype(F32)

    def band(b):
        at = slice(b * nq, (b + 1) * nq)
        keys = slice(b * 2 * wide, b * 2 * wide + span * wide)

        def grads(pbuf, dsbuf):
            p, ds = pbuf[...], dsbuf[...]
            att[2 * b : 2 * b + 2] = gather(dot(p, vhi[keys])).reshape(2, qwide, d)
            gq[2 * b : 2 * b + 2] = gather(dot(ds, khi[keys])).reshape(2, qwide, d)
            eight = slice(2 * b, 2 * b + span)
            gk[eight] += dot(ds, spread(qhi[at]), FIRST).reshape(span, wide, d)
            gv[eight] += dot(p, spread(ghi[at]), FIRST).reshape(span, wide, d)

        return {
            "q_hi": lambda: qhi[at],
            "q_lo": lambda: qlo[at],
            "g_hi": lambda: ghi[at],
            "g_lo": lambda: glo[at],
            "k_hi": lambda: khi[keys],
            "k_lo": lambda: klo[keys],
            "v_hi": lambda: vhi[keys],
            "v_lo": lambda: vlo[keys],
            "mask": lambda: near,
            "own": lambda: own_col,
            "grads": grads,
        }

    bands = [band(b) for b in range((rows - reach2) // 2)]
    total = run_bands(bands, sbuf, dbuf, pbuf, dsbuf, nq, spread)
    lane = lax.broadcasted_iota(jnp.int32, psum.shape, 1)
    sums = jnp.zeros(psum.shape, F32)
    for h in range(HEADS):
        sums = jnp.where(lane == h, total[h], sums)
    psum[...] = sums


def outer(
    tok_ref,
    go_ref,
    row_a,
    row_b,
    corner_a,
    corner_b,
    sl_ref,
    wqkv_ref,
    wout_ref,
    khi_in,
    klo_in,
    vhi_in,
    vlo_in,
    k_own,
    rk_own,
    q_own,
    rq_own,
    qe_in,
    ge_in,
    gq_in,
    att_in,
    gk_in,
    gv_in,
    psum,
    near_ref,
    grads_ref,
    kept_ref,
    sent_ref,
    tx,
    gx,
    ends,
    qe,
    ge,
    khi,
    klo,
    vhi,
    vlo,
    qhi,
    qlo,
    ghi,
    glo,
    sbuf,
    dbuf,
    pbuf,
    dsbuf,
    gq,
    att,
    gk,
    gv,
):
    rows, cols, d = tok_ref.shape
    _, wide, _ = tx.shape
    _, qwide, _ = gx.shape
    reach2 = 2 * REACH
    q0 = 8 - REACH - 2
    own_q = 8 - q0
    n_rows = rows * lax.axis_size(ROW_AXES)
    row_first = lax.axis_index(ROW_AXES) * rows
    heads, head_sum, spread, gather = tools(d)
    sl = sl_ref[0:1]

    left_k, right_k = 8 - reach2, 8 + cols
    left_q, right_q = own_q - REACH, own_q + cols
    tx[:, 0:8, :] = jnp.zeros((2 * reach2, 8, d), F32)
    tx[:, 8 + cols : wide, :] = jnp.zeros((2 * reach2, wide - 8 - cols, d), F32)
    gx[:, 0:8, :] = jnp.zeros((reach2, 8, d), F32)
    even_row = lax.axis_index("rowlo") % 2 == 0
    even_col = lax.axis_index("col") % 2 == 0
    seg = piece_layout(rows)[0]
    cut = reach2 * cols
    end = cut + REACH * cols
    has_above, has_below = has_neighbours(ROW_AXES)
    has_left, has_right = has_neighbours("col")
    for even, valid, row_k, row_q in (
        (~even_row, has_above, 0, 0),
        (even_row, has_below, reach2, REACH),
    ):
        x = jnp.where(even, row_a[...].astype(F32), row_b[...].astype(F32))
        ends[0:end] = jnp.where(valid, x, jnp.zeros_like(x))
        x = jnp.where(even, corner_a[...].astype(F32), corner_b[...].astype(F32))
        ends[end : end + 2 * seg] = jnp.where(valid, x, jnp.zeros_like(x))
        tx[row_k : row_k + reach2, 8 : 8 + cols, :] = ends[0:cut].reshape(reach2, cols, d)
        gx[row_q : row_q + REACH, own_q : own_q + cols, :] = ends[cut:end].reshape(REACH, cols, d)
        first, last = ends[end : end + seg], ends[end + seg : end + 2 * seg]
        none = jnp.zeros_like(first)
        ends[end : end + seg] = jnp.where(has_left, jnp.where(even_col, last, first), none)
        ends[end + seg : end + 2 * seg] = jnp.where(has_right, jnp.where(even_col, first, last), none)
        for base, at_k, at_q in ((end, left_k, left_q), (end + seg, right_k, right_q)):
            for r in range(reach2):
                at = base + r * reach2
                tx[row_k + r, at_k : at_k + reach2, :] = ends[at : at + reach2]
            for r in range(REACH):
                at = base + reach2 * reach2 + r * REACH
                gx[row_q + r, at_q : at_q + REACH, :] = ends[at : at + REACH]

    m = reach2 * wide
    x = tx[...].reshape(2 * m, d).astype(BF16)
    kv = dot(x, wqkv_ref[:, d:])
    k, _ = unit(kv[:, :d], head_sum)
    for hi, lo, hi_in, lo_in, fresh in (
        (khi, klo, khi_in, klo_in, k),
        (vhi, vlo, vhi_in, vlo_in, kv[:, d:]),
    ):
        fresh_hi, fresh_lo = split(fresh)
        hi[0:m], lo[0:m] = fresh_hi[0:m], fresh_lo[0:m]
        hi[3 * m :], lo[3 * m :] = fresh_hi[m:], fresh_lo[m:]
        own_end = rows * wide
        for to, source in ((hi, hi_in), (lo, lo_in)):
            to[m : 2 * m] = source[0:m]
            to[2 * m : 3 * m] = source[own_end - m : own_end]
    x = tx[REACH : 3 * REACH, q0 : q0 + qwide, :].reshape(reach2 * qwide, d).astype(BF16)
    q, _ = unit(dot(x, wqkv_ref[:, :d]), head_sum)
    q = q.reshape(reach2, qwide, d)
    g = dot(gx[...].reshape(reach2 * qwide, d).astype(BF16), wout_ref[...], LAST)
    g = g.reshape(reach2, qwide, d)
    qe[0:REACH], qe[3 * REACH :] = q[0:REACH], q[REACH:]
    ge[0:REACH], ge[3 * REACH :] = g[0:REACH], g[REACH:]
    qe[REACH : 3 * REACH] = qe_in[...]
    ge[REACH : 3 * REACH] = ge_in[...]
    flat = 2 * reach2 * qwide
    qhi[...], qlo[...] = split(qe[...].reshape(flat, d) * (sl * LOG2E))
    ghi[...], glo[...] = split(ge[...].reshape(flat, d))
    gk[...] = gk_in[...]
    gv[...] = gv_in[...]

    nq = 2 * qwide
    span = 2 + reach2
    nk = span * wide
    near = near_ref[...]
    jr = lax.broadcasted_iota(jnp.int32, (1, nk), 1) // wide
    iq = lax.broadcasted_iota(jnp.int32, (nq, 1), 0)
    own_col = (iq % qwide >= own_q) & (iq % qwide < own_q + cols)

    def band(b):
        top = b < REACH
        first = 2 * b if top else rows + 2 * (b - REACH)
        at = slice(b * nq, (b + 1) * nq)
        key_at = 2 * b if top else 2 * reach2 + 2 * (b - REACH)
        keys = slice(key_at * wide, key_at * wide + nk)
        mine = first + 1 >= REACH and first < rows + REACH
        skip = reach2 - first if top else 0
        count = span - skip if top else reach2 - 2 * (b - REACH)
        to = 0 if top else rows - count
        part = slice(skip * wide, (skip + count) * wide)

        def mask():
            key_row = jr + (row_first - reach2 + first)
            return near * ((key_row >= 0) & (key_row < n_rows)).astype(F32)

        def own():
            if not mine:
                return None
            q_row = iq // qwide + first
            return (own_col & (q_row >= REACH) & (q_row < REACH + rows)).astype(F32)

        def grads(pbuf, dsbuf):
            if mine:
                att[2 * b : 2 * b + 2] = gather(dot(pbuf[...], vhi[keys])).reshape(2, qwide, d)
                gq[2 * b : 2 * b + 2] = gather(dot(dsbuf[...], khi[keys])).reshape(2, qwide, d)
            p, ds = pbuf[:, part], dsbuf[:, part]
            own_rows = slice(to, to + count)
            gk[own_rows] += dot(ds, spread(qhi[at]), FIRST).reshape(count, wide, d)
            gv[own_rows] += dot(p, spread(ghi[at]), FIRST).reshape(count, wide, d)

        return {
            "q_hi": lambda: qhi[at],
            "q_lo": lambda: qlo[at],
            "g_hi": lambda: ghi[at],
            "g_lo": lambda: glo[at],
            "k_hi": lambda: khi[keys],
            "k_lo": lambda: klo[keys],
            "v_hi": lambda: vhi[keys],
            "v_lo": lambda: vlo[keys],
            "mask": mask,
            "own": own,
            "grads": grads,
        }

    total = run_bands([band(b) for b in range(reach2)], sbuf, dbuf, pbuf, dsbuf, nq, spread)

    n = rows * cols
    key_cols = slice(8, 8 + cols)
    query_cols = slice(own_q, own_q + cols)

    def own_queries(edge, middle):
        parts = [
            edge[REACH:reach2, query_cols, :],
            middle[:, query_cols, :],
            edge[reach2 : 3 * REACH, query_cols, :],
        ]
        return jnp.concatenate(parts, axis=0).reshape(n, d)

    def unit_back(u, r, g):
        return r * (g - u * head_sum(u * g))

    g_q = unit_back(q_own[...], rq_own[...], own_queries(gq, gq_in) * sl)
    g_k = unit_back(k_own[...], rk_own[...], gk[:, key_cols, :].reshape(n, d) * (1.0 / LOG2E))
    g_v = gv[:, key_cols, :].reshape(n, d)
    grads = jnp.concatenate([g_q.astype(BF16), g_k.astype(BF16), g_v.astype(BF16)], axis=1)
    grads_ref[...] = grads
    wq = dot(tok_ref[...].reshape(n, d), grads, FIRST)
    wo = dot(own_queries(att, att_in).astype(BF16), go_ref[...].reshape(n, d), FIRST)
    half = d // 2
    lane = lax.broadcasted_iota(jnp.int32, (8, 4 * d), 1)
    kept, sent = jnp.zeros((8, 4 * d), F32), jnp.zeros((8, 4 * d), F32)
    for h in range(HEADS):
        at = h * (d // HEADS)
        t = (total[h] + psum[0:1, h : h + 1]) / (sl[:, at : at + 1] * LOG2E)
        hi = t.astype(BF16).astype(F32)
        kept = jnp.where(lane == h, t, kept)
        sent = jnp.where(lane == h, hi, sent)
        sent = jnp.where(lane == HEADS + h, t - hi, sent)
    first = lax.axis_index("rowlo") == 0
    for x, at in ((wq, slice(0, 3 * d)), (wo, slice(3 * d, 4 * d))):
        kept_ref[0:half, at] = jnp.where(first, x[:half], x[half:])
        sent_ref[0:half, at] = jnp.where(first, x[half:], x[:half]).astype(BF16)
    kept_ref[half:, :] = kept
    sent_ref[half:, :] = sent.astype(BF16)


def sizes(rows, cols):
    wide = -(-(cols + 4 * REACH + 2) // 16) * 16
    qwide = -(-(cols + 2 * REACH + 2) // 8) * 8
    return wide, qwide


def call(body, out_shape, in_specs, scratch, flops):
    vmem = pl.BlockSpec(memory_space=pltpu.VMEM)
    return pl.pallas_call(
        body,
        out_shape=out_shape,
        in_specs=in_specs,
        out_specs=(vmem,) * len(out_shape),
        scratch_shapes=scratch,
        compiler_params=pltpu.CompilerParams(vmem_limit_bytes=24 * 1024 * 1024),
        cost_estimate=pl.CostEstimate(
            flops=flops, bytes_accessed=4_000_000, transcendentals=300_000
        ),
    )


def own_parts(scale, tokens, grad_out, w_qkv, w_out):
    rows, cols, d = tokens.shape
    f32 = lambda *s: jax.ShapeDtypeStruct(s, F32)
    bf16 = lambda *s: jax.ShapeDtypeStruct(s, BF16)
    out_shape = (f32(8, d), bf16(*w_qkv.shape), bf16(*w_out.shape)) + (f32(rows * cols, d),) * 6
    wide, qwide = sizes(rows, cols)
    out_shape += (f32(2 * qwide, (2 + 2 * REACH) * wide),)
    vmem = pl.BlockSpec(memory_space=pltpu.VMEM)
    hbm = pl.BlockSpec(memory_space=pltpu.HBM)
    scratch = [pltpu.SMEM((HEADS,), F32), pltpu.SemaphoreType.DMA((3,))]
    return call(own, out_shape, [hbm, vmem, vmem, hbm, hbm], scratch, 500_000_000)(
        pin(scale), tokens, grad_out, pin(w_qkv), pin(w_out)
    )


def inner_grads(rows, cols, col_a, col_b, *parts):
    d = col_a.shape[1]
    wide, qwide = sizes(rows, cols)
    f32 = lambda *s: jax.ShapeDtypeStruct(s, F32)
    middle = rows - 2 * REACH
    nk = (2 + 2 * REACH) * wide
    key = jax.ShapeDtypeStruct((rows * wide, d), BF16)
    edge, mid, grid = f32(2 * REACH, qwide, d), f32(middle, qwide, d), f32(rows, wide, d)
    out_shape = (key,) * 4 + (edge, edge, mid, mid, grid, grid, f32(8, 128))
    vmem = pl.BlockSpec(memory_space=pltpu.VMEM)
    tile = lambda dt: pltpu.VMEM((HEADS * 2 * qwide, nk), dt)
    sides = pltpu.VMEM((2, rows, 8, d), F32)
    scratch = [sides, sides, pltpu.VMEM(col_a.shape, F32)]
    scratch += [pltpu.VMEM((rows, wide, d), F32)] * 2 + [sides, sides]
    scratch += [pltpu.VMEM((rows, qwide, d), F32)] * 2
    scratch += [pltpu.VMEM((middle * qwide, d), BF16)] * 4
    scratch += [tile(F32), tile(F32), tile(BF16), tile(BF16)]
    args = (col_a, col_b) + parts
    return call(inner, out_shape, [vmem] * len(args), scratch, 3_000_000_000)(*args)


def outer_grads(tokens, grad_out, edges, state):
    rows, cols, d = tokens.shape
    wide, qwide = sizes(rows, cols)
    nk = (2 + 2 * REACH) * wide
    out_shape = (
        jax.ShapeDtypeStruct((rows * cols, 3 * d), BF16),
        jax.ShapeDtypeStruct((d // 2 + 8, 4 * d), F32),
        jax.ShapeDtypeStruct((d // 2 + 8, 4 * d), BF16),
    )
    edge = pltpu.VMEM((4 * REACH, qwide, d), F32)
    tile = lambda dt: pltpu.VMEM((HEADS * 2 * qwide, nk), dt)
    scratch = [
        pltpu.VMEM((4 * REACH, wide, d), F32),
        pltpu.VMEM((2 * REACH, qwide, d), F32),
        pltpu.VMEM((edges[0].shape[0] + edges[2].shape[0], d), F32),
        edge,
        edge,
    ]
    scratch += [pltpu.VMEM((8 * REACH * wide, d), BF16)] * 4
    scratch += [pltpu.VMEM((4 * REACH * qwide, d), BF16)] * 4
    scratch += [tile(F32), tile(F32), tile(BF16), tile(BF16), edge, edge]
    scratch += [pltpu.VMEM((rows, wide, d), F32)] * 2
    vmem = pl.BlockSpec(memory_space=pltpu.VMEM)
    args = (tokens, grad_out) + tuple(edges) + tuple(state)
    return call(outer, out_shape, [vmem] * len(args), scratch, 3_000_000_000)(*args)


def put_half(piece_ref, *refs, other):
    *_, wqkv_hbm, wout_hbm, wqkv, wout, sems = refs
    half = piece_ref.shape[0]
    width = wqkv.shape[1]
    lo = lax.axis_index("rowlo")
    lo = 1 - lo if other else lo
    rows = pl.ds(pl.multiple_of(lo * half, half), half)
    wqkv[...] = piece_ref[:, :width].astype(F32)
    first = pltpu.make_async_copy(wqkv, wqkv_hbm.at[rows], sems.at[0])
    first.start()
    wout[...] = piece_ref[:, width:].astype(F32)
    second = pltpu.make_async_copy(wout, wout_hbm.at[rows], sems.at[1])
    second.start()
    first.wait()
    second.wait()


def put(piece, into, other):
    half, width = piece.shape
    d = 2 * half
    hbm = pl.BlockSpec(memory_space=pltpu.HBM)
    return pl.pallas_call(
        functools.partial(put_half, other=other),
        out_shape=(
            jax.ShapeDtypeStruct((d, width - d), F32),
            jax.ShapeDtypeStruct((d, d), F32),
        ),
        in_specs=[pl.BlockSpec(memory_space=pltpu.VMEM)] + [hbm] * len(into),
        out_specs=(hbm, hbm),
        scratch_shapes=[
            pltpu.VMEM((half, width - d), F32),
            pltpu.VMEM((half, d), F32),
            pltpu.SemaphoreType.DMA((2,)),
        ],
        input_output_aliases={1: 0, 2: 1} if into else {},
        compiler_params=pltpu.CompilerParams(vmem_limit_bytes=8 * 1024 * 1024),
        cost_estimate=pl.CostEstimate(flops=0, bytes_accessed=2_000_000, transcendentals=0),
    )(piece, *into)


def swap_pairs(x, axis, first):
    shape = (lax.axis_size(ROW_AXES), lax.axis_size("col"))
    pairs = []
    for r in range(shape[0]):
        for c in range(shape[1]):
            at = [r, c]
            to = at[axis] + (1 if (at[axis] - first) % 2 == 0 else -1)
            if 0 <= to < shape[axis]:
                at[axis] = to
            else:
                at[1 - axis] ^= 1
            pairs.append((r * shape[1] + c, at[0] * shape[1] + at[1]))
    return lax.ppermute(x, ROW_AXES + ("col",), pairs)


def shards(tokens, grad_out, w_qkv, w_out, scale):
    rows, cols, d = tokens.shape
    tokens, grad_out, col_a, col_b, row_a, row_b = packed(tokens, grad_out)
    col_b = swap_pairs(col_b, 1, 1)
    col_a = swap_pairs(col_a, 1, 0)
    row_b = swap_pairs(row_b, 0, 1)
    row_a = swap_pairs(row_a, 0, 0)
    seg, last, _, _, _ = piece_layout(rows)
    odd = lax.axis_index("rowlo") % 2

    def corners(at):
        return jnp.concatenate(
            [lax.dynamic_slice_in_dim(c, at, seg, 0) for c in (col_a, col_b)], axis=0
        )

    corner_b = swap_pairs(corners(odd * last), 0, 1)
    corner_a = swap_pairs(corners((1 - odd) * last), 0, 0)

    parts = own_parts(scale, tokens, grad_out, w_qkv, w_out)
    sl, wqkv_in, wout_in, k, rk, v, q, rq, ga, near = parts
    state = inner_grads(rows, cols, col_a, col_b, sl, wqkv_in, wout_in, k, v, q, ga, near)
    state = (sl, wqkv_in, wout_in) + state[:4] + (k, rk, q, rq) + state[4:] + (near,)
    grads, kept, sent = outer_grads(tokens, grad_out, (row_a, row_b, corner_a, corner_b), state)
    grad_tokens = dot(grads, w_qkv, LAST).astype(BF16).reshape(rows, cols, d)

    swap = [(0, 1), (1, 0)]
    kept = kept + lax.ppermute(sent, "rowlo", swap).astype(F32)
    kept, grad_tokens = lax.optimization_barrier((kept, grad_tokens))
    half = d // 2
    n = lax.axis_size(SPREAD_AXES)
    pieces = half // n if half % n == 0 else 1
    part = kept[:half].reshape(n, pieces, -1)
    sums = kept[half, :HEADS] + kept[half, HEADS : 2 * HEADS]
    sums_hi = lax.reduce_precision(sums, 8, 7)
    sums = jnp.concatenate([sums_hi, sums - sums_hi, jnp.zeros((128 - 2 * HEADS,), F32)])
    part = jnp.concatenate(
        [part.astype(BF16), jnp.broadcast_to(sums.astype(BF16), (n, pieces, 128))], axis=2
    )
    part = lax.all_to_all(part, SPREAD_AXES, 0, 0, tiled=True).astype(F32)
    part = jnp.sum(part, axis=0)
    sums = part[0, -128:]
    grad_scale = sums[:HEADS] + sums[HEADS : 2 * HEADS]
    part = part[:, :-128].astype(BF16)
    mine = lax.all_to_all(
        jnp.broadcast_to(part[None], (n,) + part.shape), SPREAD_AXES, 0, 0, tiled=True
    ).reshape(half, 4 * d)
    other = lax.ppermute(mine, "rowlo", swap)
    grad_wqkv, grad_wout = put(other, put(mine, (), False), True)
    return grad_tokens, grad_wqkv, grad_wout, grad_scale


def solution(mesh):
    n_row, n_col = mesh.devices.shape
    fine = Mesh(mesh.devices.reshape(n_row // 2, 2, n_col), ("rowhi", "rowlo", "col"))
    block = P(ROW_AXES, "col", None)
    return jax.shard_map(
        shards,
        mesh=fine,
        in_specs=(block, block, P(), P(), P()),
        out_specs=(block, P(), P(), P()),
        check_vma=False,
    )
```
